128 devices in a mesh: row: 8 (over x, core), col: 16 (over y, z).
Axes of the slice: x: 4, y: 4, z: 4, core: 2. Of those that a mesh axis runs over, the one named last changes fastest.
Arguments:
- factor: float32 [4, 8, 1024, 2048], P(None, 'row', None, 'col'), as said below
- cross_cov: float32 [4, 8, 1024, 1024], P(None, 'row', 'col'), may hold values from -6 to 6
Outputs:
- overwritten: float32 [4, 8, 1024, 1024], P(None, 'row', 'col')
The draws below stay inside these ranges and needn't reach their ends.
Inputs may be any that keep to these rules, and one draw needn't show every extreme that they name: The diagonal entries of the factor lie between 1 and 3.
All inputs are finite; a program needn't handle non-finite values.
Results may differ from the reference program's by a relative error of at most 0.00014.
Values sent between devices are 32-bit elements; how exact they have to be, the bound alone decides.
No kernel may reach another device: no remote copies, remote signals or barrier semaphores. Data moves between devices by JAX's collectives and lax.ppermute only.
A program may use at most 128 MiB of HBM per device.

```python
import math
import jax
import jax.numpy as jnp
from jax import lax

NB = 1024
NRHS = 1024
ROUNDS = 4
N_ROW = 8


def draw_factor(key, part):
    shape = (ROUNDS, N_ROW, NB, 2 * NB)
    key_noise, key_diag = jax.random.split(jax.random.fold_in(key, 11), 2)
    noise = jax.random.normal(key_noise, shape, jnp.float32)
    block_id = (jnp.arange(ROUNDS)[:, None] * N_ROW + jnp.arange(N_ROW)[None, :])[:, :, None, None]
    row_id = block_id * NB + jnp.arange(NB)[None, None, :, None]
    col_id = jnp.arange(2 * NB)[None, None, None, :]
    scales = jnp.where(block_id < 2, 1.5 / math.sqrt(NB), 1.0 / math.sqrt(2 * NB))
    diagonal = jnp.exp(jax.random.uniform(key_diag, shape, jnp.float32, 0.0, math.log(3.0)))
    return jnp.where(row_id == col_id, diagonal, noise * scales).astype(jnp.float32)


def block_scale(key, shape, cuts, low, high):
    loudness, own = 1.0, jax.random.fold_in(key, 6)
    for dim, blocks in cuts:
        steps = jnp.exp(jax.random.uniform(jax.random.fold_in(own, dim), (blocks,), jnp.float32, low / len(cuts), high / len(cuts)))
        loudness = loudness * jnp.repeat(steps, shape[dim] // blocks).reshape([-1 if axis == dim else 1 for axis in range(len(shape))])
    return loudness


def normal_values(rng, shape, scale, bound, cuts=(), kind=jnp.bfloat16):
    array = scale * jax.random.normal(rng, shape, jnp.float32)
    if cuts:
        array = array * block_scale(rng, shape, cuts, -0.22, 0.18)
    return jnp.clip(array, -bound, bound).astype(kind)


def setup_inputs(seed: int = 0) -> dict:
    seeds = jax.random.split(jax.random.key(seed), 3)
    return {
        "factor": draw_factor(jax.random.fold_in(seeds[2], 71), 0),
        "cross_cov": normal_values(seeds[1], (ROUNDS, N_ROW, NB, NRHS), 1.0, 6.0, ((1, 8), (2, 16)), jnp.float32),
    }


def reference(factor, cross_cov):
    lower = factor.reshape(-1, 2 * NB)
    rhs_all = cross_cov.reshape(-1, NRHS)
    first_block = lax.linalg.triangular_solve(lower[:NB, :NB], rhs_all[:NB], left_side=True, lower=True)
    second_rhs = rhs_all[NB:2 * NB] - jnp.dot(lower[NB:2 * NB, :NB], first_block, precision=lax.Precision.HIGHEST)
    second_block = lax.linalg.triangular_solve(lower[NB:2 * NB, NB:2 * NB], second_rhs, left_side=True, lower=True)
    solved = jnp.concatenate([first_block, second_block], 0)
    updated = rhs_all - jnp.dot(lower, solved, precision=lax.Precision.HIGHEST)
    result = jnp.concatenate([solved, updated[2 * NB:]], 0)
    return result.reshape(cross_cov.shape)
```

```python
import jax
import jax.numpy as jnp
import numpy as np
from jax import lax
from jax.experimental import pallas as pl
from jax.experimental.pallas import tpu as pltpu
from jax.sharding import Mesh, PartitionSpec as P

ROW = ("x", "core")
COL = ("yh", "yl", "z")
F32 = jnp.float32
BF16 = jnp.bfloat16
TILE = 128
PARAMS = pltpu.CompilerParams(vmem_limit_bytes=48 * 2**20)
VM = pl.BlockSpec(memory_space=pltpu.VMEM)
SM = pl.BlockSpec(memory_space=pltpu.SMEM)


def split(value):
    high = value.astype(BF16)
    return high, (value - high.astype(F32)).astype(BF16)


def mm(a, b):
    return jnp.dot(a, b, preferred_element_type=F32)


def pack_left(value):
    return jnp.concatenate(split(value), 1)


def pack_right(value):
    high, low = split(value)
    return jnp.concatenate(
        [jnp.concatenate([high, low], 1), jnp.concatenate([high, jnp.zeros_like(low)], 1)], 0
    )


def packed_product(left, right):
    out = mm(left, right)
    return out[:, :TILE] + out[:, TILE:]


def full_dot(a, b):
    return jnp.dot(a, b, precision=lax.Precision.HIGHEST, preferred_element_type=F32)


def invert_body(info, lead_ref, out_ref):
    out_ref[...] = lead_ref[...]

    @pl.when(info[0] == 1)
    def _():
        start = pl.multiple_of(info[1] * TILE, TILE)
        block = lead_ref[pl.ds(start, TILE), :]
        i = lax.broadcasted_iota(jnp.int32, (TILE, TILE), 0)
        j = lax.broadcasted_iota(jnp.int32, (TILE, TILE), 1)
        zero = jnp.zeros((TILE, TILE), F32)
        inverse = jnp.where(i == j, 1.0 / jnp.where(i == j, block, 1.0), zero)
        step = 1
        while step < TILE:
            below = ((i // (2 * step)) == (j // (2 * step))) & ((i // step) > (j // step))
            corner = jnp.where(below, block, zero)
            inverse = inverse - full_dot(inverse, full_dot(corner, inverse))
            step *= 2
        out_ref[pl.ds(start, TILE), :] = inverse


def invert_diagonal(info, lead):
    return pl.pallas_call(
        invert_body,
        out_shape=jax.ShapeDtypeStruct(lead.shape, F32),
        in_specs=[SM, VM],
        out_specs=VM,
        compiler_params=PARAMS,
        name="invert_diagonal",
    )(info, lead)


def solve_body(tri_ref, rhs_ref, out_ref):
    count = tri_ref.shape[0]
    out_ref[...] = rhs_ref[...]
    for k in range(count):
        here = pl.ds(k * TILE, TILE)
        solved = packed_product(pack_left(tri_ref[k, here, :]), pack_right(out_ref[here, :]))
        out_ref[here, :] = solved
        right = pack_right(solved)
        for i in range(k + 1, count):
            there = pl.ds(i * TILE, TILE)
            out_ref[there, :] = out_ref[there, :] - packed_product(pack_left(tri_ref[k, there, :]), right)


def solve(tri, rhs):
    return pl.pallas_call(
        solve_body,
        out_shape=jax.ShapeDtypeStruct(rhs.shape, F32),
        in_specs=[VM, VM],
        out_specs=VM,
        compiler_params=PARAMS,
        name="block_solve",
    )(tri, rhs)


def residual_body(tri_ref, rhs_ref, x_ref, out_ref):
    count = tri_ref.shape[0]
    for k in range(count):
        right = pack_right(x_ref[pl.ds(k * TILE, TILE), :])
        for i in range(count):
            there = pl.ds(i * TILE, TILE)
            base = rhs_ref[there, :] if k == 0 else out_ref[there, :]
            out_ref[there, :] = base - packed_product(pack_left(tri_ref[k, there, :]), right)


def residual(tri, rhs, x):
    return pl.pallas_call(
        residual_body,
        out_shape=jax.ShapeDtypeStruct(rhs.shape, F32),
        in_specs=[VM, VM, VM],
        out_specs=VM,
        compiler_params=PARAMS,
        name="block_residual",
    )(tri, rhs, x)


def update_body(half, info, base_ref, left_ref, own_ref, other_ref, out_ref):
    core = info[0]
    rows = base_ref.shape[0]
    lefts = []
    for side, swap in ((0, core), (1, 1 - core)):
        for q in range(2):
            first = 8 * half + 4 * swap + 2 * q
            lefts.append(split(jnp.concatenate([left_ref[first], left_ref[first + 1]], 1)))
    for pair in range(4):
        cols = pl.ds(pair * 2 * TILE, 2 * TILE)
        total = None
        for side, ref in ((0, own_ref), (1, other_ref)):
            for q in range(2):
                block = jnp.concatenate([ref[q * 8 + 2 * pair], ref[q * 8 + 2 * pair + 1]], 1)
                high, low = split(block)
                left_high, left_low = lefts[2 * side + q]
                term = mm(left_high, high) + (mm(left_high, low) + mm(left_low, high))
                total = term if total is None else total + term
        out_ref[:, cols] = base_ref[:, cols] - total

    slot = info[2]
    offset = pl.multiple_of(info[3], 64)

    if half == 1:

        @pl.when(info[1] == 0)
        def _():
            out_ref[pl.ds(0, 64), :] = base_ref[pl.ds(0, 64), :]

    for ref, want in ((own_ref, 0), (other_ref, 1)):

        @pl.when((info[1] == half) & (info[4] == want))
        def _():
            for n in range(8):
                out_ref[pl.ds(0, 64), pl.ds(n * TILE, TILE)] = ref[slot * 8 + n, pl.ds(offset, 64), :]


def update(half, info, base, left, own, other):
    def body(*refs):
        update_body(half, *refs)

    return pl.pallas_call(
        body,
        out_shape=jax.ShapeDtypeStruct(base.shape, F32),
        in_specs=[SM, VM, VM, VM, VM],
        out_specs=VM,
        compiler_params=PARAMS,
        name="update_first" if half == 0 else "update_second",
    )(info, base, left, own, other)


def deal(x, core, yh, xi, core_from, yh_from):
    half_there = x[512 * (1 - core_from) : 512 * (2 - core_from)]
    half_here = x[512 * core_from : 512 * (core_from + 1)]
    half = jnp.where(
        core == core_from, half_here, lax.ppermute(half_there, "core", [(core_from, 1 - core_from)])
    )
    there = half[256 * (1 - yh_from) : 256 * (2 - yh_from)]
    here = half[256 * yh_from : 256 * (yh_from + 1)]
    quarter = jnp.where(yh == yh_from, here, lax.ppermute(there, "yh", [(yh_from, 1 - yh_from)]))
    sent = [lax.ppermute(quarter, "x", [(0, k)]) for k in (2, 1, 3)]
    return jnp.where(xi == 0, quarter, sent[0] + sent[1] + sent[2])


def gather_solution(quarter):
    own = lax.all_gather(quarter, COL, axis=0, tiled=False)
    other = lax.ppermute(own, "core", [(0, 1), (1, 0)])
    return own, other


def shards(factor, cross_cov):
    xi, core = lax.axis_index("x"), lax.axis_index("core")
    yh, yl, z = lax.axis_index("yh"), lax.axis_index("yl"), lax.axis_index("z")
    row_id = 2 * xi + core
    col_id = 8 * yh + 4 * yl + z
    slice_id = 4 * yl + z
    local = factor[:, 0]
    rhs = cross_cov[:, 0]

    own_rhs = rhs[0].reshape(64, 8, TILE).transpose(1, 0, 2)
    columns = lax.all_to_all(jnp.concatenate([own_rhs, own_rhs], 0), COL, 0, 0, tiled=True)
    columns = columns.reshape(1024, TILE)

    diagonal = ((row_id == 0) & (yh == 0)) | ((row_id == 1) & (yh == 1))
    info = jnp.stack([diagonal.astype(jnp.int32), slice_id.astype(jnp.int32)])
    lead = invert_diagonal(info, local[0])
    tri = lax.all_gather(lead, ("yl", "z"), axis=0, tiled=False)

    first = solve(tri, columns)
    sent = lax.ppermute(first, "core", [(0, 1)])
    second_rhs = lax.ppermute(residual(tri, columns, sent), "yh", [(0, 1)])
    second = solve(tri, second_rhs)

    by_rows = local.reshape(4, 16, 64, TILE).transpose(1, 0, 2, 3).reshape(16, 256, TILE)
    by_rows, _ = lax.optimization_barrier((by_rows, tri[0, :8]))
    left = lax.all_to_all(by_rows, COL, 0, 0, tiled=True)

    quarter_of_mine = col_id // 4
    info2 = jnp.stack(
        [
            core,
            row_id,
            quarter_of_mine % 2,
            (col_id % 4) * 64,
            (quarter_of_mine // 2 != core).astype(jnp.int32),
        ]
    ).astype(jnp.int32)
    base = rhs.reshape(256, 1024)
    own0, other0 = gather_solution(deal(first, core, yh, xi, 0, 0))
    partly = update(0, info2, base, left, own0, other0)
    own1, other1 = gather_solution(deal(second, core, yh, xi, 1, 1))
    out = update(1, info2, partly, left, own1, other1)
    return out.reshape(4, 1, 64, 1024)


def solution(mesh):
    fine = Mesh(mesh.devices.reshape(4, 2, 2, 2, 4), ROW + COL)
    return jax.shard_map(
        shards,
        mesh=fine,
        in_specs=(P(None, ROW, None, COL), P(None, ROW, COL, None)),
        out_specs=P(None, ROW, COL, None),
        check_vma=False,
    )
```

```python
import jax
import jax.numpy as jnp
import numpy as np
from jax import lax
from jax.experimental import pallas as pl
from jax.experimental.pallas import tpu as pltpu
from jax.sharding import Mesh, PartitionSpec as P

ROW = ("x", "core")
COL = ("yh", "yl", "z")
F32 = jnp.float32
BF16 = jnp.bfloat16
TILE = 128
PARAMS = pltpu.CompilerParams(vmem_limit_bytes=48 * 2**20)
VM = pl.BlockSpec(memory_space=pltpu.VMEM)
SM = pl.BlockSpec(memory_space=pltpu.SMEM)


def split(value):
    high = value.astype(BF16)
    return high, (value - high.astype(F32)).astype(BF16)


def mm(a, b):
    return jnp.dot(a, b, preferred_element_type=F32)


def pack_left(value):
    return jnp.concatenate(split(value), 1)


def pack_right(value):
    high, low = split(value)
    return jnp.concatenate(
        [jnp.concatenate([high, low], 1), jnp.concatenate([high, jnp.zeros_like(low)], 1)], 0
    )


def packed_product(left, right):
    out = mm(left, right)
    return out[:, :TILE] + out[:, TILE:]


def full_dot(a, b):
    return jnp.dot(a, b, precision=lax.Precision.HIGHEST, preferred_element_type=F32)


def invert_body(info, lead_ref, out_ref):
    out_ref[...] = lead_ref[...]

    @pl.when(info[0] == 1)
    def _():
        start = pl.multiple_of(info[1] * TILE, TILE)
        block = lead_ref[pl.ds(start, TILE), :]
        i = lax.broadcasted_iota(jnp.int32, (TILE, TILE), 0)
        j = lax.broadcasted_iota(jnp.int32, (TILE, TILE), 1)
        zero = jnp.zeros((TILE, TILE), F32)
        inverse = jnp.where(i == j, 1.0 / jnp.where(i == j, block, 1.0), zero)
        step = 1
        while step < TILE:
            below = ((i // (2 * step)) == (j // (2 * step))) & ((i // step) > (j // step))
            corner = jnp.where(below, block, zero)
            inverse = inverse - full_dot(inverse, full_dot(corner, inverse))
            step *= 2
        out_ref[pl.ds(start, TILE), :] = inverse


def invert_diagonal(info, lead):
    return pl.pallas_call(
        invert_body,
        out_shape=jax.ShapeDtypeStruct(lead.shape, F32),
        in_specs=[SM, VM],
        out_specs=VM,
        compiler_params=PARAMS,
        name="invert_diagonal",
    )(info, lead)


def solve_body(tri_ref, rhs_ref, out_ref):
    count = tri_ref.shape[0]
    out_ref[...] = rhs_ref[...]
    for k in range(count):
        here = pl.ds(k * TILE, TILE)
        solved = packed_product(pack_left(tri_ref[k, here, :]), pack_right(out_ref[here, :]))
        out_ref[here, :] = solved
        right = pack_right(solved)
        for i in range(k + 1, count):
            there = pl.ds(i * TILE, TILE)
            out_ref[there, :] = out_ref[there, :] - packed_product(pack_left(tri_ref[k, there, :]), right)


def solve(tri, rhs):
    return pl.pallas_call(
        solve_body,
        out_shape=jax.ShapeDtypeStruct(rhs.shape, F32),
        in_specs=[VM, VM],
        out_specs=VM,
        compiler_params=PARAMS,
        name="block_solve",
    )(tri, rhs)


def residual_body(tri_ref, rhs_ref, x_ref, out_ref):
    count = tri_ref.shape[0]
    for k in range(count):
        right = pack_right(x_ref[pl.ds(k * TILE, TILE), :])
        for i in range(count):
            there = pl.ds(i * TILE, TILE)
            base = rhs_ref[there, :] if k == 0 else out_ref[there, :]
            out_ref[there, :] = base - packed_product(pack_left(tri_ref[k, there, :]), right)


def residual(tri, rhs, x):
    return pl.pallas_call(
        residual_body,
        out_shape=jax.ShapeDtypeStruct(rhs.shape, F32),
        in_specs=[VM, VM, VM],
        out_specs=VM,
        compiler_params=PARAMS,
        name="block_residual",
    )(tri, rhs, x)


def prepare_body(info, left_ref, base_ref, high_ref, low_ref, out_ref):
    for h in range(2):
        for q in range(4):
            c = 8 * h + 2 * q
            high, low = split(jnp.concatenate([left_ref[c], left_ref[c + 1]], 1))
            high_ref[4 * h + q] = high
            low_ref[4 * h + q] = low
    out_ref[...] = base_ref[...]

    @pl.when(info[0] < 2)
    def _():
        for n in range(8):
            high_ref[n, pl.ds(0, 64), :] = jnp.zeros((64, 256), BF16)
            low_ref[n, pl.ds(0, 64), :] = jnp.zeros((64, 256), BF16)
        out_ref[pl.ds(0, 64), :] = jnp.zeros((64, 1024), F32)


def prepare(info, left, base):
    return pl.pallas_call(
        prepare_body,
        out_shape=[
            jax.ShapeDtypeStruct((8, 256, 256), BF16),
            jax.ShapeDtypeStruct((8, 256, 256), BF16),
            jax.ShapeDtypeStruct(base.shape, F32),
        ],
        in_specs=[SM, VM, VM],
        out_specs=[VM, VM, VM],
        compiler_params=PARAMS,
        name="prepare_update",
    )(info, left, base)


def accumulate(info, base, high, low, pieces, places, name):
    def body(info, base_ref, high_ref, low_ref, *refs):
        out_ref = refs[-1]
        row, core, y, z, col = (info[k] for k in range(5))
        out_ref[...] = base_ref[...]
        for ref, (side, far, slot) in zip(refs, places):
            holder = core if side == 0 else 1 - core
            for n in range(ref.shape[0]):
                near = slot + n
                py = lax.rem(y + jnp.where(holder == 0, far, near), 4)
                pz = lax.rem(z + jnp.where(holder == 0, near, far), 4)
                upper = py // 2
                bit = jnp.where(upper == 0, py, 3 - py)
                cols = pl.ds(pl.multiple_of((4 * bit + pz) * TILE, TILE), TILE)
                q = 2 * holder + upper
                total = None
                for h in range(2):
                    x_high, x_low = split(ref[n, h])
                    left_high = high_ref[4 * h + q]
                    wide = mm(left_high, jnp.concatenate([x_high, x_low], 1))
                    term = wide[:, :TILE] + (wide[:, TILE:] + mm(low_ref[4 * h + q], x_high))
                    total = term if total is None else total + term
                out_ref[:, cols] = out_ref[:, cols] - total

                @pl.when((row < 2) & (col // 4 == q))
                def _():
                    there = pl.ds(pl.multiple_of(lax.rem(col, 4) * 64, 64), 64)
                    out_ref[pl.ds(0, 64), cols] = out_ref[pl.ds(0, 64), cols] + ref[n, row, there, :]

    return pl.pallas_call(
        body,
        out_shape=jax.ShapeDtypeStruct(base.shape, F32),
        in_specs=[SM] + [VM] * (3 + len(pieces)),
        out_specs=VM,
        input_output_aliases={1: 0},
        compiler_params=PARAMS,
        name=name,
    )(info, base, high, low, *pieces)


AXES = ROW + COL


def move(value, where):
    pairs = []
    for x in range(4):
        for core in range(2):
            for y in range(4):
                for z in range(4):
                    to = where(x, core, y, z)
                    if to is not None:
                        a, b, c, d = to
                        pairs.append((((x * 2 + core) * 4 + y) * 4 + z, ((a * 2 + b) * 4 + c % 4) * 4 + d % 4))
    return lax.ppermute(value, AXES, pairs)


def deal(x, core, yh, xi, core_from, yh_from):
    top = core_from == 0
    half_here, half_there = (x[:512], x[512:]) if top else (x[512:], x[:512])
    got = move(half_there, lambda a, b, c, d: (0, 1 - b, c, d) if a == 0 and b == core_from else None)
    half = jnp.where(core == core_from, half_here, got)
    here, there = (half[:256], half[256:]) if yh_from == 0 else (half[256:], half[:256])
    got = move(there, lambda a, b, c, d: (0, b, 3 - c, d) if a == 0 and c // 2 == yh_from else None)
    quarter = jnp.where(yh == yh_from, here, got)
    one = move(quarter, lambda a, b, c, d: (1 if b == 0 else 3, b, c, d) if a == 0 else None)
    two = move(quarter, lambda a, b, c, d: (3 if b == 0 else 1, b, c, d) if a == 0 else None)
    far = move(one, lambda a, b, c, d: (2, b, c, d) if a == (1 if b == 0 else 3) else None)
    return jnp.where(xi == 0, quarter, one + two + far)


def ring(value, first):
    def along(step):
        def where(a, b, c, d):
            on_z = (b == 0) == first
            return (a, b, c, d + step) if on_z else (a, b, c + step, d)

        return where

    before = move(value, along(1))
    after = move(value, along(-1))
    cut = value.shape[0] // 2
    far_low = move(before[:cut], along(1))
    far_high = move(after[cut:], along(-1))
    return after, far_low, far_high, before


def shards(factor, cross_cov):
    xi, core = lax.axis_index("x"), lax.axis_index("core")
    yh, yl, z = lax.axis_index("yh"), lax.axis_index("yl"), lax.axis_index("z")
    row_id = 2 * xi + core
    col_id = 8 * yh + 4 * yl + z
    slice_id = 4 * yl + z
    local = factor[:, 0]
    rhs = cross_cov[:, 0]

    own_rhs = rhs[0].reshape(64, 8, TILE).transpose(1, 0, 2)
    columns = lax.all_to_all(jnp.concatenate([own_rhs, own_rhs], 0), COL, 0, 0, tiled=True)
    columns = columns.reshape(1024, TILE)

    diagonal = ((row_id == 0) & (yh == 0)) | ((row_id == 1) & (yh == 1))
    info = jnp.stack([diagonal.astype(jnp.int32), slice_id.astype(jnp.int32)])
    lead = invert_diagonal(info, local[0])
    tri = lax.all_gather(lead, ("yl", "z"), axis=0, tiled=False)

    by_rows = local.reshape(4, 16, 64, TILE).transpose(1, 0, 2, 3).reshape(16, 256, TILE)
    by_rows, tri = lax.optimization_barrier((by_rows, tri))
    left = lax.all_to_all(by_rows, COL, 0, 0, tiled=True)

    first = solve(tri, columns)
    sent = move(first, lambda a, b, c, d: (0, 1, c, d) if a == 0 and b == 0 and c < 2 else None)
    second_rhs = move(
        residual(tri, columns, sent),
        lambda a, b, c, d: (0, 1, 3 - c, d) if a == 0 and b == 1 and c < 2 else None,
    )
    second = solve(tri, second_rhs)
    dealt0 = deal(first, core, yh, xi, 0, 0)
    second, left = lax.optimization_barrier((second, left))
    dealt1 = deal(second, core, yh, xi, 1, 1)

    info2 = jnp.stack([row_id, core, 2 * yh + yl, z, col_id]).astype(jnp.int32)
    high, low, out = prepare(info2[:1], left, rhs.reshape(256, 1024))

    def swap(value):
        return move(value, lambda a, b, c, d: (a, 1 - b, c, d))

    mine = jnp.stack([dealt0, dealt1])
    after, far_low, far_high, before = ring(mine, True)
    near = jnp.stack([mine, after, jnp.concatenate([far_low, far_high], 0), before])
    near_other = swap(near)
    after, far_low, far_high, before = ring(near, False)
    out = accumulate(info2, out, high, low, [near, near_other], [(0, 0, 0), (1, 0, 0)], "update_near")
    out = accumulate(
        info2, out, high, low, [after, before, swap(after), swap(before)],
        [(0, 1, 0), (0, 3, 0), (1, 1, 0), (1, 3, 0)], "update_next",
    )
    out = accumulate(
        info2, out, high, low, [far_low, far_high, swap(far_low), swap(far_high)],
        [(0, 2, 0), (0, 2, 2), (1, 2, 0), (1, 2, 2)], "update_far",
    )
    return out.reshape(4, 1, 64, 1024)


def solution(mesh):
    fine = Mesh(mesh.devices.reshape(4, 2, 2, 2, 4), ROW + COL)
    return jax.shard_map(
        shards,
        mesh=fine,
        in_specs=(P(None, ROW, None, COL), P(None, ROW, COL, None)),
        out_specs=P(None, ROW, COL, None),
        check_vma=False,
    )
```

```python
import jax
import jax.numpy as jnp
import numpy as np
from jax import lax
from jax.experimental import pallas as pl
from jax.experimental.pallas import tpu as pltpu
from jax.sharding import Mesh, PartitionSpec as P

ROW = ("x", "core")
COL = ("yh", "yl", "z")
F32 = jnp.float32
BF16 = jnp.bfloat16
TILE = 128
PARAMS = pltpu.CompilerParams(vmem_limit_bytes=48 * 2**20)
VM = pl.BlockSpec(memory_space=pltpu.VMEM)
SM = pl.BlockSpec(memory_space=pltpu.SMEM)


def split(value):
    high = value.astype(BF16)
    return high, (value - high.astype(F32)).astype(BF16)


def mm(a, b):
    return jnp.dot(a, b, preferred_element_type=F32)


def pack_left(value):
    return jnp.concatenate(split(value), 1)


def pack_right(value):
    high, low = split(value)
    return jnp.concatenate(
        [jnp.concatenate([high, low], 1), jnp.concatenate([high, jnp.zeros_like(low)], 1)], 0
    )


def packed_product(left, right):
    out = mm(left, right)
    return out[:, :TILE] + out[:, TILE:]


def invert_body(info, lead_ref, out_ref):
    out_ref[...] = lead_ref[...]

    @pl.when(info[0] == 1)
    def _():
        start = pl.multiple_of(info[1] * TILE, TILE)
        block = lead_ref[pl.ds(start, TILE), :]
        i = lax.broadcasted_iota(jnp.int32, (TILE, TILE), 0)
        j = lax.broadcasted_iota(jnp.int32, (TILE, TILE), 1)
        zero = jnp.zeros((TILE, TILE), F32)
        inverse = jnp.where(i == j, 1.0 / jnp.where(i == j, block, 1.0), zero)
        step = 1
        while step < TILE:
            below = ((i // (2 * step)) == (j // (2 * step))) & ((i // step) > (j // step))
            corner = jnp.where(below, block, zero)
            product = packed_product(pack_left(corner), pack_right(inverse))
            inverse = inverse - packed_product(pack_left(inverse), pack_right(product))
            step *= 2
        out_ref[pl.ds(start, TILE), :] = inverse


def invert_diagonal(info, lead):
    return pl.pallas_call(
        invert_body,
        out_shape=jax.ShapeDtypeStruct(lead.shape, F32),
        in_specs=[SM, VM],
        out_specs=VM,
        compiler_params=PARAMS,
        name="invert_diagonal",
    )(info, lead)


def pack_slices(info, pieces, places, name):
    def body(info, *refs):
        out_ref = refs[-1]
        for ref, parts in zip(refs, places):
            for group, steps, start, to, rows in parts:
                half = {"own": info[0], "pair": 1 - info[0]}.get(group, group)
                k = 4 * half + lax.rem(info[1] + steps, 4)
                out_ref[k, pl.ds(to, rows), :] = pack_left(ref[pl.ds(start, rows), :])

    return pl.pallas_call(
        body,
        out_shape=jax.ShapeDtypeStruct((8, 1024, 256), BF16),
        in_specs=[SM] + [VM] * len(pieces),
        out_specs=VM,
        compiler_params=PARAMS,
        name=name,
    )(info, *pieces)


def solve_body(tri_ref, rhs_ref, out_ref):
    count = tri_ref.shape[0]
    out_ref[...] = rhs_ref[...]
    for k in range(count):
        here = pl.ds(k * TILE, TILE)
        solved = packed_product(tri_ref[k, here, :], pack_right(out_ref[here, :]))
        out_ref[here, :] = solved
        right = pack_right(solved)
        for i in range(k + 1, count):
            there = pl.ds(i * TILE, TILE)
            out_ref[there, :] = out_ref[there, :] - packed_product(tri_ref[k, there, :], right)


def solve(tri, rhs):
    return pl.pallas_call(
        solve_body,
        out_shape=jax.ShapeDtypeStruct(rhs.shape, F32),
        in_specs=[VM, VM],
        out_specs=VM,
        compiler_params=PARAMS,
        name="block_solve",
    )(tri, rhs)


def residual_body(tri_ref, rhs_ref, x_ref, out_ref):
    count = tri_ref.shape[0]
    for k in range(count):
        right = pack_right(x_ref[pl.ds(k * TILE, TILE), :])
        for i in range(count):
            there = pl.ds(i * TILE, TILE)
            base = rhs_ref[there, :] if k == 0 else out_ref[there, :]
            out_ref[there, :] = base - packed_product(tri_ref[k, there, :], right)


def residual(tri, rhs, x):
    return pl.pallas_call(
        residual_body,
        out_shape=jax.ShapeDtypeStruct(rhs.shape, F32),
        in_specs=[VM, VM, VM],
        out_specs=VM,
        compiler_params=PARAMS,
        name="block_residual",
    )(tri, rhs, x)


def prepare_body(info, left_ref, base_ref, high_ref, low_ref, out_ref):
    for h in range(2):
        for q in range(4):
            c = 8 * h + 2 * q
            high, low = split(jnp.concatenate([left_ref[c], left_ref[c + 1]], 1))
            high_ref[4 * h + q] = high
            low_ref[4 * h + q] = low
    out_ref[...] = base_ref[...]

    @pl.when(info[0] < 2)
    def _():
        for n in range(8):
            high_ref[n, pl.ds(0, 64), :] = jnp.zeros((64, 256), BF16)
            low_ref[n, pl.ds(0, 64), :] = jnp.zeros((64, 256), BF16)
        out_ref[pl.ds(0, 64), :] = jnp.zeros((64, 1024), F32)


def prepare(info, left, base):
    return pl.pallas_call(
        prepare_body,
        out_shape=[
            jax.ShapeDtypeStruct((8, 256, 256), BF16),
            jax.ShapeDtypeStruct((8, 256, 256), BF16),
            jax.ShapeDtypeStruct(base.shape, F32),
        ],
        in_specs=[SM, VM, VM],
        out_specs=[VM, VM, VM],
        compiler_params=PARAMS,
        name="prepare_update",
    )(info, left, base)


def accumulate(info, base, high, low, pieces, places, name):
    def body(info, base_ref, high_ref, low_ref, *refs):
        out_ref = refs[-1]
        row, core, y, z, col = (info[k] for k in range(5))
        out_ref[...] = base_ref[...]
        for ref, (side, far, slot) in zip(refs, places):
            holder = core if side == 0 else 1 - core
            for n in range(ref.shape[0]):
                near = slot + n
                py = lax.rem(y + jnp.where(holder == 0, far, near), 4)
                pz = lax.rem(z + jnp.where(holder == 0, near, far), 4)
                upper = py // 2
                bit = jnp.where(upper == 0, py, 3 - py)
                cols = pl.ds(pl.multiple_of((4 * bit + pz) * TILE, TILE), TILE)
                q = 2 * holder + upper
                total = None
                for h in range(2):
                    x_high, x_low = split(ref[n, h])
                    left_high = high_ref[4 * h + q]
                    wide = mm(left_high, jnp.concatenate([x_high, x_low], 1))
                    term = wide[:, :TILE] + (wide[:, TILE:] + mm(low_ref[4 * h + q], x_high))
                    total = term if total is None else total + term
                out_ref[:, cols] = out_ref[:, cols] - total

                @pl.when((row < 2) & (col // 4 == q))
                def _():
                    there = pl.ds(pl.multiple_of(lax.rem(col, 4) * 64, 64), 64)
                    out_ref[pl.ds(0, 64), cols] = out_ref[pl.ds(0, 64), cols] + ref[n, row, there, :]

    return pl.pallas_call(
        body,
        out_shape=jax.ShapeDtypeStruct(base.shape, F32),
        in_specs=[SM] + [VM] * (3 + len(pieces)),
        out_specs=VM,
        input_output_aliases={1: 0},
        compiler_params=PARAMS,
        name=name,
    )(info, base, high, low, *pieces)


AXES = ROW + COL


def move(value, where):
    pairs = []
    for x in range(4):
        for core in range(2):
            for y in range(4):
                for z in range(4):
                    to = where(x, core, y, z)
                    if to is not None:
                        a, b, c, d = to
                        pairs.append((((x * 2 + core) * 4 + y) * 4 + z, ((a * 2 + b) * 4 + c % 4) * 4 + d % 4))
    return lax.ppermute(value, AXES, pairs)


def deal(x, core, yh, xi, core_from, yh_from):
    top = core_from == 0
    half_here, half_there = (x[:512], x[512:]) if top else (x[512:], x[:512])
    got = move(half_there, lambda a, b, c, d: (0, 1 - b, c, d) if a == 0 and b == core_from else None)
    half = jnp.where(core == core_from, half_here, got)
    here, there = (half[:256], half[256:]) if yh_from == 0 else (half[256:], half[:256])
    got = move(there, lambda a, b, c, d: (0, b, 3 - c, d) if a == 0 and c // 2 == yh_from else None)
    quarter = jnp.where(yh == yh_from, here, got)
    one = move(quarter, lambda a, b, c, d: (1 if b == 0 else 3, b, c, d) if a == 0 else None)
    two = move(quarter, lambda a, b, c, d: (3 if b == 0 else 1, b, c, d) if a == 0 else None)
    far = move(one, lambda a, b, c, d: (2, b, c, d) if a == (1 if b == 0 else 3) else None)
    return jnp.where(xi == 0, quarter, one + two + far)


def ring(value, first):
    def along(step):
        def where(a, b, c, d):
            on_z = (b == 0) == first
            return (a, b, c, d + step) if on_z else (a, b, c + step, d)

        return where

    before = move(value, along(1))
    after = move(value, along(-1))
    cut = value.shape[0] // 2
    far_low = move(before[:cut], along(1))
    far_high = move(after[cut:], along(-1))
    return after, far_low, far_high, before


def gather_first(lead, yl):
    swapped = move(lead, lambda a, b, c, d: (0, 0, 1 - c, d) if a == 0 and b == 0 and c < 2 else None)
    full = jnp.where(yl == 0, lead, swapped)
    lower = jnp.where(yl == 0, swapped[512:], lead[512:])
    pair = jnp.concatenate([full, lower], 0)

    def along(step):
        return lambda a, b, c, d: (0, 0, c, d + step) if a == 0 and b == 0 and c < 2 else None

    before, after = move(pair, along(1)), move(pair, along(-1))
    far_low, far_high = move(before[:768], along(1)), move(after[768:], along(-1))
    pieces, places = [], []
    for piece, steps in ((pair, 0), (after, 1), (before, 3)):
        pieces.append(piece)
        places.append([(0, steps, 0, 0, 1024), (1, steps, 1024, 512, 512)])
    pieces += [far_low, far_high]
    places += [[(0, 2, 0, 0, 768)], [(0, 2, 0, 768, 256), (1, 2, 256, 512, 512)]]
    return pieces, places


def gather_second(lead):
    def along(step):
        return lambda a, b, c, d: (0, 1, c, d + step) if a == 0 and b == 1 else None

    def pair(value):
        return move(value, lambda a, b, c, d: (0, 1, c + 1 - 2 * (c % 2), d) if a == 0 and b == 1 else None)

    before, after = move(lead, along(1)), move(lead, along(-1))
    far_low, far_high = move(before[:512], along(1)), move(after[512:], along(-1))
    pieces, places = [], []
    for piece, steps, row in ((lead, 0, 0), (after, 1, 0), (before, 3, 0), (far_low, 2, 0), (far_high, 2, 512)):
        for group, value in (("own", piece), ("pair", pair(piece))):
            pieces.append(value)
            places.append([(group, steps, 0, row, value.shape[0])])
    return pieces, places


def shards(factor, cross_cov):
    xi, core = lax.axis_index("x"), lax.axis_index("core")
    yh, yl, z = lax.axis_index("yh"), lax.axis_index("yl"), lax.axis_index("z")
    row_id = 2 * xi + core
    col_id = 8 * yh + 4 * yl + z
    slice_id = 4 * yl + z
    local = factor[:, 0]
    rhs = cross_cov[:, 0]

    diagonal = ((row_id == 0) & (yh == 0)) | ((row_id == 1) & (yh == 1))
    info = jnp.stack([diagonal.astype(jnp.int32), slice_id.astype(jnp.int32)])
    lead = invert_diagonal(info, local[0])

    own_rhs = rhs[0].reshape(64, 2, 4, TILE).transpose(1, 2, 0, 3)
    own_rhs = jnp.where(yh == 0, own_rhs, own_rhs[::-1]).reshape(8, 64, TILE)
    half = lax.all_to_all(own_rhs, ("yl", "z"), 0, 0, tiled=True).reshape(512, TILE)
    other_half = move(half, lambda a, b, c, d: (0, b, 3 - c, d) if a == 0 and c >= 2 else None)
    columns = jnp.concatenate([half, other_half], 0)

    place = jnp.stack([yl, z]).astype(jnp.int32)
    tri_first = pack_slices(place, *gather_first(lead, yl), "pack_first")
    tri_second = pack_slices(place, *gather_second(lead), "pack_second")

    first = solve(tri_first, columns)
    sent = move(first, lambda a, b, c, d: (0, 1, c, d) if a == 0 and b == 0 and c < 2 else None)
    second_rhs = move(
        residual(tri_second, columns, sent),
        lambda a, b, c, d: (0, 1, 3 - c, d) if a == 0 and b == 1 and c < 2 else None,
    )
    by_rows = local.reshape(4, 16, 64, TILE).transpose(1, 0, 2, 3).reshape(16, 256, TILE)
    by_rows, second_rhs = lax.optimization_barrier((by_rows, second_rhs))
    left = lax.all_to_all(by_rows, COL, 0, 0, tiled=True)
    second = solve(tri_second, second_rhs)
    dealt0 = deal(first, core, yh, xi, 0, 0)
    dealt1 = deal(second, core, yh, xi, 1, 1)

    info2 = jnp.stack([row_id, core, 2 * yh + yl, z, col_id]).astype(jnp.int32)

    def swap(value):
        return move(value, lambda a, b, c, d: (a, 1 - b, c, d))

    def add(out, pieces, places, name):
        return accumulate(info2, out, high, low, pieces, places, name)

    mine = jnp.stack([dealt0, dealt1])
    after, far_low, far_high, before = ring(mine, True)
    near = jnp.stack([mine, after, jnp.concatenate([far_low, far_high], 0), before])

    def along(step):
        return lambda a, b, c, d: (a, b, c + step, d) if b == 0 else (a, b, c, d + step)

    before, after, near_other = move(near, along(1)), move(near, along(-1)), swap(near)
    high, low, out = prepare(info2[:1], left, rhs.reshape(256, 1024))
    out = add(out, [near], [(0, 0, 0)], "update_near")
    before, after, out = lax.optimization_barrier((before, after, out))
    far_low, far_high = move(before[:2], along(1)), move(after[2:], along(-1))
    before_other, after_other = swap(before), swap(after)
    out = add(out, [near_other, after, before], [(1, 0, 0), (0, 1, 0), (0, 3, 0)], "update_next")
    far_low, far_high, out = lax.optimization_barrier((far_low, far_high, out))
    far_low_other, far_high_other = swap(far_low), swap(far_high)
    out = add(
        out, [after_other, before_other, far_low, far_high],
        [(1, 1, 0), (1, 3, 0), (0, 2, 0), (0, 2, 2)], "update_far",
    )
    out = add(out, [far_low_other, far_high_other], [(1, 2, 0), (1, 2, 2)], "update_last")
    return out.reshape(4, 1, 64, 1024)


def solution(mesh):
    fine = Mesh(mesh.devices.reshape(4, 2, 2, 2, 4), ROW + COL)
    return jax.shard_map(
        shards,
        mesh=fine,
        in_specs=(P(None, ROW, None, COL), P(None, ROW, COL, None)),
        out_specs=P(None, ROW, COL, None),
        check_vma=False,
    )
```

```python
import jax
import jax.numpy as jnp
import numpy as np
from jax import lax
from jax.experimental import pallas as pl
from jax.experimental.pallas import tpu as pltpu
from jax.sharding import Mesh, PartitionSpec as P

ROW = ("x", "core")
COL = ("yh", "yl", "z")
F32 = jnp.float32
BF16 = jnp.bfloat16
TILE = 128
PARAMS = pltpu.CompilerParams(vmem_limit_bytes=20 * 2**20)
VM = pl.BlockSpec(memory_space=pltpu.VMEM)
SM = pl.BlockSpec(memory_space=pltpu.SMEM)


def split(value):
    high = value.astype(BF16)
    return high, (value - high.astype(F32)).astype(BF16)


def mm(a, b):
    return jnp.dot(a, b, preferred_element_type=F32)


def pack_left(value):
    return jnp.concatenate(split(value), 1)


def pack_right(value):
    high, low = split(value)
    return jnp.concatenate(
        [jnp.concatenate([high, low], 1), jnp.concatenate([high, jnp.zeros_like(low)], 1)], 0
    )


def packed_product(left, right):
    out = mm(left, right)
    return out[:, :TILE] + out[:, TILE:]


def invert_body(info, lead_ref, out_ref):
    out_ref[...] = lead_ref[...]

    @pl.when(info[0] == 1)
    def _():
        start = pl.multiple_of(info[1] * TILE, TILE)
        block = lead_ref[pl.ds(start, TILE), :]
        i = lax.broadcasted_iota(jnp.int32, (TILE, TILE), 0)
        j = lax.broadcasted_iota(jnp.int32, (TILE, TILE), 1)
        zero = jnp.zeros((TILE, TILE), F32)
        inverse = jnp.where(i == j, 1.0 / jnp.where(i == j, block, 1.0), zero)
        step = 1
        while step < TILE:
            below = ((i // (2 * step)) == (j // (2 * step))) & ((i // step) > (j // step))
            corner = jnp.where(below, block, zero)
            product = packed_product(pack_left(corner), pack_right(inverse))
            inverse = inverse - packed_product(pack_left(inverse), pack_right(product))
            step *= 2
        out_ref[pl.ds(start, TILE), :] = inverse


def invert_diagonal(info, lead):
    return pl.pallas_call(
        invert_body,
        out_shape=jax.ShapeDtypeStruct(lead.shape, F32),
        in_specs=[SM, VM],
        out_specs=VM,
        compiler_params=PARAMS,
        name="invert_diagonal",
    )(info, lead)


def pack_and_solve(info, pieces, places, rhs):
    def body(info, *refs):
        rhs_ref, tri_ref, out_ref = refs[-3:]
        for ref, (other, steps, row) in zip(refs, places):
            half = 1 - info[0] if other else info[0]
            k = 4 * half + lax.rem(info[1] + steps, 4)
            tri_ref[k, pl.ds(row, ref.shape[0]), :] = pack_left(ref[...])
        solve_body(tri_ref, rhs_ref, out_ref)

    return pl.pallas_call(
        body,
        out_shape=[jax.ShapeDtypeStruct((8, 1024, 256), BF16), jax.ShapeDtypeStruct(rhs.shape, F32)],
        in_specs=[SM] + [VM] * (len(pieces) + 1),
        out_specs=[VM, VM],
        compiler_params=PARAMS,
        name="pack_and_solve",
    )(info, *pieces, rhs)


def solve_body(tri_ref, rhs_ref, out_ref):
    count = tri_ref.shape[0]
    out_ref[...] = rhs_ref[...]
    for k in range(count):
        here = pl.ds(k * TILE, TILE)
        solved = packed_product(tri_ref[k, here, :], pack_right(out_ref[here, :]))
        out_ref[here, :] = solved
        right = pack_right(solved)
        for i in range(k + 1, count):
            there = pl.ds(i * TILE, TILE)
            out_ref[there, :] = out_ref[there, :] - packed_product(tri_ref[k, there, :], right)


def solve(tri, rhs):
    return pl.pallas_call(
        solve_body,
        out_shape=jax.ShapeDtypeStruct(rhs.shape, F32),
        in_specs=[VM, VM],
        out_specs=VM,
        compiler_params=PARAMS,
        name="block_solve",
    )(tri, rhs)


def residual_body(tri_ref, rhs_ref, x_ref, out_ref):
    count = tri_ref.shape[0]
    for k in range(count):
        right = pack_right(x_ref[pl.ds(k * TILE, TILE), :])
        for i in range(count):
            there = pl.ds(i * TILE, TILE)
            base = rhs_ref[there, :] if k == 0 else out_ref[there, :]
            out_ref[there, :] = base - packed_product(tri_ref[k, there, :], right)


def residual(tri, rhs, x):
    return pl.pallas_call(
        residual_body,
        out_shape=jax.ShapeDtypeStruct(rhs.shape, F32),
        in_specs=[VM, VM, VM],
        out_specs=VM,
        compiler_params=PARAMS,
        name="block_residual",
    )(tri, rhs, x)


def prepare_body(info, left_ref, base_ref, high_ref, low_ref, out_ref):
    for h in range(2):
        for q in range(4):
            c = 8 * h + 2 * q
            high, low = split(jnp.concatenate([left_ref[c], left_ref[c + 1]], 1))
            high_ref[4 * h + q] = high
            low_ref[4 * h + q] = low
    out_ref[...] = base_ref[...]

    @pl.when(info[0] < 2)
    def _():
        for n in range(8):
            high_ref[n, pl.ds(0, 64), :] = jnp.zeros((64, 256), BF16)
            low_ref[n, pl.ds(0, 64), :] = jnp.zeros((64, 256), BF16)
        out_ref[pl.ds(0, 64), :] = jnp.zeros((64, 1024), F32)


def prepare(info, left, base):
    return pl.pallas_call(
        prepare_body,
        out_shape=[
            jax.ShapeDtypeStruct((8, 256, 256), BF16),
            jax.ShapeDtypeStruct((8, 256, 256), BF16),
            jax.ShapeDtypeStruct(base.shape, F32),
        ],
        in_specs=[SM, VM, VM],
        out_specs=[VM, VM, VM],
        compiler_params=PARAMS,
        name="prepare_update",
    )(info, left, base)


def accumulate(info, base, high, low, pieces, places, name):
    def body(info, base_ref, high_ref, low_ref, *refs):
        out_ref = refs[-1]
        row, core, y, z, col = (info[k] for k in range(5))
        out_ref[...] = base_ref[...]
        for ref, (side, far, slot) in zip(refs, places):
            holder = core if side == 0 else 1 - core
            for n in range(ref.shape[0]):
                near = slot + n
                py = lax.rem(y + jnp.where(holder == 0, far, near), 4)
                pz = lax.rem(z + jnp.where(holder == 0, near, far), 4)
                upper = py // 2
                bit = jnp.where(upper == 0, py, 3 - py)
                cols = pl.ds(pl.multiple_of((4 * bit + pz) * TILE, TILE), TILE)
                q = 2 * holder + upper
                total = None
                for h in range(2):
                    x_high, x_low = split(ref[n, h])
                    left_high = high_ref[4 * h + q]
                    wide = mm(left_high, jnp.concatenate([x_high, x_low], 1))
                    term = wide[:, :TILE] + (wide[:, TILE:] + mm(low_ref[4 * h + q], x_high))
                    total = term if total is None else total + term
                out_ref[:, cols] = out_ref[:, cols] - total

                @pl.when((row < 2) & (col // 4 == q))
                def _():
                    there = pl.ds(pl.multiple_of(lax.rem(col, 4) * 64, 64), 64)
                    out_ref[pl.ds(0, 64), cols] = out_ref[pl.ds(0, 64), cols] + ref[n, row, there, :]

    return pl.pallas_call(
        body,
        out_shape=jax.ShapeDtypeStruct(base.shape, F32),
        in_specs=[SM] + [VM] * (3 + len(pieces)),
        out_specs=VM,
        input_output_aliases={1: 0},
        compiler_params=PARAMS,
        name=name,
    )(info, base, high, low, *pieces)


AXES = ROW + COL


def move(value, where):
    pairs = []
    for x in range(4):
        for core in range(2):
            for y in range(4):
                for z in range(4):
                    to = where(x, core, y, z)
                    if to is not None:
                        a, b, c, d = to
                        pairs.append((((x * 2 + core) * 4 + y) * 4 + z, ((a * 2 + b) * 4 + c % 4) * 4 + d % 4))
    return lax.ppermute(value, AXES, pairs)


def deal(x, core, yh, xi, core_from, yh_from):
    top = core_from == 0
    half_here, half_there = (x[:512], x[512:]) if top else (x[512:], x[:512])
    got = move(half_there, lambda a, b, c, d: (0, 1 - b, c, d) if a == 0 and b == core_from else None)
    half = jnp.where(core == core_from, half_here, got)
    here, there = (half[:256], half[256:]) if yh_from == 0 else (half[256:], half[:256])
    got = move(there, lambda a, b, c, d: (0, b, 3 - c, d) if a == 0 and c // 2 == yh_from else None)
    quarter = jnp.where(yh == yh_from, here, got)
    one = move(quarter, lambda a, b, c, d: (1 if b == 0 else 3, b, c, d) if a == 0 else None)
    two = move(quarter, lambda a, b, c, d: (3 if b == 0 else 1, b, c, d) if a == 0 else None)
    far = move(one, lambda a, b, c, d: (2, b, c, d) if a == (1 if b == 0 else 3) else None)
    return jnp.where(xi == 0, quarter, one + two + far)


def ring(value, first):
    def along(step):
        def where(a, b, c, d):
            on_z = (b == 0) == first
            return (a, b, c, d + step) if on_z else (a, b, c + step, d)

        return where

    before = move(value, along(1))
    after = move(value, along(-1))
    cut = value.shape[0] // 2
    far_low = move(before[:cut], along(1))
    far_high = move(after[cut:], along(-1))
    return after, far_low, far_high, before


def holds(a, b, c):
    return (a, b, c // 2) in ((0, 0, 0), (0, 1, 1), (1, 0, 0))


def gather_slices(lead, xi):
    def flip(c):
        return c + 1 - 2 * (c % 2)

    def across(a, b, c, d):
        return (1 if b == 1 and c < 2 else 0, 0 if c < 2 else 1, flip(c), d) if a == 0 and (b == 1 or c < 2) else None

    def along(step):
        return lambda a, b, c, d: (a, b, c, d + step) if holds(a, b, c) else None

    hop = move(lead, lambda a, b, c, d: (1, 0, c, d) if (a, b) == (0, 1) and c < 2 else None)
    pair = move(lead, across)
    own = jnp.where(xi == 1, hop, lead)
    pieces, places = [], []
    for other, value in ((False, own), (True, pair)):
        before, after = move(value, along(1)), move(value, along(-1))
        far_low, far_high = move(before[:512], along(1)), move(after[512:], along(-1))
        pieces += [value, after, before, far_low, far_high]
        places += [(other, 0, 0), (other, 1, 0), (other, 3, 0), (other, 2, 0), (other, 2, 512)]
    return pieces, places


def shards(factor, cross_cov):
    xi, core = lax.axis_index("x"), lax.axis_index("core")
    yh, yl, z = lax.axis_index("yh"), lax.axis_index("yl"), lax.axis_index("z")
    row_id = 2 * xi + core
    col_id = 8 * yh + 4 * yl + z
    slice_id = 4 * yl + z
    local = factor[:, 0]
    rhs = cross_cov[:, 0]

    diagonal = ((row_id == 0) & (yh == 0)) | ((row_id == 1) & (yh == 1))
    info = jnp.stack([diagonal.astype(jnp.int32), slice_id.astype(jnp.int32)])
    lead = invert_diagonal(info, local[0])
    pieces, places = gather_slices(lead, xi)

    own_rhs = rhs[0].reshape(64, 2, 4, TILE).transpose(1, 2, 0, 3)
    own_rhs = jnp.where(yh == 0, own_rhs, own_rhs[::-1]).reshape(8, 64, TILE)
    half = lax.all_to_all(own_rhs, ("yl", "z"), 0, 0, tiled=True).reshape(512, TILE)
    half, pieces[6] = lax.optimization_barrier((half, pieces[6]))
    low_half = move(half, lambda a, b, c, d: (1, 0, c, d) if (a, b) == (0, 1) and c < 2 else None)
    high_half = move(half, lambda a, b, c, d: (b, 0, 3 - c, d) if a == 0 and c >= 2 else None)
    columns = jnp.concatenate([jnp.where(xi == 1, low_half, half), high_half], 0)

    place = jnp.stack([yl, z]).astype(jnp.int32)
    tri, first = pack_and_solve(place, pieces, places, columns)
    sent = move(first, lambda a, b, c, d: (1, 0, c, d) if a == 0 and b == 0 and c < 2 else None)
    rest = residual(tri, columns, sent)
    second_rhs = move(rest, lambda a, b, c, d: (0, 1, 3 - c, d) if (a, b) == (1, 0) and c < 2 else None)

    by_rows = local.reshape(4, 16, 64, TILE).transpose(1, 0, 2, 3).reshape(16, 256, TILE)
    by_rows, rest = lax.optimization_barrier((by_rows, sent))
    left = lax.all_to_all(by_rows, COL, 0, 0, tiled=True)
    dealt0 = deal(first, core, yh, xi, 0, 0)
    second_rhs, dealt0 = lax.optimization_barrier((second_rhs, dealt0))
    second = solve(tri, second_rhs)
    dealt1 = deal(second, core, yh, xi, 1, 1)
    dealt1, left = lax.optimization_barrier((dealt1, left))

    info2 = jnp.stack([row_id, core, 2 * yh + yl, z, col_id]).astype(jnp.int32)

    def swap(value):
        return move(value, lambda a, b, c, d: (a, 1 - b, c, d))

    def add(out, pieces, places, name):
        return accumulate(info2, out, high, low, pieces, places, name)

    mine = jnp.stack([dealt0, dealt1])
    after, far_low, far_high, before = ring(mine, True)
    near = jnp.stack([mine, after, jnp.concatenate([far_low, far_high], 0), before])

    def along(step):
        return lambda a, b, c, d: (a, b, c + step, d) if b == 0 else (a, b, c, d + step)

    before, after, near_other = move(near, along(1)), move(near, along(-1)), swap(near)
    high, low, out = prepare(info2[:1], left, rhs.reshape(256, 1024))
    out = add(out, [near], [(0, 0, 0)], "update_near")
    before, after, out = lax.optimization_barrier((before, after, out))
    far_low, far_high = move(before[:2], along(1)), move(after[2:], along(-1))
    before_other, after_other = swap(before), swap(after)
    out = add(out, [near_other, after, before], [(1, 0, 0), (0, 1, 0), (0, 3, 0)], "update_next")
    far_low, far_high, out = lax.optimization_barrier((far_low, far_high, out))
    far_low_other, far_high_other = swap(far_low), swap(far_high)
    out = add(
        out, [after_other, before_other, far_low, far_high],
        [(1, 1, 0), (1, 3, 0), (0, 2, 0), (0, 2, 2)], "update_far",
    )
    out = add(out, [far_low_other, far_high_other], [(1, 2, 0), (1, 2, 2)], "update_last")
    return out.reshape(4, 1, 64, 1024)


def solution(mesh):
    fine = Mesh(mesh.devices.reshape(4, 2, 2, 2, 4), ROW + COL)
    return jax.shard_map(
        shards,
        mesh=fine,
        in_specs=(P(None, ROW, None, COL), P(None, ROW, COL, None)),
        out_specs=P(None, ROW, COL, None),
        check_vma=False,
    )
```

```python
import jax
import jax.numpy as jnp
import numpy as np
from jax import lax
from jax.experimental import pallas as pl
from jax.experimental.pallas import tpu as pltpu
from jax.sharding import Mesh, PartitionSpec as P

ROW = ("x", "core")
COL = ("yh", "yl", "z")
F32 = jnp.float32
BF16 = jnp.bfloat16
TILE = 128
PARAMS = pltpu.CompilerParams(vmem_limit_bytes=20 * 2**20)
VM = pl.BlockSpec(memory_space=pltpu.VMEM)
SM = pl.BlockSpec(memory_space=pltpu.SMEM)


def split(value):
    high = value.astype(BF16)
    return high, (value - high.astype(F32)).astype(BF16)


def mm(a, b):
    return jnp.dot(a, b, preferred_element_type=F32)


def pack_left(value):
    return jnp.concatenate(split(value), 1)


def pack_right(value):
    high, low = split(value)
    return jnp.concatenate(
        [jnp.concatenate([high, low], 1), jnp.concatenate([high, jnp.zeros_like(low)], 1)], 0
    )


def packed_product(left, right):
    out = mm(left, right)
    return out[:, :TILE] + out[:, TILE:]


def invert_body(info, lead_ref, out_ref):
    out_ref[...] = lead_ref[...]

    @pl.when(info[0] == 1)
    def _():
        start = pl.multiple_of(info[1] * TILE, TILE)
        block = lead_ref[pl.ds(start, TILE), :]
        i = lax.broadcasted_iota(jnp.int32, (TILE, TILE), 0)
        j = lax.broadcasted_iota(jnp.int32, (TILE, TILE), 1)
        zero = jnp.zeros((TILE, TILE), F32)
        inverse = jnp.where(i == j, 1.0 / jnp.where(i == j, block, 1.0), zero)
        step = 1
        while step < TILE:
            below = ((i // (2 * step)) == (j // (2 * step))) & ((i // step) > (j // step))
            corner = jnp.where(below, block, zero)
            product = packed_product(pack_left(corner), pack_right(inverse))
            inverse = inverse - packed_product(pack_left(inverse), pack_right(product))
            step *= 2
        out_ref[pl.ds(start, TILE), :] = inverse


def invert_diagonal(info, lead):
    return pl.pallas_call(
        invert_body,
        out_shape=jax.ShapeDtypeStruct(lead.shape, F32),
        in_specs=[SM, VM],
        out_specs=VM,
        compiler_params=PARAMS,
        name="invert_diagonal",
    )(info, lead)


def pack_and_solve(info, pieces, places, rhs):
    def body(info, *refs):
        rhs_ref, tri_ref, out_ref = refs[-3:]
        for ref, (other, steps, row) in zip(refs, places):
            half = 1 - info[0] if other else info[0]
            k = 4 * half + lax.rem(info[1] + steps, 4)
            tri_ref[k, pl.ds(row, ref.shape[0]), :] = pack_left(ref[...])
        solve_body(tri_ref, rhs_ref, out_ref)

    return pl.pallas_call(
        body,
        out_shape=[jax.ShapeDtypeStruct((8, 1024, 256), BF16), jax.ShapeDtypeStruct(rhs.shape, F32)],
        in_specs=[SM] + [VM] * (len(pieces) + 1),
        out_specs=[VM, VM],
        compiler_params=PARAMS,
        name="pack_and_solve",
    )(info, *pieces, rhs)


def solve_body(tri_ref, rhs_ref, out_ref):
    count = tri_ref.shape[0]
    out_ref[...] = rhs_ref[...]
    for k in range(count):
        here = pl.ds(k * TILE, TILE)
        solved = packed_product(tri_ref[k, here, :], pack_right(out_ref[here, :]))
        out_ref[here, :] = solved
        right = pack_right(solved)
        for i in range(k + 1, count):
            there = pl.ds(i * TILE, TILE)
            out_ref[there, :] = out_ref[there, :] - packed_product(tri_ref[k, there, :], right)


def solve(tri, rhs):
    return pl.pallas_call(
        solve_body,
        out_shape=jax.ShapeDtypeStruct(rhs.shape, F32),
        in_specs=[VM, VM],
        out_specs=VM,
        compiler_params=PARAMS,
        name="block_solve",
    )(tri, rhs)


def residual_body(tri_ref, rhs_ref, x_ref, out_ref):
    count = tri_ref.shape[0]
    for k in range(count):
        right = pack_right(x_ref[pl.ds(k * TILE, TILE), :])
        for i in range(count):
            there = pl.ds(i * TILE, TILE)
            base = rhs_ref[there, :] if k == 0 else out_ref[there, :]
            out_ref[there, :] = base - packed_product(tri_ref[k, there, :], right)


def residual(tri, rhs, x):
    return pl.pallas_call(
        residual_body,
        out_shape=jax.ShapeDtypeStruct(rhs.shape, F32),
        in_specs=[VM, VM, VM],
        out_specs=VM,
        compiler_params=PARAMS,
        name="block_residual",
    )(tri, rhs, x)


def prepare_body(info, mine_ref, other_ref, high_ref, low_ref):
    for side, ref in enumerate((mine_ref, other_ref)):
        rows = pl.ds(256 * side, 256)
        for n in range(4):
            high, low = split(jnp.concatenate([ref[2 * n], ref[2 * n + 1]], 1))
            high_ref[n, rows, :] = high
            low_ref[n, rows, :] = low

    @pl.when(info[0] == 0)
    def _():
        for n in range(4):
            for side in range(2):
                high_ref[n, pl.ds(256 * side, 64), :] = jnp.zeros((64, 256), BF16)
                low_ref[n, pl.ds(256 * side, 64), :] = jnp.zeros((64, 256), BF16)


def prepare(info, mine, other):
    return pl.pallas_call(
        prepare_body,
        out_shape=[jax.ShapeDtypeStruct((4, 512, 256), BF16)] * 2,
        in_specs=[SM, VM, VM],
        out_specs=[VM, VM],
        compiler_params=PARAMS,
        name="prepare_update",
    )(info, mine, other)


def accumulate(info, sums, high, low, pieces, places, name):
    first = sums is None

    def body(info, high_ref, low_ref, *refs):
        out_ref = refs[-1]
        x, core, y, z, col = (info[k] for k in range(5))
        if first:
            out_ref[...] = jnp.zeros(out_ref.shape, F32)
        else:
            out_ref[...] = refs[0][...]
        for ref, (far, slot) in zip(refs[0 if first else 1 :], places):
            for n in range(ref.shape[0]):
                near = slot + n
                py = lax.rem(y + jnp.where(core == 0, far, near), 4)
                pz = lax.rem(z + jnp.where(core == 0, near, far), 4)
                upper = py // 2
                bit = jnp.where(upper == 0, py, 3 - py)
                cols = pl.ds(pl.multiple_of((4 * bit + pz) * TILE, TILE), TILE)
                total = None
                for h in range(2):
                    x_high, x_low = split(ref[n, h])
                    wide = mm(high_ref[2 * h + upper], jnp.concatenate([x_high, x_low], 1))
                    term = wide[:, :TILE] + (wide[:, TILE:] + mm(low_ref[2 * h + upper], x_high))
                    total = term if total is None else total + term
                out_ref[:, cols] = out_ref[:, cols] + total

                @pl.when((x == 0) & (col // 4 == 2 * core + upper))
                def _():
                    there = pl.ds(pl.multiple_of(lax.rem(col, 4) * 64, 64), 64)
                    for side in range(2):
                        here = pl.ds(256 * side, 64)
                        block = core if side == 0 else 1 - core
                        out_ref[here, cols] = out_ref[here, cols] - ref[n, block, there, :]

    start = [] if first else [sums]
    return pl.pallas_call(
        body,
        out_shape=jax.ShapeDtypeStruct((512, 1024), F32),
        in_specs=[SM] + [VM] * (2 + len(start) + len(pieces)),
        out_specs=VM,
        input_output_aliases={} if first else {3: 0},
        compiler_params=PARAMS,
        name=name,
    )(info, high, low, *start, *pieces)


AXES = ROW + COL


def move(value, where):
    pairs = []
    for x in range(4):
        for core in range(2):
            for y in range(4):
                for z in range(4):
                    to = where(x, core, y, z)
                    if to is not None:
                        a, b, c, d = to
                        pairs.append((((x * 2 + core) * 4 + y) * 4 + z, ((a * 2 + b) * 4 + c % 4) * 4 + d % 4))
    return lax.ppermute(value, AXES, pairs)


def deal(x, core, yh, xi, core_from, yh_from):
    top = core_from == 0
    half_here, half_there = (x[:512], x[512:]) if top else (x[512:], x[:512])
    got = move(half_there, lambda a, b, c, d: (0, 1 - b, c, d) if a == 0 and b == core_from else None)
    half = jnp.where(core == core_from, half_here, got)
    here, there = (half[:256], half[256:]) if yh_from == 0 else (half[256:], half[:256])
    got = move(there, lambda a, b, c, d: (0, b, 3 - c, d) if a == 0 and c // 2 == yh_from else None)
    quarter = jnp.where(yh == yh_from, here, got)
    one = move(quarter, lambda a, b, c, d: (1 if b == 0 else 3, b, c, d) if a == 0 else None)
    two = move(quarter, lambda a, b, c, d: (3 if b == 0 else 1, b, c, d) if a == 0 else None)
    far = move(one, lambda a, b, c, d: (2, b, c, d) if a == (1 if b == 0 else 3) else None)
    return jnp.where(xi == 0, quarter, one + two + far)


def ring(value, first):
    def along(step):
        def where(a, b, c, d):
            on_z = (b == 0) == first
            return (a, b, c, d + step) if on_z else (a, b, c + step, d)

        return where

    before = move(value, along(1))
    after = move(value, along(-1))
    cut = value.shape[0] // 2
    far_low = move(before[:cut], along(1))
    far_high = move(after[cut:], along(-1))
    return after, far_low, far_high, before


def holds(a, b, c):
    return (a, b, c // 2) in ((0, 0, 0), (0, 1, 1), (1, 0, 0))


def gather_slices(lead, xi):
    def flip(c):
        return c + 1 - 2 * (c % 2)

    def across(a, b, c, d):
        return (1 if b == 1 and c < 2 else 0, 0 if c < 2 else 1, flip(c), d) if a == 0 and (b == 1 or c < 2) else None

    def along(step):
        return lambda a, b, c, d: (a, b, c, d + step) if holds(a, b, c) else None

    hop = move(lead, lambda a, b, c, d: (1, 0, c, d) if (a, b) == (0, 1) and c < 2 else None)
    pair = move(lead, across)
    own = jnp.where(xi == 1, hop, lead)
    pieces, places = [], []
    for other, value in ((False, own), (True, pair)):
        before, after = move(value, along(1)), move(value, along(-1))
        far_low, far_high = move(before[:512], along(1)), move(after[512:], along(-1))
        pieces += [value, after, before, far_low, far_high]
        places += [(other, 0, 0), (other, 1, 0), (other, 3, 0), (other, 2, 0), (other, 2, 512)]
    return pieces, places


def shards(factor, cross_cov):
    xi, core = lax.axis_index("x"), lax.axis_index("core")
    yh, yl, z = lax.axis_index("yh"), lax.axis_index("yl"), lax.axis_index("z")
    row_id = 2 * xi + core
    col_id = 8 * yh + 4 * yl + z
    slice_id = 4 * yl + z
    local = factor[:, 0]
    rhs = cross_cov[:, 0]

    diagonal = ((row_id == 0) & (yh == 0)) | ((row_id == 1) & (yh == 1))
    info = jnp.stack([diagonal.astype(jnp.int32), slice_id.astype(jnp.int32)])
    lead = invert_diagonal(info, local[0])
    pieces, places = gather_slices(lead, xi)

    own_rhs = rhs[0].reshape(64, 8, TILE).transpose(1, 0, 2)
    columns = lax.all_to_all(jnp.concatenate([own_rhs, own_rhs], 0), COL, 0, 0, tiled=True).reshape(1024, TILE)

    place = jnp.stack([yl, z]).astype(jnp.int32)
    tri, first = pack_and_solve(place, pieces, places, columns)
    columns, first = lax.optimization_barrier((columns, first))
    sent = move(first, lambda a, b, c, d: (1, 0, c, d) if a == 0 and b == 0 and c < 2 else None)
    columns = move(columns, lambda a, b, c, d: (1, 0, c, d) if (a, b) == (0, 1) and c < 2 else None)
    rest = residual(tri, columns, sent)
    second_rhs = move(rest, lambda a, b, c, d: (0, 1, 3 - c, d) if (a, b) == (1, 0) and c < 2 else None)

    by_rows = local.reshape(4, 16, 64, TILE).transpose(1, 0, 2, 3).reshape(16, 256, TILE)
    by_rows, sent = lax.optimization_barrier((by_rows, sent))
    left = lax.all_to_all(by_rows, COL, 0, 0, tiled=True)
    dealt0 = deal(first, core, yh, xi, 0, 0)
    second_rhs, dealt0 = lax.optimization_barrier((second_rhs, dealt0))
    second = solve(tri, second_rhs)
    dealt1 = deal(second, core, yh, xi, 1, 1)
    dealt1, left = lax.optimization_barrier((dealt1, left))

    def swap(value):
        return move(value, lambda a, b, c, d: (a, 1 - b, c, d))

    left = left.reshape(2, 2, 4, 256, TILE)
    kept = jnp.where(core == 0, left[:, 0], left[:, 1]).reshape(8, 256, TILE)
    given = jnp.where(core == 0, left[:, 1], left[:, 0]).reshape(8, 256, TILE)
    info2 = jnp.stack([xi, core, 2 * yh + yl, z, col_id]).astype(jnp.int32)

    mine = jnp.stack([dealt0, dealt1])
    after, far_low, far_high, before = ring(mine, True)
    near = jnp.stack([mine, after, jnp.concatenate([far_low, far_high], 0), before])

    def along(step):
        return lambda a, b, c, d: (a, b, c + step, d) if b == 0 else (a, b, c, d + step)

    before, after = move(near, along(1)), move(near, along(-1))
    high, low = prepare(info2[:1], kept, swap(given))
    sums = accumulate(info2, None, high, low, [near], [(0, 0)], "update_near")
    before, after, sums = lax.optimization_barrier((before, after, sums))
    far_low, far_high = move(before[:2], along(1)), move(after[2:], along(-1))
    sums = accumulate(info2, sums, high, low, [after, before], [(1, 0), (3, 0)], "update_next")
    far_low, far_high, sums = lax.optimization_barrier((far_low, far_high, sums))
    sums = accumulate(info2, sums, high, low, [far_low, far_high], [(2, 0), (2, 2)], "update_far")

    replaced = (xi == 0) & (lax.broadcasted_iota(jnp.int32, (256, 1024), 0) < 64)
    base = jnp.where(replaced, 0.0, rhs.reshape(256, 1024))
    out = base - (sums[:256] + swap(sums[256:]))
    return out.reshape(4, 1, 64, 1024)


def solution(mesh):
    fine = Mesh(mesh.devices.reshape(4, 2, 2, 2, 4), ROW + COL)
    return jax.shard_map(
        shards,
        mesh=fine,
        in_specs=(P(None, ROW, None, COL), P(None, ROW, COL, None)),
        out_specs=P(None, ROW, COL, None),
        check_vma=False,
    )
```

```python
import jax
import jax.numpy as jnp
import numpy as np
from jax import lax
from jax.experimental import pallas as pl
from jax.experimental.pallas import tpu as pltpu
from jax.sharding import Mesh, PartitionSpec as P

ROW = ("x", "core")
COL = ("yh", "yl", "z")
F32 = jnp.float32
BF16 = jnp.bfloat16
TILE = 128
PARAMS = pltpu.CompilerParams(vmem_limit_bytes=20 * 2**20)
VM = pl.BlockSpec(memory_space=pltpu.VMEM)
SM = pl.BlockSpec(memory_space=pltpu.SMEM)


def split(value):
    high = value.astype(BF16)
    return high, (value - high.astype(F32)).astype(BF16)


def mm(a, b):
    return jnp.dot(a, b, preferred_element_type=F32)


def pack_left(value):
    return jnp.concatenate(split(value), 1)


def pack_right(value):
    high, low = split(value)
    return jnp.concatenate(
        [jnp.concatenate([high, low], 1), jnp.concatenate([high, jnp.zeros_like(low)], 1)], 0
    )


def packed_product(left, right):
    out = mm(left, right)
    return out[:, :TILE] + out[:, TILE:]


def invert_body(info, lead_ref, out_ref):
    out_ref[...] = lead_ref[...]

    @pl.when(info[0] == 1)
    def _():
        start = pl.multiple_of(info[1] * TILE, TILE)
        block = lead_ref[pl.ds(start, TILE), :]
        i = lax.broadcasted_iota(jnp.int32, (TILE, TILE), 0)
        j = lax.broadcasted_iota(jnp.int32, (TILE, TILE), 1)
        zero = jnp.zeros((TILE, TILE), F32)
        inverse = jnp.where(i == j, 1.0 / jnp.where(i == j, block, 1.0), zero)
        step = 1
        while step < TILE:
            below = ((i // (2 * step)) == (j // (2 * step))) & ((i // step) > (j // step))
            corner = jnp.where(below, block, zero)
            product = packed_product(pack_left(corner), pack_right(inverse))
            inverse = inverse - packed_product(pack_left(inverse), pack_right(product))
            step *= 2
        out_ref[pl.ds(start, TILE), :] = inverse


def invert_diagonal(info, lead):
    return pl.pallas_call(
        invert_body,
        out_shape=jax.ShapeDtypeStruct(lead.shape, F32),
        in_specs=[SM, VM],
        out_specs=VM,
        compiler_params=PARAMS,
        name="invert_diagonal",
    )(info, lead)


def solve_body(tri_ref, rhs_ref, out_ref):
    count = tri_ref.shape[0]
    out_ref[...] = rhs_ref[...]
    for k in range(count):
        here = pl.ds(k * TILE, TILE)
        solved = packed_product(pack_left(tri_ref[k, here, :]), pack_right(out_ref[here, :]))
        out_ref[here, :] = solved
        right = pack_right(solved)
        for i in range(k + 1, count):
            there = pl.ds(i * TILE, TILE)
            out_ref[there, :] = out_ref[there, :] - packed_product(pack_left(tri_ref[k, there, :]), right)


def solve(tri, rhs):
    return pl.pallas_call(
        solve_body,
        out_shape=jax.ShapeDtypeStruct(rhs.shape, F32),
        in_specs=[VM, VM],
        out_specs=VM,
        compiler_params=PARAMS,
        name="block_solve",
    )(tri, rhs)


def residual_body(tri_ref, rhs_ref, x_ref, out_ref):
    count = tri_ref.shape[0]
    for k in range(count):
        right = pack_right(x_ref[pl.ds(k * TILE, TILE), :])
        for i in range(count):
            there = pl.ds(i * TILE, TILE)
            base = rhs_ref[there, :] if k == 0 else out_ref[there, :]
            out_ref[there, :] = base - packed_product(pack_left(tri_ref[k, there, :]), right)


def residual(tri, rhs, x):
    return pl.pallas_call(
        residual_body,
        out_shape=jax.ShapeDtypeStruct(rhs.shape, F32),
        in_specs=[VM, VM, VM],
        out_specs=VM,
        compiler_params=PARAMS,
        name="block_residual",
    )(tri, rhs, x)


def prepare_body(info, mine_ref, other_ref, high_ref, low_ref):
    for side, ref in enumerate((mine_ref, other_ref)):
        rows = pl.ds(256 * side, 256)
        for n in range(4):
            high, low = split(jnp.concatenate([ref[2 * n], ref[2 * n + 1]], 1))
            high_ref[n, rows, :] = high
            low_ref[n, rows, :] = low

    @pl.when(info[0] == 0)
    def _():
        for n in range(4):
            for side in range(2):
                high_ref[n, pl.ds(256 * side, 64), :] = jnp.zeros((64, 256), BF16)
                low_ref[n, pl.ds(256 * side, 64), :] = jnp.zeros((64, 256), BF16)


def prepare(info, mine, other):
    return pl.pallas_call(
        prepare_body,
        out_shape=[jax.ShapeDtypeStruct((4, 512, 256), BF16)] * 2,
        in_specs=[SM, VM, VM],
        out_specs=[VM, VM],
        compiler_params=PARAMS,
        name="prepare_update",
    )(info, mine, other)


def accumulate(info, sums, high, low, pieces, places, name):
    first = sums is None

    def body(info, high_ref, low_ref, *refs):
        out_ref = refs[-1]
        x, core, y, z, col = (info[k] for k in range(5))
        if first:
            out_ref[...] = jnp.zeros(out_ref.shape, F32)
        else:
            out_ref[...] = refs[0][...]
        for ref, (far, slot) in zip(refs[0 if first else 1 :], places):
            for n in range(ref.shape[0]):
                near = slot + n
                py = lax.rem(y + jnp.where(core == 0, far, near), 4)
                pz = lax.rem(z + jnp.where(core == 0, near, far), 4)
                upper = py // 2
                bit = jnp.where(upper == 0, py, 3 - py)
                cols = pl.ds(pl.multiple_of((4 * bit + pz) * TILE, TILE), TILE)
                total = None
                for h in range(2):
                    x_high, x_low = split(ref[n, h])
                    wide = mm(high_ref[2 * h + upper], jnp.concatenate([x_high, x_low], 1))
                    term = wide[:, :TILE] + (wide[:, TILE:] + mm(low_ref[2 * h + upper], x_high))
                    total = term if total is None else total + term
                out_ref[:, cols] = out_ref[:, cols] + total

                @pl.when((x == 0) & (col // 4 == 2 * core + upper))
                def _():
                    there = pl.ds(pl.multiple_of(lax.rem(col, 4) * 64, 64), 64)
                    for side in range(2):
                        here = pl.ds(256 * side, 64)
                        block = core if side == 0 else 1 - core
                        out_ref[here, cols] = out_ref[here, cols] - ref[n, block, there, :]

    start = [] if first else [sums]
    return pl.pallas_call(
        body,
        out_shape=jax.ShapeDtypeStruct((512, 1024), F32),
        in_specs=[SM] + [VM] * (2 + len(start) + len(pieces)),
        out_specs=VM,
        input_output_aliases={} if first else {3: 0},
        compiler_params=PARAMS,
        name=name,
    )(info, high, low, *start, *pieces)


AXES = ROW + COL


def move(value, where):
    pairs = []
    for x in range(4):
        for core in range(2):
            for y in range(4):
                for z in range(4):
                    to = where(x, core, y, z)
                    if to is not None:
                        a, b, c, d = to
                        pairs.append((((x * 2 + core) * 4 + y) * 4 + z, ((a * 2 + b) * 4 + c % 4) * 4 + d % 4))
    return lax.ppermute(value, AXES, pairs)


def deal(x, core, yh, xi, core_from, yh_from):
    top = core_from == 0
    half_here, half_there = (x[:512], x[512:]) if top else (x[512:], x[:512])
    got = move(half_there, lambda a, b, c, d: (0, 1 - b, c, d) if a == 0 and b == core_from else None)
    half = jnp.where(core == core_from, half_here, got)
    here, there = (half[:256], half[256:]) if yh_from == 0 else (half[256:], half[:256])
    got = move(there, lambda a, b, c, d: (0, b, 3 - c, d) if a == 0 and c // 2 == yh_from else None)
    quarter = jnp.where(yh == yh_from, here, got)
    one = move(quarter, lambda a, b, c, d: (1 if b == 0 else 3, b, c, d) if a == 0 else None)
    two = move(quarter, lambda a, b, c, d: (3 if b == 0 else 1, b, c, d) if a == 0 else None)
    far = move(one, lambda a, b, c, d: (2, b, c, d) if a == (1 if b == 0 else 3) else None)
    return jnp.where(xi == 0, quarter, one + two + far)


def ring(value, first):
    def along(step):
        def where(a, b, c, d):
            on_z = (b == 0) == first
            return (a, b, c, d + step) if on_z else (a, b, c + step, d)

        return where

    before = move(value, along(1))
    after = move(value, along(-1))
    cut = value.shape[0] // 2
    far_low = move(before[:cut], along(1))
    far_high = move(after[cut:], along(-1))
    return after, far_low, far_high, before


def shards(factor, cross_cov):
    xi, core = lax.axis_index("x"), lax.axis_index("core")
    yh, yl, z = lax.axis_index("yh"), lax.axis_index("yl"), lax.axis_index("z")
    row_id = 2 * xi + core
    col_id = 8 * yh + 4 * yl + z
    slice_id = 4 * yl + z
    local = factor[:, 0]
    rhs = cross_cov[:, 0]

    diagonal = ((row_id == 0) & (yh == 0)) | ((row_id == 1) & (yh == 1))
    info = jnp.stack([diagonal.astype(jnp.int32), slice_id.astype(jnp.int32)])
    lead = invert_diagonal(info, local[0])
    tri = lax.all_gather(lead, ("yl", "z"), axis=0, tiled=False)

    own_rhs = rhs[0].reshape(64, 8, TILE).transpose(1, 0, 2)
    columns = lax.all_to_all(jnp.concatenate([own_rhs, own_rhs], 0), COL, 0, 0, tiled=True).reshape(1024, TILE)
    by_rows = local.reshape(4, 16, 64, TILE).transpose(1, 0, 2, 3).reshape(16, 256, TILE)
    by_rows, columns = lax.optimization_barrier((by_rows, columns))
    left = lax.all_to_all(by_rows, COL, 0, 0, tiled=True)

    first = solve(tri, columns)
    sent = move(first, lambda a, b, c, d: (0, 1, c, d) if a == 0 and b == 0 and c < 2 else None)
    rest = residual(tri, columns, sent)
    second_rhs = move(rest, lambda a, b, c, d: (0, 1, 3 - c, d) if (a, b) == (0, 1) and c < 2 else None)
    first, left, rest = lax.optimization_barrier((first, left, rest))
    dealt0 = deal(first, core, yh, xi, 0, 0)
    second_rhs, dealt0 = lax.optimization_barrier((second_rhs, dealt0))
    second = solve(tri, second_rhs)
    dealt1 = deal(second, core, yh, xi, 1, 1)

    def swap(value):
        return move(value, lambda a, b, c, d: (a, 1 - b, c, d))

    left = left.reshape(2, 2, 4, 256, TILE)
    kept = jnp.where(core == 0, left[:, 0], left[:, 1]).reshape(8, 256, TILE)
    given = jnp.where(core == 0, left[:, 1], left[:, 0]).reshape(8, 256, TILE)
    info2 = jnp.stack([xi, core, 2 * yh + yl, z, col_id]).astype(jnp.int32)

    mine = jnp.stack([dealt0, dealt1])
    after, far_low, far_high, before = ring(mine, True)
    near = jnp.stack([mine, after, jnp.concatenate([far_low, far_high], 0), before])

    def along(step):
        return lambda a, b, c, d: (a, b, c + step, d) if b == 0 else (a, b, c, d + step)

    before, after = move(near, along(1)), move(near, along(-1))
    high, low = prepare(info2[:1], kept, swap(given))
    sums = accumulate(info2, None, high, low, [near], [(0, 0)], "update_near")
    before, after, sums = lax.optimization_barrier((before, after, sums))
    far_low, far_high = move(before[:2], along(1)), move(after[2:], along(-1))
    sums = accumulate(info2, sums, high, low, [after, before], [(1, 0), (3, 0)], "update_next")
    far_low, far_high, sums = lax.optimization_barrier((far_low, far_high, sums))
    sums = accumulate(info2, sums, high, low, [far_low, far_high], [(2, 0), (2, 2)], "update_far")

    replaced = (xi == 0) & (lax.broadcasted_iota(jnp.int32, (256, 1024), 0) < 64)
    base = jnp.where(replaced, 0.0, rhs.reshape(256, 1024))
    out = base - (sums[:256] + swap(sums[256:]))
    return out.reshape(4, 1, 64, 1024)


def solution(mesh):
    fine = Mesh(mesh.devices.reshape(4, 2, 2, 2, 4), ROW + COL)
    return jax.shard_map(
        shards,
        mesh=fine,
        in_specs=(P(None, ROW, None, COL), P(None, ROW, COL, None)),
        out_specs=P(None, ROW, COL, None),
        check_vma=False,
    )
```

```python
import jax
import jax.numpy as jnp
import numpy as np
from jax import lax
from jax.experimental import pallas as pl
from jax.experimental.pallas import tpu as pltpu
from jax.sharding import Mesh, PartitionSpec as P

ROW = ("x", "core")
COL = ("yh", "yl", "z")
F32 = jnp.float32
BF16 = jnp.bfloat16
TILE = 128
PARAMS = pltpu.CompilerParams(vmem_limit_bytes=20 * 2**20)
VM = pl.BlockSpec(memory_space=pltpu.VMEM)
SM = pl.BlockSpec(memory_space=pltpu.SMEM)


def split(value):
    high = value.astype(BF16)
    return high, (value - high.astype(F32)).astype(BF16)


def mm(a, b):
    return jnp.dot(a, b, preferred_element_type=F32)


def pack_left(value):
    return jnp.concatenate(split(value), 1)


def pack_right(value):
    high, low = split(value)
    return jnp.concatenate(
        [jnp.concatenate([high, low], 1), jnp.concatenate([high, jnp.zeros_like(low)], 1)], 0
    )


def packed_product(left, right):
    out = mm(left, right)
    return out[:, :TILE] + out[:, TILE:]


def invert_body(info, lead_ref, out_ref):
    out_ref[...] = lead_ref[...]

    @pl.when(info[0] == 1)
    def _():
        start = pl.multiple_of(info[1] * TILE, TILE)
        block = lead_ref[pl.ds(start, TILE), :]
        i = lax.broadcasted_iota(jnp.int32, (TILE, TILE), 0)
        j = lax.broadcasted_iota(jnp.int32, (TILE, TILE), 1)
        zero = jnp.zeros((TILE, TILE), F32)
        inverse = jnp.where(i == j, 1.0 / jnp.where(i == j, block, 1.0), zero)
        step = 1
        while step < TILE:
            below = ((i // (2 * step)) == (j // (2 * step))) & ((i // step) > (j // step))
            corner = jnp.where(below, block, zero)
            product = packed_product(pack_left(corner), pack_right(inverse))
            inverse = inverse - packed_product(pack_left(inverse), pack_right(product))
            step *= 2
        out_ref[pl.ds(start, TILE), :] = inverse


def invert_diagonal(info, lead):
    return pl.pallas_call(
        invert_body,
        out_shape=jax.ShapeDtypeStruct(lead.shape, F32),
        in_specs=[SM, VM],
        out_specs=VM,
        compiler_params=PARAMS,
        name="invert_diagonal",
    )(info, lead)


def solve(info, pieces, places, rhs):
    def body(info, *refs):
        rhs_ref, out_ref, tri_ref = refs[-3:]
        for ref, parts in zip(refs, places):
            for half, steps, start, to, rows in parts:
                k = 4 * half + lax.rem(info[1] + steps, 4)
                tri_ref[k, pl.ds(to, rows), :] = pack_left(ref[pl.ds(start, rows), :])
        out_ref[...] = rhs_ref[...]
        for k in range(8):
            here = pl.ds(k * TILE, TILE)
            solved = packed_product(tri_ref[k, here, :], pack_right(out_ref[here, :]))
            out_ref[here, :] = solved
            right = pack_right(solved)
            for i in range(k + 1, 8):
                there = pl.ds(i * TILE, TILE)
                out_ref[there, :] = out_ref[there, :] - packed_product(tri_ref[k, there, :], right)

    return pl.pallas_call(
        body,
        out_shape=jax.ShapeDtypeStruct(rhs.shape, F32),
        in_specs=[SM] + [VM] * (len(pieces) + 1),
        out_specs=VM,
        scratch_shapes=[pltpu.VMEM((8, 1024, 256), BF16)],
        compiler_params=PARAMS,
        name="block_solve",
    )(info, *pieces, rhs)


def residual(info, pieces, places, rhs, x):
    def body(info, *refs):
        rhs_ref, x_ref, out_ref = refs[-3:]
        out_ref[...] = rhs_ref[...]
        for ref, (other, steps, row) in zip(refs, places):
            half = 1 - info[0] if other else info[0]
            k = 4 * half + lax.rem(info[1] + steps, 4)
            right = pack_right(x_ref[pl.ds(pl.multiple_of(k * TILE, TILE), TILE), :])
            for start in range(0, ref.shape[0], TILE):
                there = pl.ds(row + start, TILE)
                out_ref[there, :] = out_ref[there, :] - packed_product(pack_left(ref[pl.ds(start, TILE), :]), right)

    return pl.pallas_call(
        body,
        out_shape=jax.ShapeDtypeStruct(rhs.shape, F32),
        in_specs=[SM] + [VM] * (len(pieces) + 2),
        out_specs=VM,
        compiler_params=PARAMS,
        name="block_residual",
    )(info, *pieces, rhs, x)


def arrange_body(factor_ref, out_ref):
    for c in range(16):
        for a in range(4):
            out_ref[c, pl.ds(64 * a, 64), :] = factor_ref[a, pl.ds(64 * c, 64), :]


def arrange(factor):
    return pl.pallas_call(
        arrange_body,
        out_shape=jax.ShapeDtypeStruct((16, 256, TILE), F32),
        in_specs=[VM],
        out_specs=VM,
        compiler_params=PARAMS,
        name="arrange_rows",
    )(factor)


def prepare_body(info, mine_ref, other_ref, high_ref, low_ref):
    for side, ref in enumerate((mine_ref, other_ref)):
        rows = pl.ds(256 * side, 256)
        for n in range(4):
            high, low = split(jnp.concatenate([ref[2 * n], ref[2 * n + 1]], 1))
            high_ref[n, rows, :] = high
            low_ref[n, rows, :] = low

    @pl.when(info[0] == 0)
    def _():
        for n in range(4):
            for side in range(2):
                high_ref[n, pl.ds(256 * side, 64), :] = jnp.zeros((64, 256), BF16)
                low_ref[n, pl.ds(256 * side, 64), :] = jnp.zeros((64, 256), BF16)


def prepare(info, mine, other):
    return pl.pallas_call(
        prepare_body,
        out_shape=[jax.ShapeDtypeStruct((4, 512, 256), BF16)] * 2,
        in_specs=[SM, VM, VM],
        out_specs=[VM, VM],
        compiler_params=PARAMS,
        name="prepare_update",
    )(info, mine, other)


def accumulate(info, sums, high, low, pieces, places, name):
    first = sums is None

    def body(info, high_ref, low_ref, *refs):
        out_ref = refs[-1]
        x, core, y, z, col = (info[k] for k in range(5))
        if first:
            out_ref[...] = jnp.zeros(out_ref.shape, F32)
        else:
            out_ref[...] = refs[0][...]
        for ref, (far, slot) in zip(refs[0 if first else 1 :], places):
            for n in range(ref.shape[0]):
                near = slot + n
                py = lax.rem(y + jnp.where(core == 0, far, near), 4)
                pz = lax.rem(z + jnp.where(core == 0, near, far), 4)
                upper = py // 2
                bit = jnp.where(upper == 0, py, 3 - py)
                cols = pl.ds(pl.multiple_of((4 * bit + pz) * TILE, TILE), TILE)
                total = None
                for h in range(2):
                    x_high, x_low = split(ref[n, h])
                    wide = mm(high_ref[2 * h + upper], jnp.concatenate([x_high, x_low], 1))
                    term = wide[:, :TILE] + (wide[:, TILE:] + mm(low_ref[2 * h + upper], x_high))
                    total = term if total is None else total + term
                out_ref[:, cols] = out_ref[:, cols] + total

                @pl.when((x == 0) & (col // 4 == 2 * core + upper))
                def _():
                    there = pl.ds(pl.multiple_of(lax.rem(col, 4) * 64, 64), 64)
                    for side in range(2):
                        here = pl.ds(256 * side, 64)
                        block = core if side == 0 else 1 - core
                        out_ref[here, cols] = out_ref[here, cols] - ref[n, block, there, :]

    start = [] if first else [sums]
    return pl.pallas_call(
        body,
        out_shape=jax.ShapeDtypeStruct((512, 1024), F32),
        in_specs=[SM] + [VM] * (2 + len(start) + len(pieces)),
        out_specs=VM,
        input_output_aliases={} if first else {3: 0},
        compiler_params=PARAMS,
        name=name,
    )(info, high, low, *start, *pieces)


AXES = ROW + COL


def move(value, where):
    pairs = []
    for x in range(4):
        for core in range(2):
            for y in range(4):
                for z in range(4):
                    to = where(x, core, y, z)
                    if to is not None:
                        a, b, c, d = to
                        pairs.append((((x * 2 + core) * 4 + y) * 4 + z, ((a * 2 + b) * 4 + c % 4) * 4 + d % 4))
    return lax.ppermute(value, AXES, pairs)


def deal(first, second, core, yh, xi):
    lower = yh == 0
    here = jnp.where(lower, first[:512], second[512:])
    there = jnp.where(lower, first[512:], second[:512])
    got = move(there, lambda a, b, c, d: (0, 1 - b, c, d) if a == 0 and b == c // 2 else None)
    half = jnp.where(core == yh, here, got)
    here = jnp.where(lower, half[:256], half[256:])
    there = jnp.where(lower, half[256:], half[:256])
    got = move(there, lambda a, b, c, d: (0, b, 3 - c, d) if a == 0 else None)
    both = jnp.stack([jnp.where(lower, here, got), jnp.where(lower, got, here)])
    one = move(both, lambda a, b, c, d: (1 if b == 0 else 3, b, c, d) if a == 0 else None)
    two = move(both, lambda a, b, c, d: (3 if b == 0 else 1, b, c, d) if a == 0 else None)
    far = move(one, lambda a, b, c, d: (2, b, c, d) if a == (1 if b == 0 else 3) else None)
    return jnp.where(xi == 0, both, one + two + far)


def ring(value, first):
    def along(step):
        def where(a, b, c, d):
            on_z = (b == 0) == first
            return (a, b, c, d + step) if on_z else (a, b, c + step, d)

        return where

    before = move(value, along(1))
    after = move(value, along(-1))
    cut = value.shape[0] // 2
    far_low = move(before[:cut], along(1))
    far_high = move(after[cut:], along(-1))
    return after, far_low, far_high, before


def gather_triangles(lead, yl):
    def holds(a, b, c):
        return a == 0 and b == c // 2

    swapped = move(lead, lambda a, b, c, d: (a, b, c + 1 - 2 * (c % 2), d) if holds(a, b, c) else None)
    full = jnp.where(yl == 0, lead, swapped)
    lower = jnp.where(yl == 0, swapped[512:], lead[512:])
    pair = jnp.concatenate([full, lower], 0)

    def along(step):
        return lambda a, b, c, d: (a, b, c, d + step) if holds(a, b, c) else None

    before, after = move(pair, along(1)), move(pair, along(-1))
    far_low, far_high = move(before[:768], along(1)), move(after[768:], along(-1))
    pieces, places = [], []
    for piece, steps in ((pair, 0), (after, 1), (before, 3)):
        pieces.append(piece)
        places.append([(0, steps, 0, 0, 1024), (1, steps, 1024, 512, 512)])
    pieces += [far_low, far_high]
    places += [[(0, 2, 0, 0, 768)], [(0, 2, 0, 768, 256), (1, 2, 256, 512, 512)]]
    return pieces, places


def gather_square(lead):
    def holds(a, b, c):
        return a == 0 and b == 0 and c >= 2

    def along(step):
        return lambda a, b, c, d: (a, b, c, d + step) if holds(a, b, c) else None

    def pair(value):
        return move(value, lambda a, b, c, d: (a, b, 5 - c, d) if holds(a, b, c) else None)

    own = move(lead, lambda a, b, c, d: (0, 0, 3 - c, d) if (a, b) == (0, 1) and c < 2 else None)
    before, after = move(own, along(1)), move(own, along(-1))
    far_low, far_high = move(before[:512], along(1)), move(after[512:], along(-1))
    pieces, places = [], []
    for piece, steps, row in ((own, 0, 0), (after, 1, 0), (before, 3, 0), (far_low, 2, 0), (far_high, 2, 512)):
        pieces += [piece, pair(piece)]
        places += [(False, steps, row), (True, steps, row)]
    return pieces, places


def shards(factor, cross_cov):
    xi, core = lax.axis_index("x"), lax.axis_index("core")
    yh, yl, z = lax.axis_index("yh"), lax.axis_index("yl"), lax.axis_index("z")
    row_id = 2 * xi + core
    col_id = 8 * yh + 4 * yl + z
    local = factor[:, 0]
    rhs = cross_cov[:, 0]

    diagonal = ((row_id == 0) & (yh == 0)) | ((row_id == 1) & (yh == 1))
    info = jnp.stack([diagonal.astype(jnp.int32), (4 * yl + z).astype(jnp.int32)])
    lead = invert_diagonal(info, local[0])

    own_rhs = rhs[0].reshape(64, 2, 4, TILE).transpose(1, 2, 0, 3)
    own_rhs = jnp.stack([own_rhs, own_rhs[::-1]]).reshape(16, 64, TILE)
    columns = lax.all_to_all(own_rhs, COL, 0, 0, tiled=True).reshape(1024, TILE)

    place = jnp.stack([1 - yl, z]).astype(jnp.int32)
    triangle = gather_triangles(lead, yl)
    square = gather_square(lead)
    first = solve(place, *triangle, columns)
    sent = move(first, lambda a, b, c, d: (0, 0, 3 - c, d) if (a, b) == (0, 0) and c < 2 else None)
    columns = move(columns, lambda a, b, c, d: (0, 0, c, d) if (a, b) == (0, 1) and c >= 2 else None)
    rest = residual(place, *square, columns, sent)
    second_rhs = move(rest, lambda a, b, c, d: (0, 1, c, d) if (a, b) == (0, 0) and c >= 2 else None)

    by_rows, sent = lax.optimization_barrier((arrange(local), sent))
    left = lax.all_to_all(by_rows, COL, 0, 0, tiled=True)
    second = solve(place, *triangle, second_rhs)
    mine = deal(first, second, core, yh, xi)
    mine, left = lax.optimization_barrier((mine, left))

    def swap(value):
        return move(value, lambda a, b, c, d: (a, 1 - b, c, d))

    left = left.reshape(2, 2, 4, 256, TILE)
    kept = jnp.where(core == 0, left[:, 0], left[:, 1]).reshape(8, 256, TILE)
    given = jnp.where(core == 0, left[:, 1], left[:, 0]).reshape(8, 256, TILE)
    info2 = jnp.stack([xi, core, 2 * yh + yl, z, col_id]).astype(jnp.int32)

    after, far_low, far_high, before = ring(mine, True)
    near = jnp.stack([mine, after, jnp.concatenate([far_low, far_high], 0), before])

    def along(step):
        return lambda a, b, c, d: (a, b, c + step, d) if b == 0 else (a, b, c, d + step)

    before, after = move(near, along(1)), move(near, along(-1))
    high, low = prepare(info2[:1], kept, swap(given))
    sums = accumulate(info2, None, high, low, [near], [(0, 0)], "update_near")
    before, after, sums = lax.optimization_barrier((before, after, sums))
    far_low, far_high = move(before[:2], along(1)), move(after[2:], along(-1))
    sums = accumulate(info2, sums, high, low, [after, before], [(1, 0), (3, 0)], "update_next")
    far_low, far_high, sums = lax.optimization_barrier((far_low, far_high, sums))
    sums = accumulate(info2, sums, high, low, [far_low, far_high], [(2, 0), (2, 2)], "update_far")

    replaced = (xi == 0) & (lax.broadcasted_iota(jnp.int32, (256, 1024), 0) < 64)
    base = jnp.where(replaced, 0.0, rhs.reshape(256, 1024))
    out = base - (sums[:256] + swap(sums[256:]))
    return out.reshape(4, 1, 64, 1024)


def solution(mesh):
    fine = Mesh(mesh.devices.reshape(4, 2, 2, 2, 4), ROW + COL)
    return jax.shard_map(
        shards,
        mesh=fine,
        in_specs=(P(None, ROW, None, COL), P(None, ROW, COL, None)),
        out_specs=P(None, ROW, COL, None),
        check_vma=False,
    )
```

```python
import jax
import jax.numpy as jnp
import numpy as np
from jax import lax
from jax.experimental import pallas as pl
from jax.experimental.pallas import tpu as pltpu
from jax.sharding import Mesh, PartitionSpec as P

ROW = ("x", "core")
COL = ("yh", "yl", "z")
F32 = jnp.float32
BF16 = jnp.bfloat16
TILE = 128
PARAMS = pltpu.CompilerParams(vmem_limit_bytes=20 * 2**20)
VM = pl.BlockSpec(memory_space=pltpu.VMEM)
SM = pl.BlockSpec(memory_space=pltpu.SMEM)


def split(value):
    high = value.astype(BF16)
    return high, (value - high.astype(F32)).astype(BF16)


def mm(a, b):
    return jnp.dot(a, b, preferred_element_type=F32)


def pack_left(value):
    return jnp.concatenate(split(value), 1)


def pack_right(value):
    high, low = split(value)
    return jnp.concatenate(
        [jnp.concatenate([high, low], 1), jnp.concatenate([high, jnp.zeros_like(low)], 1)], 0
    )


def packed_product(left, right):
    out = mm(left, right)
    return out[:, :TILE] + out[:, TILE:]


def invert_body(info, factor_ref, out_ref):
    lead_ref = factor_ref.at[0]
    out_ref[...] = lead_ref[...]

    @pl.when(info[0] == 1)
    def _():
        start = pl.multiple_of(info[1] * TILE, TILE)
        block = lead_ref[pl.ds(start, TILE), :]
        i = lax.broadcasted_iota(jnp.int32, (TILE, TILE), 0)
        j = lax.broadcasted_iota(jnp.int32, (TILE, TILE), 1)
        zero = jnp.zeros((TILE, TILE), F32)
        inverse = jnp.where(i == j, 1.0 / jnp.where(i == j, block, 1.0), zero)
        step = 1
        while step < TILE:
            below = ((i // (2 * step)) == (j // (2 * step))) & ((i // step) > (j // step))
            corner = jnp.where(below, block, zero)
            product = packed_product(pack_left(corner), pack_right(inverse))
            inverse = inverse - packed_product(pack_left(inverse), pack_right(product))
            step *= 2
        out_ref[pl.ds(start, TILE), :] = inverse


def invert_diagonal(info, factor):
    return pl.pallas_call(
        invert_body,
        grid=(1,),
        out_shape=jax.ShapeDtypeStruct(factor.shape[1:], F32),
        in_specs=[SM, pl.BlockSpec((1, 1024, TILE), lambda i: (0, 0, 0))],
        out_specs=pl.BlockSpec((1024, TILE), lambda i: (0, 0)),
        compiler_params=PARAMS,
        name="invert_diagonal",
    )(info, factor)


def solve(info, pieces, places, rhs):
    def body(info, *refs):
        rhs_ref, out_ref, tri_ref = refs[-3:]
        for ref, parts in zip(refs, places):
            for half, steps, start, to, rows in parts:
                k = 4 * half + lax.rem(info[1] + steps, 4)
                tri_ref[k, pl.ds(to, rows), :] = pack_left(ref[pl.ds(start, rows), :])
        out_ref[...] = rhs_ref[...]
        for k in range(8):
            here = pl.ds(k * TILE, TILE)
            solved = packed_product(tri_ref[k, here, :], pack_right(out_ref[here, :]))
            out_ref[here, :] = solved
            right = pack_right(solved)
            for i in range(k + 1, 8):
                there = pl.ds(i * TILE, TILE)
                out_ref[there, :] = out_ref[there, :] - packed_product(tri_ref[k, there, :], right)

    return pl.pallas_call(
        body,
        out_shape=jax.ShapeDtypeStruct(rhs.shape, F32),
        in_specs=[SM] + [VM] * (len(pieces) + 1),
        out_specs=VM,
        scratch_shapes=[pltpu.VMEM((8, 1024, 256), BF16)],
        compiler_params=PARAMS,
        name="block_solve",
    )(info, *pieces, rhs)


def residual(info, pieces, places, rhs, x):
    def body(info, *refs):
        rhs_ref, x_ref, out_ref = refs[-3:]
        out_ref[...] = rhs_ref[...]
        for ref, (other, steps, row) in zip(refs, places):
            half = 1 - info[0] if other else info[0]
            k = 4 * half + lax.rem(info[1] + steps, 4)
            right = pack_right(x_ref[pl.ds(pl.multiple_of(k * TILE, TILE), TILE), :])
            for start in range(0, ref.shape[0], TILE):
                there = pl.ds(row + start, TILE)
                out_ref[there, :] = out_ref[there, :] - packed_product(pack_left(ref[pl.ds(start, TILE), :]), right)

    return pl.pallas_call(
        body,
        out_shape=jax.ShapeDtypeStruct(rhs.shape, F32),
        in_specs=[SM] + [VM] * (len(pieces) + 2),
        out_specs=VM,
        compiler_params=PARAMS,
        name="block_residual",
    )(info, *pieces, rhs, x)


def arrange_body(factor_ref, first_ref, second_ref):
    for c in range(16):
        for a in range(2):
            rows = pl.ds(64 * a, 64)
            first_ref[c, rows, :] = factor_ref[a, pl.ds(64 * c, 64), :]
            second_ref[c, rows, :] = factor_ref[2 + a, pl.ds(64 * c, 64), :]


def arrange(factor):
    return pl.pallas_call(
        arrange_body,
        out_shape=[jax.ShapeDtypeStruct((16, 128, TILE), F32)] * 2,
        in_specs=[VM],
        out_specs=[VM, VM],
        compiler_params=PARAMS,
        name="arrange_rows",
    )(factor)


def arrange_rhs_body(rhs_ref, out_ref):
    for n in range(8):
        out_ref[n, :, :] = rhs_ref[0, :, pl.ds(n * TILE, TILE)]
        out_ref[8 + n, :, :] = rhs_ref[0, :, pl.ds((n + 4) % 8 * TILE, TILE)]


def arrange_rhs(rhs):
    return pl.pallas_call(
        arrange_rhs_body,
        grid=(1,),
        out_shape=jax.ShapeDtypeStruct((16, 64, TILE), F32),
        in_specs=[pl.BlockSpec((1, 64, 1024), lambda i: (0, 0, 0))],
        out_specs=pl.BlockSpec((16, 64, TILE), lambda i: (0, 0, 0)),
        compiler_params=PARAMS,
        name="arrange_rhs",
    )(rhs)


def prepare_body(info, *refs):
    high_ref, low_ref = refs[-2:]
    for place, ref in enumerate(refs[:4]):
        rows = pl.ds(128 * place, 128)
        for n in range(4):
            high, low = split(jnp.concatenate([ref[2 * n], ref[2 * n + 1]], 1))
            high_ref[n, rows, :] = high
            low_ref[n, rows, :] = low

    @pl.when(info[0] == 0)
    def _():
        for n in range(4):
            for side in range(2):
                high_ref[n, pl.ds(256 * side, 64), :] = jnp.zeros((64, 256), BF16)
                low_ref[n, pl.ds(256 * side, 64), :] = jnp.zeros((64, 256), BF16)


def prepare(info, *parts):
    return pl.pallas_call(
        prepare_body,
        out_shape=[jax.ShapeDtypeStruct((4, 512, 256), BF16)] * 2,
        in_specs=[SM, VM, VM, VM, VM],
        out_specs=[VM, VM],
        compiler_params=PARAMS,
        name="prepare_update",
    )(info, *parts)


def accumulate(info, sums, high, low, pieces, places, name):
    first = sums is None

    def body(info, high_ref, low_ref, *refs):
        out_ref = refs[-1]
        x, core, y, z, col = (info[k] for k in range(5))
        if first:
            out_ref[...] = jnp.zeros(out_ref.shape, F32)
        else:
            out_ref[...] = refs[0][...]
        for ref, (far, slot) in zip(refs[0 if first else 1 :], places):
            for n in range(ref.shape[0]):
                near = slot + n
                py = lax.rem(y + jnp.where(core == 0, far, near), 4)
                pz = lax.rem(z + jnp.where(core == 0, near, far), 4)
                upper = py // 2
                bit = jnp.where(upper == 0, py, 3 - py)
                cols = pl.ds(pl.multiple_of((4 * bit + pz) * TILE, TILE), TILE)
                total = None
                for h in range(2):
                    x_high, x_low = split(ref[n, h])
                    wide = mm(high_ref[2 * h + upper], jnp.concatenate([x_high, x_low], 1))
                    term = wide[:, :TILE] + (wide[:, TILE:] + mm(low_ref[2 * h + upper], x_high))
                    total = term if total is None else total + term
                out_ref[:, cols] = out_ref[:, cols] + total

                @pl.when((x == 0) & (col // 4 == 2 * core + upper))
                def _():
                    there = pl.ds(pl.multiple_of(lax.rem(col, 4) * 64, 64), 64)
                    for side in range(2):
                        here = pl.ds(256 * side, 64)
                        block = core if side == 0 else 1 - core
                        out_ref[here, cols] = out_ref[here, cols] - ref[n, block, there, :]

    start = [] if first else [sums]
    return pl.pallas_call(
        body,
        out_shape=jax.ShapeDtypeStruct((512, 1024), F32),
        in_specs=[SM] + [VM] * (2 + len(start) + len(pieces)),
        out_specs=VM,
        input_output_aliases={} if first else {3: 0},
        compiler_params=PARAMS,
        name=name,
    )(info, high, low, *start, *pieces)


AXES = ROW + COL


def move(value, where):
    pairs = []
    for x in range(4):
        for core in range(2):
            for y in range(4):
                for z in range(4):
                    to = where(x, core, y, z)
                    if to is not None:
                        a, b, c, d = to
                        pairs.append((((x * 2 + core) * 4 + y) * 4 + z, ((a * 2 + b) * 4 + c % 4) * 4 + d % 4))
    return lax.ppermute(value, AXES, pairs)


def deal(first, second, core, yh, xi, by_rows):
    lower = yh == 0
    here = jnp.where(lower, first[:512], second[512:])
    there = jnp.where(lower, first[512:], second[:512])
    got = move(there, lambda a, b, c, d: (0, 1 - b, c, d) if a == 0 and b == c // 2 else None)
    half = jnp.where(core == yh, here, got)
    here = jnp.where(lower, half[:256], half[256:])
    there = jnp.where(lower, half[256:], half[:256])
    got = move(there, lambda a, b, c, d: (0, b, 3 - c, d) if a == 0 else None)
    got, by_rows = lax.optimization_barrier((got, by_rows))
    left = lax.all_to_all(by_rows, COL, 0, 0, tiled=True)
    both = jnp.stack([jnp.where(lower, here, got), jnp.where(lower, got, here)])
    one = move(both, lambda a, b, c, d: (1 if b == 0 else 3, b, c, d) if a == 0 else None)
    two = move(both, lambda a, b, c, d: (3 if b == 0 else 1, b, c, d) if a == 0 else None)
    far = move(one, lambda a, b, c, d: (2, b, c, d) if a == (1 if b == 0 else 3) else None)
    return lax.optimization_barrier((jnp.where(xi == 0, both, one + two + far), left))


def ring(value, first):
    def along(step):
        def where(a, b, c, d):
            on_z = (b == 0) == first
            return (a, b, c, d + step) if on_z else (a, b, c + step, d)

        return where

    before = move(value, along(1))
    after = move(value, along(-1))
    cut = value.shape[0] // 2
    far_low = move(before[:cut], along(1))
    far_high = move(after[cut:], along(-1))
    return after, far_low, far_high, before


def gather_triangles(lead, yl):
    def holds(a, b, c):
        return a == 0 and b == c // 2

    swapped = move(lead, lambda a, b, c, d: (a, b, c + 1 - 2 * (c % 2), d) if holds(a, b, c) else None)
    full = jnp.where(yl == 0, lead, swapped)
    lower = jnp.where(yl == 0, swapped[512:], lead[512:])
    pair = jnp.concatenate([full, lower], 0)

    def along(step):
        return lambda a, b, c, d: (a, b, c, d + step) if holds(a, b, c) else None

    before, after = move(pair, along(1)), move(pair, along(-1))
    far_low, far_high = move(before[:768], along(1)), move(after[768:], along(-1))
    pieces, places = [], []
    for piece, steps in ((pair, 0), (after, 1), (before, 3)):
        pieces.append(piece)
        places.append([(0, steps, 0, 0, 1024), (1, steps, 1024, 512, 512)])
    pieces += [far_low, far_high]
    places += [[(0, 2, 0, 0, 768)], [(0, 2, 0, 768, 256), (1, 2, 256, 512, 512)]]
    return pieces, places


def gather_square(lead):
    def holds(a, b, c):
        return a == 0 and b == 0 and c >= 2

    def along(step):
        return lambda a, b, c, d: (a, b, c, d + step) if holds(a, b, c) else None

    def pair(value):
        return move(value, lambda a, b, c, d: (a, b, 5 - c, d) if holds(a, b, c) else None)

    own = move(lead, lambda a, b, c, d: (0, 0, 3 - c, d) if (a, b) == (0, 1) and c < 2 else None)
    before, after = move(own, along(1)), move(own, along(-1))
    far_low, far_high = move(before[:512], along(1)), move(after[512:], along(-1))
    pieces, places = [], []
    for piece, steps, row in ((own, 0, 0), (after, 1, 0), (before, 3, 0), (far_low, 2, 0), (far_high, 2, 512)):
        pieces += [piece, pair(piece)]
        places += [(False, steps, row), (True, steps, row)]
    return pieces, places


def shards(factor, cross_cov):
    xi, core = lax.axis_index("x"), lax.axis_index("core")
    yh, yl, z = lax.axis_index("yh"), lax.axis_index("yl"), lax.axis_index("z")
    row_id = 2 * xi + core
    col_id = 8 * yh + 4 * yl + z
    local = factor[:, 0]
    rhs = cross_cov[:, 0]

    diagonal = ((row_id == 0) & (yh == 0)) | ((row_id == 1) & (yh == 1))
    info = jnp.stack([diagonal.astype(jnp.int32), (4 * yl + z).astype(jnp.int32)])
    columns = lax.all_to_all(arrange_rhs(rhs), COL, 0, 0, tiled=True).reshape(1024, TILE)
    lead, columns = lax.optimization_barrier((invert_diagonal(info, local), columns))

    place = jnp.stack([1 - yl, z]).astype(jnp.int32)
    triangle = gather_triangles(lead, yl)
    square = gather_square(lead)
    early, late = arrange(local)
    first = solve(place, *triangle, columns)
    sent = move(first, lambda a, b, c, d: (0, 0, 3 - c, d) if (a, b) == (0, 0) and c < 2 else None)
    early, first = lax.optimization_barrier((early, first))
    left_early = lax.all_to_all(early, COL, 0, 0, tiled=True)
    columns = move(columns, lambda a, b, c, d: (0, 0, c, d) if (a, b) == (0, 1) and c >= 2 else None)
    rest = residual(place, *square, columns, sent)
    second_rhs = move(rest, lambda a, b, c, d: (0, 1, c, d) if (a, b) == (0, 0) and c >= 2 else None)
    second_rhs, left_early = lax.optimization_barrier((second_rhs, left_early))
    second = solve(place, *triangle, second_rhs)
    mine, left_late = deal(first, second, core, yh, xi, late)

    def swap(value):
        return move(value, lambda a, b, c, d: (a, 1 - b, c, d))

    kept, given = [], []
    for left in (left_early, left_late):
        left = left.reshape(2, 2, 4, 128, TILE)
        kept.append(jnp.where(core == 0, left[:, 0], left[:, 1]).reshape(8, 128, TILE))
        given.append(swap(jnp.where(core == 0, left[:, 1], left[:, 0]).reshape(8, 128, TILE)))
    info2 = jnp.stack([xi, core, 2 * yh + yl, z, col_id]).astype(jnp.int32)

    after, far_low, far_high, before = ring(mine, True)
    near = jnp.stack([mine, after, jnp.concatenate([far_low, far_high], 0), before])

    def along(step):
        return lambda a, b, c, d: (a, b, c + step, d) if b == 0 else (a, b, c, d + step)

    before, after = move(near, along(1)), move(near, along(-1))
    high, low = prepare(info2[:1], *kept, *given)
    sums = accumulate(info2, None, high, low, [near], [(0, 0)], "update_near")
    before, after, sums = lax.optimization_barrier((before, after, sums))
    far_low, far_high = move(before[:2], along(1)), move(after[2:], along(-1))
    sums = accumulate(info2, sums, high, low, [after, before], [(1, 0), (3, 0)], "update_next")
    far_low, far_high, sums = lax.optimization_barrier((far_low, far_high, sums))
    sums = accumulate(info2, sums, high, low, [far_low, far_high], [(2, 0), (2, 2)], "update_far")

    replaced = (xi == 0) & (lax.broadcasted_iota(jnp.int32, (256, 1024), 0) < 64)
    base = jnp.where(replaced, 0.0, rhs.reshape(256, 1024))
    out = base - (sums[:256] + swap(sums[256:]))
    return out.reshape(4, 1, 64, 1024)


def solution(mesh):
    fine = Mesh(mesh.devices.reshape(4, 2, 2, 2, 4), ROW + COL)
    return jax.shard_map(
        shards,
        mesh=fine,
        in_specs=(P(None, ROW, None, COL), P(None, ROW, COL, None)),
        out_specs=P(None, ROW, COL, None),
        check_vma=False,
    )
```

```python
import jax
import jax.numpy as jnp
from jax import lax
from jax.experimental import pallas as pl
from jax.experimental.pallas import tpu as pltpu
from jax.sharding import Mesh, PartitionSpec as P

ROW = ("x", "core")
COL = ("yh", "yl", "z")
F32 = jnp.float32
BF16 = jnp.bfloat16
TILE = 128
PARAMS = pltpu.CompilerParams(vmem_limit_bytes=20 * 2**20)
VM = pl.BlockSpec(memory_space=pltpu.VMEM)
SM = pl.BlockSpec(memory_space=pltpu.SMEM)


def split(value):
    high = value.astype(BF16)
    return high, (value - high.astype(F32)).astype(BF16)


def mm(a, b):
    return jnp.dot(a, b, preferred_element_type=F32)


def pack_left(value):
    return jnp.concatenate(split(value), 1)


def pack_right(value):
    high, low = split(value)
    return jnp.concatenate(
        [jnp.concatenate([high, low], 1), jnp.concatenate([high, jnp.zeros_like(low)], 1)], 0
    )


def packed_product(left, right):
    out = mm(left, right)
    return out[:, :TILE] + out[:, TILE:]


def invert_body(info, lead_ref, out_ref):
    out_ref[...] = lead_ref[...]

    @pl.when(info[0] == 1)
    def _():
        start = pl.multiple_of(info[1] * TILE, TILE)
        block = lead_ref[pl.ds(start, TILE), :]
        i = lax.broadcasted_iota(jnp.int32, (TILE, TILE), 0)
        j = lax.broadcasted_iota(jnp.int32, (TILE, TILE), 1)
        zero = jnp.zeros((TILE, TILE), F32)
        inverse = jnp.where(i == j, 1.0 / jnp.where(i == j, block, 1.0), zero)
        step = 1
        while step < TILE:
            below = ((i // (2 * step)) == (j // (2 * step))) & ((i // step) > (j // step))
            corner = jnp.where(below, block, zero)
            product = packed_product(pack_left(corner), pack_right(inverse))
            inverse = inverse - packed_product(pack_left(inverse), pack_right(product))
            step *= 2
        out_ref[pl.ds(start, TILE), :] = inverse


def invert_diagonal(info, lead):
    return pl.pallas_call(
        invert_body,
        out_shape=jax.ShapeDtypeStruct(lead.shape, F32),
        in_specs=[SM, VM],
        out_specs=VM,
        compiler_params=PARAMS,
        name="invert_diagonal",
    )(info, lead)


def solve(info, pieces, places, rhs):
    def body(info, *refs):
        rhs_ref, out_ref, tri_ref = refs[-3:]
        for ref, parts in zip(refs, places):
            for half, steps, start, to, rows in parts:
                half = {"own": info[0], "pair": 1 - info[0]}.get(half, half)
                k = 4 * half + lax.rem(info[1] + steps, 4)
                tri_ref[k, pl.ds(to, rows), :] = pack_left(ref[pl.ds(start, rows), :])
        out_ref[...] = rhs_ref[...]
        for k in range(8):
            here = pl.ds(k * TILE, TILE)
            solved = packed_product(tri_ref[k, here, :], pack_right(out_ref[here, :]))
            out_ref[here, :] = solved
            right = pack_right(solved)
            for i in range(k + 1, 8):
                there = pl.ds(i * TILE, TILE)
                out_ref[there, :] = out_ref[there, :] - packed_product(tri_ref[k, there, :], right)

    return pl.pallas_call(
        body,
        out_shape=jax.ShapeDtypeStruct(rhs.shape, F32),
        in_specs=[SM] + [VM] * (len(pieces) + 1),
        out_specs=VM,
        scratch_shapes=[pltpu.VMEM((8, 1024, 256), BF16)],
        compiler_params=PARAMS,
        name="block_solve",
    )(info, *pieces, rhs)


def residual(info, pieces, places, rhs, x):
    def body(info, *refs):
        rhs_ref, x_ref, out_ref = refs[-3:]
        out_ref[...] = rhs_ref[...]
        for ref, parts in zip(refs, places):
            ((half, steps, _, row, rows),) = parts
            half = {"own": info[0], "pair": 1 - info[0]}[half]
            k = 4 * half + lax.rem(info[1] + steps, 4)
            right = pack_right(x_ref[pl.ds(pl.multiple_of(k * TILE, TILE), TILE), :])
            for start in range(0, rows, TILE):
                there = pl.ds(row + start, TILE)
                out_ref[there, :] = out_ref[there, :] - packed_product(pack_left(ref[pl.ds(start, TILE), :]), right)

    return pl.pallas_call(
        body,
        out_shape=jax.ShapeDtypeStruct(rhs.shape, F32),
        in_specs=[SM] + [VM] * (len(pieces) + 2),
        out_specs=VM,
        compiler_params=PARAMS,
        name="block_residual",
    )(info, *pieces, rhs, x)


def arrange_body(factor_ref, out_ref):
    for c in range(16):
        for a in range(4):
            out_ref[c, pl.ds(64 * a, 64), :] = factor_ref[a, pl.ds(64 * c, 64), :]


def arrange(factor):
    return pl.pallas_call(
        arrange_body,
        out_shape=jax.ShapeDtypeStruct((16, 256, TILE), F32),
        in_specs=[VM],
        out_specs=VM,
        compiler_params=PARAMS,
        name="arrange_rows",
    )(factor)


def prepare_body(info, mine_ref, other_ref, high_ref, low_ref):
    for side, ref in enumerate((mine_ref, other_ref)):
        rows = pl.ds(256 * side, 256)
        for n in range(4):
            high, low = split(jnp.concatenate([ref[2 * n], ref[2 * n + 1]], 1))
            high_ref[n, rows, :] = high
            low_ref[n, rows, :] = low

    @pl.when(info[0] == 0)
    def _():
        for n in range(4):
            for side in range(2):
                high_ref[n, pl.ds(256 * side, 64), :] = jnp.zeros((64, 256), BF16)
                low_ref[n, pl.ds(256 * side, 64), :] = jnp.zeros((64, 256), BF16)


def prepare(info, mine, other):
    return pl.pallas_call(
        prepare_body,
        out_shape=[jax.ShapeDtypeStruct((4, 512, 256), BF16)] * 2,
        in_specs=[SM, VM, VM],
        out_specs=[VM, VM],
        compiler_params=PARAMS,
        name="prepare_update",
    )(info, mine, other)


def accumulate(info, sums, high, low, pieces, places, name):
    first = sums is None

    def body(info, high_ref, low_ref, *refs):
        out_ref = refs[-1]
        x, core, y, z, col = (info[k] for k in range(5))
        if first:
            out_ref[...] = jnp.zeros(out_ref.shape, F32)
        else:
            out_ref[...] = refs[0][...]
        for ref, (far, slot) in zip(refs[0 if first else 1 :], places):
            for n in range(ref.shape[0]):
                near = slot + n
                py = lax.rem(y + jnp.where(core == 0, far, near), 4)
                pz = lax.rem(z + jnp.where(core == 0, near, far), 4)
                upper = py // 2
                bit = jnp.where(upper == 0, py, 3 - py)
                cols = pl.ds(pl.multiple_of((4 * bit + pz) * TILE, TILE), TILE)
                total = None
                for h in range(2):
                    x_high, x_low = split(ref[n, pl.ds(256 * h, 256), :])
                    wide = mm(high_ref[2 * upper + h], jnp.concatenate([x_high, x_low], 1))
                    term = wide[:, :TILE] + (wide[:, TILE:] + mm(low_ref[2 * upper + h], x_high))
                    total = term if total is None else total + term
                out_ref[:, cols] = out_ref[:, cols] + total

                @pl.when((x == 0) & (col // 8 == upper))
                def _():
                    there = pl.ds(pl.multiple_of(lax.rem(col, 8) * 64, 64), 64)
                    here = pl.ds(0, 64)
                    out_ref[here, cols] = out_ref[here, cols] - ref[n, there, :]

    start = [] if first else [sums]
    return pl.pallas_call(
        body,
        out_shape=jax.ShapeDtypeStruct((512, 1024), F32),
        in_specs=[SM] + [VM] * (2 + len(start) + len(pieces)),
        out_specs=VM,
        input_output_aliases={} if first else {3: 0},
        compiler_params=PARAMS,
        name=name,
    )(info, high, low, *start, *pieces)


AXES = ROW + COL


def move(value, where):
    pairs = []
    for x in range(4):
        for core in range(2):
            for y in range(4):
                for z in range(4):
                    to = where(x, core, y, z)
                    if to is not None:
                        a, b, c, d = to
                        pairs.append((((x * 2 + core) * 4 + y) * 4 + z, ((a * 2 + b) * 4 + c % 4) * 4 + d % 4))
    return lax.ppermute(value, AXES, pairs)


def deal(first, second, core, yh, xi):
    solved = jnp.where(core == 0, first, second)
    lower = yh == 0
    here = jnp.where(lower, solved[:512], solved[512:])
    there = jnp.where(core == 0, solved[512:], solved[:512])
    got = move(there, lambda a, b, c, d: (0, b, 3 - c, d) if a == 0 and b == c // 2 else None)
    mine = jnp.where(core == yh, here, got)
    one = move(mine, lambda a, b, c, d: (1 if b == 0 else 3, b, c, d) if a == 0 else None)
    two = move(mine, lambda a, b, c, d: (3 if b == 0 else 1, b, c, d) if a == 0 else None)
    far = move(one, lambda a, b, c, d: (2, b, c, d) if a == (1 if b == 0 else 3) else None)
    return jnp.where(xi == 0, mine, one + two + far)


def ring(value, first):
    def along(step):
        def where(a, b, c, d):
            on_z = (b == 0) == first
            return (a, b, c, d + step) if on_z else (a, b, c + step, d)

        return where

    before = move(value, along(1))
    after = move(value, along(-1))
    cut = value.shape[0] // 2
    far_low = move(before[:cut], along(1))
    far_high = move(after[cut:], along(-1))
    return after, far_low, far_high, before


def gather_first(lead, yl):
    def holds(a, b, c):
        return a == 0 and b == 0 and c < 2

    swapped = move(lead, lambda a, b, c, d: (a, b, 1 - c, d) if holds(a, b, c) else None)
    full = jnp.where(yl == 0, lead, swapped)
    lower = jnp.where(yl == 0, swapped[512:], lead[512:])
    pair = jnp.concatenate([full, lower], 0)

    def along(step):
        return lambda a, b, c, d: (a, b, c, d + step) if holds(a, b, c) else None

    before, after = move(pair, along(1)), move(pair, along(-1))
    far_low, far_high = move(before[:768], along(1)), move(after[768:], along(-1))
    pieces, places = [], []
    for piece, steps in ((pair, 0), (after, 1), (before, 3)):
        pieces.append(piece)
        places.append([(0, steps, 0, 0, 1024), (1, steps, 1024, 512, 512)])
    pieces += [far_low, far_high]
    places += [[(0, 2, 0, 0, 768)], [(0, 2, 0, 768, 256), (1, 2, 256, 512, 512)]]
    return pieces, places


def gather_second(lead):
    def along(step):
        return lambda a, b, c, d: (0, 1, c, d + step) if a == 0 and b == 1 else None

    def pair(value):
        return move(value, lambda a, b, c, d: (0, 1, c + 1 - 2 * (c % 2), d) if a == 0 and b == 1 else None)

    before, after = move(lead, along(1)), move(lead, along(-1))
    far_low, far_high = move(before[:512], along(1)), move(after[512:], along(-1))
    pieces, places = [], []
    for piece, steps, row in ((lead, 0, 0), (after, 1, 0), (before, 3, 0), (far_low, 2, 0), (far_high, 2, 512)):
        pieces += [piece, pair(piece)]
        places += [[(half, steps, 0, row, piece.shape[0])] for half in ("own", "pair")]
    return pieces, places


def shards(factor, cross_cov):
    xi, core = lax.axis_index("x"), lax.axis_index("core")
    yh, yl, z = lax.axis_index("yh"), lax.axis_index("yl"), lax.axis_index("z")
    row_id = 2 * xi + core
    col_id = 8 * yh + 4 * yl + z
    local = factor[:, 0]
    rhs = cross_cov[:, 0]

    diagonal = ((row_id == 0) & (yh == 0)) | ((row_id == 1) & (yh == 1))
    info = jnp.stack([diagonal.astype(jnp.int32), (4 * yl + z).astype(jnp.int32)])
    lead = invert_diagonal(info, local[0])

    own_rhs = rhs[0].reshape(64, 2, 4, TILE).transpose(1, 2, 0, 3)
    own_rhs = jnp.where(yh == 0, own_rhs, own_rhs[::-1]).reshape(8, 64, TILE)
    half = lax.all_to_all(own_rhs, ("yl", "z"), 0, 0, tiled=True).reshape(512, TILE)
    other_half = move(half, lambda a, b, c, d: (0, b, 3 - c, d) if a == 0 and c >= 2 else None)
    columns = jnp.concatenate([half, other_half], 0)

    place = jnp.stack([yl, z]).astype(jnp.int32)
    upper_left = gather_first(lead, yl)
    lower_row = gather_second(lead)
    first = solve(place, *upper_left, columns)
    sent = move(first, lambda a, b, c, d: (0, 1, c, d) if (a, b) == (0, 0) and c < 2 else None)
    rest = residual(place, *lower_row, columns, sent)
    second_rhs = move(rest, lambda a, b, c, d: (0, 1, 3 - c, d) if (a, b) == (0, 1) and c < 2 else None)
    by_rows, second_rhs = lax.optimization_barrier((arrange(local), second_rhs))
    left = lax.all_to_all(by_rows, COL, 0, 0, tiled=True)
    second = solve(place, *lower_row, second_rhs)
    mine = deal(first, second, core, yh, xi)

    def swap(value):
        return move(value, lambda a, b, c, d: (a, 1 - b, c, d))

    left = left.reshape(2, 8, 256, TILE)
    kept = jnp.where(core == 0, left[0], left[1])
    given = jnp.where(core == 0, left[1], left[0])
    info2 = jnp.stack([xi, core, 2 * yh + yl, z, col_id]).astype(jnp.int32)

    after, far_low, far_high, before = ring(mine, True)
    near = jnp.stack([mine, after, jnp.concatenate([far_low, far_high], 0), before])

    def along(step):
        return lambda a, b, c, d: (a, b, c + step, d) if b == 0 else (a, b, c, d + step)

    before, after = move(near, along(1)), move(near, along(-1))
    high, low = prepare(info2[:1], kept, swap(given))
    sums = accumulate(info2, None, high, low, [near], [(0, 0)], "update_near")
    before, after, sums = lax.optimization_barrier((before, after, sums))
    far_low, far_high = move(before[:2], along(1)), move(after[2:], along(-1))
    sums = accumulate(info2, sums, high, low, [after, before], [(1, 0), (3, 0)], "update_next")
    far_low, far_high, sums = lax.optimization_barrier((far_low, far_high, sums))
    sums = accumulate(info2, sums, high, low, [far_low, far_high], [(2, 0), (2, 2)], "update_far")

    replaced = (xi == 0) & (lax.broadcasted_iota(jnp.int32, (256, 1024), 0) < 64)
    base = jnp.where(replaced, 0.0, rhs.reshape(256, 1024))
    out = base - (sums[:256] + swap(sums[256:]))
    return out.reshape(4, 1, 64, 1024)


def solution(mesh):
    fine = Mesh(mesh.devices.reshape(4, 2, 2, 2, 4), ROW + COL)
    return jax.shard_map(
        shards,
        mesh=fine,
        in_specs=(P(None, ROW, None, COL), P(None, ROW, COL, None)),
        out_specs=P(None, ROW, COL, None),
        check_vma=False,
    )
```

```python
import jax
import jax.numpy as jnp
from jax import lax
from jax.experimental import pallas as pl
from jax.experimental.pallas import tpu as pltpu
from jax.sharding import Mesh, PartitionSpec as P

ROW = ("x", "core")
COL = ("yh", "yl", "z")
F32 = jnp.float32
BF16 = jnp.bfloat16
TILE = 128
PARAMS = pltpu.CompilerParams(vmem_limit_bytes=20 * 2**20)
VM = pl.BlockSpec(memory_space=pltpu.VMEM)
SM = pl.BlockSpec(memory_space=pltpu.SMEM)


def split(value):
    high = value.astype(BF16)
    return high, (value - high.astype(F32)).astype(BF16)


def mm(a, b):
    return jnp.dot(a, b, preferred_element_type=F32)


def pack_left(value):
    return jnp.concatenate(split(value), 1)


def pack_right(value):
    high, low = split(value)
    return jnp.concatenate(
        [jnp.concatenate([high, low], 1), jnp.concatenate([high, jnp.zeros_like(low)], 1)], 0
    )


def packed_product(left, right):
    out = mm(left, right)
    return out[:, :TILE] + out[:, TILE:]


def invert_body(info, lead_ref, out_ref):
    out_ref[...] = lead_ref[...]

    @pl.when(info[0] == 1)
    def _():
        start = pl.multiple_of(info[1] * TILE, TILE)
        block = lead_ref[pl.ds(start, TILE), :]
        i = lax.broadcasted_iota(jnp.int32, (TILE, TILE), 0)
        j = lax.broadcasted_iota(jnp.int32, (TILE, TILE), 1)
        zero = jnp.zeros((TILE, TILE), F32)
        inverse = jnp.where(i == j, 1.0 / jnp.where(i == j, block, 1.0), zero)
        step = 1
        while step < TILE:
            below = ((i // (2 * step)) == (j // (2 * step))) & ((i // step) > (j // step))
            corner = jnp.where(below, block, zero)
            product = packed_product(pack_left(corner), pack_right(inverse))
            inverse = inverse - packed_product(pack_left(inverse), pack_right(product))
            step *= 2
        out_ref[pl.ds(start, TILE), :] = inverse


def invert_diagonal(info, lead):
    return pl.pallas_call(
        invert_body,
        out_shape=jax.ShapeDtypeStruct(lead.shape, F32),
        in_specs=[SM, VM],
        out_specs=VM,
        compiler_params=PARAMS,
        name="invert_diagonal",
    )(info, lead)


def solve(info, pieces, places, rhs):
    def body(info, *refs):
        rhs_ref, out_ref, tri_ref = refs[-3:]
        for ref, parts in zip(refs, places):
            for half, steps, start, to, rows in parts:
                half = {"own": info[0], "pair": 1 - info[0]}.get(half, half)
                k = 4 * half + lax.rem(info[1] + steps, 4)
                tri_ref[k, pl.ds(to, rows), :] = pack_left(ref[pl.ds(start, rows), :])
        out_ref[...] = rhs_ref[...]
        for k in range(8):
            here = pl.ds(k * TILE, TILE)
            solved = packed_product(tri_ref[k, here, :], pack_right(out_ref[here, :]))
            out_ref[here, :] = solved
            right = pack_right(solved)
            for i in range(k + 1, 8):
                there = pl.ds(i * TILE, TILE)
                out_ref[there, :] = out_ref[there, :] - packed_product(tri_ref[k, there, :], right)

    return pl.pallas_call(
        body,
        out_shape=jax.ShapeDtypeStruct(rhs.shape, F32),
        in_specs=[SM] + [VM] * (len(pieces) + 1),
        out_specs=VM,
        scratch_shapes=[pltpu.VMEM((8, 1024, 256), BF16)],
        compiler_params=PARAMS,
        name="block_solve",
    )(info, *pieces, rhs)


def residual(info, pieces, places, rhs, x):
    def body(info, *refs):
        rhs_ref, x_ref, out_ref = refs[-3:]
        out_ref[...] = rhs_ref[...]
        for ref, parts in zip(refs, places):
            for half, steps, start, to, rows in parts:
                half = {"own": info[0], "pair": 1 - info[0]}[half]
                k = 4 * half + lax.rem(info[1] + steps, 4)
                right = pack_right(x_ref[pl.ds(pl.multiple_of(k * TILE, TILE), TILE), :])
                for n in range(0, rows, TILE):
                    there = pl.ds(to + n, TILE)
                    left = pack_left(ref[pl.ds(start + n, TILE), :])
                    out_ref[there, :] = out_ref[there, :] - packed_product(left, right)

    return pl.pallas_call(
        body,
        out_shape=jax.ShapeDtypeStruct(rhs.shape, F32),
        in_specs=[SM] + [VM] * (len(pieces) + 2),
        out_specs=VM,
        compiler_params=PARAMS,
        name="block_residual",
    )(info, *pieces, rhs, x)


def arrange_body(factor_ref, out_ref):
    for c in range(16):
        for a in range(4):
            out_ref[c, pl.ds(64 * a, 64), :] = factor_ref[a, pl.ds(64 * c, 64), :]


def arrange(factor):
    return pl.pallas_call(
        arrange_body,
        out_shape=jax.ShapeDtypeStruct((16, 256, TILE), F32),
        in_specs=[VM],
        out_specs=VM,
        compiler_params=PARAMS,
        name="arrange_rows",
    )(factor)


def arrange_rhs_body(info, rhs_ref, out_ref):
    for n in range(8):
        to = jnp.where(info[0] == 0, n, (n + 4) % 8)
        out_ref[to, :, :] = rhs_ref[0, :, pl.ds(n * TILE, TILE)]


def arrange_rhs(yh, rhs):
    return pl.pallas_call(
        arrange_rhs_body,
        grid=(1,),
        out_shape=jax.ShapeDtypeStruct((8, 64, TILE), F32),
        in_specs=[SM, pl.BlockSpec((1, 64, 1024), lambda i: (0, 0, 0))],
        out_specs=pl.BlockSpec((8, 64, TILE), lambda i: (0, 0, 0)),
        compiler_params=PARAMS,
        name="arrange_rhs",
    )(jnp.reshape(yh, (1,)).astype(jnp.int32), rhs)


def prepare_body(info, left_ref, other_ref, high_ref, low_ref):
    for side, ref in enumerate((left_ref, other_ref)):
        rows = pl.ds(256 * side, 256)
        first = 8 * info[1] if side == 0 else 0
        for n in range(4):
            high, low = split(jnp.concatenate([ref[first + 2 * n], ref[first + 2 * n + 1]], 1))
            high_ref[n, rows, :] = high
            low_ref[n, rows, :] = low

    @pl.when(info[0] == 0)
    def _():
        for n in range(4):
            for side in range(2):
                high_ref[n, pl.ds(256 * side, 64), :] = jnp.zeros((64, 256), BF16)
                low_ref[n, pl.ds(256 * side, 64), :] = jnp.zeros((64, 256), BF16)


def prepare(info, left, other):
    return pl.pallas_call(
        prepare_body,
        out_shape=[jax.ShapeDtypeStruct((4, 512, 256), BF16)] * 2,
        in_specs=[SM, VM, VM],
        out_specs=[VM, VM],
        compiler_params=PARAMS,
        name="prepare_update",
    )(info, left, other)


def accumulate(info, sums, high, low, pieces, places, name):
    first = sums is None

    def body(info, high_ref, low_ref, *refs):
        out_ref = refs[-1]
        x, core, y, z, col = (info[k] for k in range(5))
        if first:
            out_ref[...] = jnp.zeros(out_ref.shape, F32)
        else:
            out_ref[...] = refs[0][...]
        for ref, (far, slot) in zip(refs[0 if first else 1 :], places):
            for n in range(ref.shape[0]):
                near = slot + n
                py = lax.rem(y + jnp.where(core == 0, far, near), 4)
                pz = lax.rem(z + jnp.where(core == 0, near, far), 4)
                upper = py // 2
                bit = jnp.where(upper == 0, py, 3 - py)
                cols = pl.ds(pl.multiple_of((4 * bit + pz) * TILE, TILE), TILE)
                total = None
                for h in range(2):
                    x_high, x_low = split(ref[n, pl.ds(256 * h, 256), :])
                    wide = mm(high_ref[2 * upper + h], jnp.concatenate([x_high, x_low], 1))
                    term = wide[:, :TILE] + (wide[:, TILE:] + mm(low_ref[2 * upper + h], x_high))
                    total = term if total is None else total + term
                out_ref[:, cols] = out_ref[:, cols] + total

                @pl.when((x == 0) & (col // 8 == upper))
                def _():
                    there = pl.ds(pl.multiple_of(lax.rem(col, 8) * 64, 64), 64)
                    here = pl.ds(0, 64)
                    out_ref[here, cols] = out_ref[here, cols] - ref[n, there, :]

    start = [] if first else [sums]
    return pl.pallas_call(
        body,
        out_shape=jax.ShapeDtypeStruct((512, 1024), F32),
        in_specs=[SM] + [VM] * (2 + len(start) + len(pieces)),
        out_specs=VM,
        input_output_aliases={} if first else {3: 0},
        compiler_params=PARAMS,
        name=name,
    )(info, high, low, *start, *pieces)


AXES = ROW + COL


def move(value, where):
    pairs = []
    for x in range(4):
        for core in range(2):
            for y in range(4):
                for z in range(4):
                    to = where(x, core, y, z)
                    if to is not None:
                        a, b, c, d = to
                        pairs.append((((x * 2 + core) * 4 + y) * 4 + z, ((a * 2 + b) * 4 + c % 4) * 4 + d % 4))
    return lax.ppermute(value, AXES, pairs)


def deal(first, second, core, yh, xi):
    solved = jnp.where(core == 0, first, second)
    lower = yh == 0
    here = jnp.where(lower, solved[:512], solved[512:])
    there = jnp.where(core == 0, solved[512:], solved[:512])
    got = move(there, lambda a, b, c, d: (0, b, 3 - c, d) if a == 0 and b == c // 2 else None)
    mine = jnp.where(core == yh, here, got)
    one = move(mine, lambda a, b, c, d: (1 if b == 0 else 3, b, c, d) if a == 0 else None)
    two = move(mine, lambda a, b, c, d: (3 if b == 0 else 1, b, c, d) if a == 0 else None)
    far = move(one, lambda a, b, c, d: (2, b, c, d) if a == (1 if b == 0 else 3) else None)
    return jnp.where(xi == 0, mine, one + two + far)


def ring(value, first):
    def along(step):
        def where(a, b, c, d):
            on_z = (b == 0) == first
            return (a, b, c, d + step) if on_z else (a, b, c + step, d)

        return where

    before = move(value, along(1))
    after = move(value, along(-1))
    cut = value.shape[0] // 2
    far_low = move(before[:cut], along(1))
    far_high = move(after[cut:], along(-1))
    return after, far_low, far_high, before


def gather(lead, half, core, yl):
    def holds(a, b, c):
        return a == 0 and (b == 1 or c < 2)

    def step(b_on_z, amount):
        def where(a, b, c, d):
            if not holds(a, b, c):
                return None
            return (a, b, c, d + amount) if b == b_on_z else (a, b, c + 1 - 2 * (c % 2), d)

        return where

    def only(b_only, amount):
        return lambda a, b, c, d: (a, b, c, d + amount) if holds(a, b, c) and b == b_only else None

    mixed = move(lead, step(1, 1))
    after = move(lead, only(1, -1))
    swapped = move(lead, lambda a, b, c, d: (a, b, c + 1 - 2 * (c % 2), d) if holds(a, b, c) and b == 1 else None)
    mixed, swapped, half = lax.optimization_barrier((mixed, swapped, half))
    far_low = move(mixed[:512], only(1, 1))
    far_high = move(after[512:], only(1, -1))

    full = jnp.where(yl == 0, lead, mixed)
    lower = jnp.where(yl == 0, mixed[512:], lead[512:])
    zero = core == 0
    first = jnp.concatenate([jnp.where(zero, full, mixed), jnp.where(zero, lower, far_low)], 0)
    second = jnp.concatenate([jnp.where(zero, full, after), jnp.where(zero, lower, far_high)], 0)
    got_first = move(first, step(0, 1))
    got_second = move(second, step(0, -1))
    end_low = move(got_first[:768], only(0, 1))
    end_high = move(got_second[768:], only(0, -1))

    corner_pieces = [first, got_second, got_first, end_low, end_high]
    corner_places = [[(0, n, 0, 0, 1024), (1, n, 1024, 512, 512)] for n in (0, 1, 3)]
    corner_places += [[(0, 2, 0, 0, 768)], [(0, 2, 0, 768, 256), (1, 2, 256, 512, 512)]]
    lower_pieces = [lead, swapped, first, second, got_first, got_second]
    lower_places = [[("own", 0, 0, 0, 1024)], [("pair", 0, 0, 0, 1024)]]
    for group in ("own", "pair"):
        lower_places.append([(group, 3, 0, 0, 1024), (group, 2, 1024, 0, 512)])
        lower_places.append([(group, 1, 0, 0, 1024), (group, 2, 1024, 512, 512)])
    return (corner_pieces, corner_places), (lower_pieces, lower_places), half


def shards(factor, cross_cov):
    xi, core = lax.axis_index("x"), lax.axis_index("core")
    yh, yl, z = lax.axis_index("yh"), lax.axis_index("yl"), lax.axis_index("z")
    row_id = 2 * xi + core
    col_id = 8 * yh + 4 * yl + z
    local = factor[:, 0]
    rhs = cross_cov[:, 0]

    diagonal = ((row_id == 0) & (yh == 0)) | ((row_id == 1) & (yh == 1))
    info = jnp.stack([diagonal.astype(jnp.int32), (4 * yl + z).astype(jnp.int32)])
    lead = invert_diagonal(info, local[0])

    half = lax.all_to_all(arrange_rhs(yh, rhs), ("yl", "z"), 0, 0, tiled=True).reshape(512, TILE)
    upper_left, lower_row, half = gather(lead, half, core, yl)
    other_half = move(half, lambda a, b, c, d: (0, b, 3 - c, d) if a == 0 and c >= 2 else None)
    columns = jnp.concatenate([half, other_half], 0)

    place = jnp.stack([yl, z]).astype(jnp.int32)
    first = solve(place, *upper_left, columns)
    sent = move(first, lambda a, b, c, d: (0, 1, c, d) if (a, b) == (0, 0) and c < 2 else None)
    rest = residual(place, *lower_row, columns, sent)
    second_rhs = move(rest, lambda a, b, c, d: (0, 1, 3 - c, d) if (a, b) == (0, 1) and c < 2 else None)
    by_rows, rest = lax.optimization_barrier((arrange(local), rest))
    left = lax.all_to_all(by_rows, COL, 0, 0, tiled=True)
    second = solve(place, *lower_row, second_rhs)
    mine, left = lax.optimization_barrier((deal(first, second, core, yh, xi), left))

    def swap(value):
        return move(value, lambda a, b, c, d: (a, 1 - b, c, d))

    given = swap(lax.dynamic_slice_in_dim(left, 8 * (1 - core), 8, 0))
    info2 = jnp.stack([xi, core, 2 * yh + yl, z, col_id]).astype(jnp.int32)

    after, far_low, far_high, before = ring(mine, True)
    near = jnp.stack([mine, after, jnp.concatenate([far_low, far_high], 0), before])

    def along(step):
        return lambda a, b, c, d: (a, b, c + step, d) if b == 0 else (a, b, c, d + step)

    before, after = move(near, along(1)), move(near, along(-1))
    high, low = prepare(info2[:2], left, given)
    sums = accumulate(info2, None, high, low, [near], [(0, 0)], "update_near")
    before, after, sums = lax.optimization_barrier((before, after, sums))
    far_low, far_high = move(before[:2], along(1)), move(after[2:], along(-1))
    sums = accumulate(info2, sums, high, low, [after, before], [(1, 0), (3, 0)], "update_next")
    far_low, far_high, sums = lax.optimization_barrier((far_low, far_high, sums))
    sums = accumulate(info2, sums, high, low, [far_low, far_high], [(2, 0), (2, 2)], "update_far")

    replaced = (xi == 0) & (lax.broadcasted_iota(jnp.int32, (256, 1024), 0) < 64)
    base = jnp.where(replaced, 0.0, rhs.reshape(256, 1024))
    out = base - (sums[:256] + swap(sums[256:]))
    return out.reshape(4, 1, 64, 1024)


def solution(mesh):
    fine = Mesh(mesh.devices.reshape(4, 2, 2, 2, 4), ROW + COL)
    return jax.shard_map(
        shards,
        mesh=fine,
        in_specs=(P(None, ROW, None, COL), P(None, ROW, COL, None)),
        out_specs=P(None, ROW, COL, None),
        check_vma=False,
    )
```

```python
import jax
import jax.numpy as jnp
from jax import lax
from jax.experimental import pallas as pl
from jax.experimental.pallas import tpu as pltpu
from jax.sharding import Mesh, PartitionSpec as P

ROW = ("x", "core")
COL = ("yh", "yl", "z")
F32 = jnp.float32
BF16 = jnp.bfloat16
TILE = 128
PARAMS = pltpu.CompilerParams(vmem_limit_bytes=20 * 2**20)
VM = pl.BlockSpec(memory_space=pltpu.VMEM)
SM = pl.BlockSpec(memory_space=pltpu.SMEM)
FAR = pl.BlockSpec(memory_space=pltpu.HBM)


def split(value):
    high = value.astype(BF16)
    return high, (value - high.astype(F32)).astype(BF16)


def mm(a, b):
    return jnp.dot(a, b, preferred_element_type=F32)


def pack_left(value):
    return jnp.concatenate(split(value), 1)


def pack_right(value):
    high, low = split(value)
    return jnp.concatenate(
        [jnp.concatenate([high, low], 1), jnp.concatenate([high, jnp.zeros_like(low)], 1)], 0
    )


def packed_product(left, right):
    out = mm(left, right)
    return out[:, :TILE] + out[:, TILE:]


def invert_body(info, lead_ref, out_ref):
    out_ref[...] = lead_ref[...]

    @pl.when(info[0] == 1)
    def _():
        start = pl.multiple_of(info[1] * TILE, TILE)
        block = lead_ref[pl.ds(start, TILE), :]
        i = lax.broadcasted_iota(jnp.int32, (TILE, TILE), 0)
        j = lax.broadcasted_iota(jnp.int32, (TILE, TILE), 1)
        zero = jnp.zeros((TILE, TILE), F32)
        inverse = jnp.where(i == j, 1.0 / jnp.where(i == j, block, 1.0), zero)
        step = 1
        while step < TILE:
            below = ((i // (2 * step)) == (j // (2 * step))) & ((i // step) > (j // step))
            corner = jnp.where(below, block, zero)
            product = packed_product(pack_left(corner), pack_right(inverse))
            inverse = inverse - packed_product(pack_left(inverse), pack_right(product))
            step *= 2
        out_ref[pl.ds(start, TILE), :] = inverse


def invert_diagonal(info, lead):
    return pl.pallas_call(
        invert_body,
        out_shape=jax.ShapeDtypeStruct(lead.shape, F32),
        in_specs=[SM, VM],
        out_specs=VM,
        compiler_params=PARAMS,
        name="invert_diagonal",
    )(info, lead)


def solve(info, pieces, places, rhs, streamed, name):
    count = len(pieces)

    def body(info, *refs):
        sources, (rhs_ref, out_ref, tri_ref) = refs[:count], refs[count : count + 3]

        @pl.when(info[2] == 1)
        def _():
            copies = []
            if streamed:
                buffers, semaphores = refs[count + 3 : 2 * count + 3], refs[-1]
                for n in range(count):
                    copies.append(pltpu.make_async_copy(sources[n], buffers[n], semaphores.at[n]))
                    copies[-1].start()
            else:
                buffers = sources
            for n in range(count):
                if streamed:
                    copies[n].wait()
                for half, steps, start, to, rows in places[n]:
                    half = {"own": info[0], "pair": 1 - info[0]}.get(half, half)
                    k = 4 * half + lax.rem(info[1] + steps, 4)
                    tri_ref[k, pl.ds(to, rows), :] = pack_left(buffers[n][pl.ds(start, rows), :])
            out_ref[...] = rhs_ref[...]
            for k in range(8):
                here = pl.ds(k * TILE, TILE)
                solved = packed_product(tri_ref[k, here, :], pack_right(out_ref[here, :]))
                out_ref[here, :] = solved
                right = pack_right(solved)
                for i in range(k + 1, 8):
                    there = pl.ds(i * TILE, TILE)
                    out_ref[there, :] = out_ref[there, :] - packed_product(tri_ref[k, there, :], right)

    scratch = [pltpu.VMEM((8, 1024, 256), BF16)]
    if streamed:
        scratch += [pltpu.VMEM(piece.shape, F32) for piece in pieces] + [pltpu.SemaphoreType.DMA((count,))]
    return pl.pallas_call(
        body,
        out_shape=jax.ShapeDtypeStruct(rhs.shape, F32),
        in_specs=[SM] + [FAR if streamed else VM] * count + [VM],
        out_specs=VM,
        scratch_shapes=scratch,
        compiler_params=PARAMS,
        name=name,
    )(info, *pieces, rhs)


def residual(info, pieces, places, rhs, x):
    count = len(pieces)

    def body(info, *refs):
        sources, (rhs_ref, x_ref, out_ref) = refs[:count], refs[count : count + 3]
        buffers, semaphores = refs[count + 3 : 2 * count + 3], refs[-1]

        @pl.when(info[2] == 1)
        def _():
            copies = []
            for n in range(count):
                copies.append(pltpu.make_async_copy(sources[n], buffers[n], semaphores.at[n]))
                copies[-1].start()
            out_ref[...] = rhs_ref[...]
            for copy, ref, parts in zip(copies, buffers, places):
                copy.wait()
                for half, steps, start, to, rows in parts:
                    half = {"own": info[0], "pair": 1 - info[0]}[half]
                    k = 4 * half + lax.rem(info[1] + steps, 4)
                    right = pack_right(x_ref[pl.ds(pl.multiple_of(k * TILE, TILE), TILE), :])
                    for n in range(0, rows, TILE):
                        there = pl.ds(to + n, TILE)
                        left = pack_left(ref[pl.ds(start + n, TILE), :])
                        out_ref[there, :] = out_ref[there, :] - packed_product(left, right)

    return pl.pallas_call(
        body,
        out_shape=jax.ShapeDtypeStruct(rhs.shape, F32),
        in_specs=[SM] + [FAR] * count + [VM, VM],
        out_specs=VM,
        scratch_shapes=[pltpu.VMEM(piece.shape, F32) for piece in pieces] + [pltpu.SemaphoreType.DMA((count,))],
        compiler_params=PARAMS,
        name="block_residual",
    )(info, *pieces, rhs, x)


def arrange_body(factor_ref, out_ref):
    for c in range(16):
        for a in range(4):
            out_ref[c, pl.ds(64 * a, 64), :] = factor_ref[a, pl.ds(64 * c, 64), :]


def arrange(factor):
    return pl.pallas_call(
        arrange_body,
        out_shape=jax.ShapeDtypeStruct((16, 256, TILE), F32),
        in_specs=[VM],
        out_specs=VM,
        compiler_params=PARAMS,
        name="arrange_rows",
    )(factor)


def arrange_rhs_body(rhs_ref, out_ref):
    for n in range(16):
        out_ref[n, :, :] = rhs_ref[0, :, pl.ds(n % 8 * TILE, TILE)]


def arrange_rhs(rhs):
    return pl.pallas_call(
        arrange_rhs_body,
        grid=(1,),
        out_shape=jax.ShapeDtypeStruct((16, 64, TILE), F32),
        in_specs=[pl.BlockSpec((1, 64, 1024), lambda i: (0, 0, 0))],
        out_specs=pl.BlockSpec((16, 64, TILE), lambda i: (0, 0, 0)),
        compiler_params=PARAMS,
        name="arrange_rhs",
    )(rhs)


def prepare_body(info, left_ref, other_ref, high_ref, low_ref):
    for side, ref in enumerate((left_ref, other_ref)):
        rows = pl.ds(256 * side, 256)
        first = 8 * info[1] if side == 0 else 0
        for n in range(4):
            high, low = split(jnp.concatenate([ref[first + 2 * n], ref[first + 2 * n + 1]], 1))
            high_ref[n, rows, :] = high
            low_ref[n, rows, :] = low

    @pl.when(info[0] == 0)
    def _():
        for n in range(4):
            for side in range(2):
                high_ref[n, pl.ds(256 * side, 64), :] = jnp.zeros((64, 256), BF16)
                low_ref[n, pl.ds(256 * side, 64), :] = jnp.zeros((64, 256), BF16)


def prepare(info, left, other):
    return pl.pallas_call(
        prepare_body,
        out_shape=[jax.ShapeDtypeStruct((4, 512, 256), BF16)] * 2,
        in_specs=[SM, VM, VM],
        out_specs=[VM, VM],
        compiler_params=PARAMS,
        name="prepare_update",
    )(info, left, other)


def accumulate(info, sums, high, low, pieces, places, name):
    first = sums is None

    def body(info, high_ref, low_ref, *refs):
        out_ref = refs[-1]
        x, core, y, z, col = (info[k] for k in range(5))
        if first:
            out_ref[...] = jnp.zeros(out_ref.shape, F32)
        else:
            out_ref[...] = refs[0][...]
        for ref, (far, slot) in zip(refs[0 if first else 1 :], places):
            for n in range(ref.shape[0]):
                near = slot + n
                py = lax.rem(y + jnp.where(core == 0, far, near), 4)
                pz = lax.rem(z + jnp.where(core == 0, near, far), 4)
                upper = py // 2
                bit = jnp.where(upper == 0, py, 3 - py)
                cols = pl.ds(pl.multiple_of((4 * bit + pz) * TILE, TILE), TILE)
                total = None
                for h in range(2):
                    x_high, x_low = split(ref[n, pl.ds(256 * h, 256), :])
                    wide = mm(high_ref[2 * upper + h], jnp.concatenate([x_high, x_low], 1))
                    term = wide[:, :TILE] + (wide[:, TILE:] + mm(low_ref[2 * upper + h], x_high))
                    total = term if total is None else total + term
                out_ref[:, cols] = out_ref[:, cols] + total

                @pl.when((x == 0) & (col // 8 == upper))
                def _():
                    there = pl.ds(pl.multiple_of(lax.rem(col, 8) * 64, 64), 64)
                    here = pl.ds(0, 64)
                    out_ref[here, cols] = out_ref[here, cols] - ref[n, there, :]

    start = [] if first else [sums]
    return pl.pallas_call(
        body,
        out_shape=jax.ShapeDtypeStruct((512, 1024), F32),
        in_specs=[SM] + [VM] * (2 + len(start) + len(pieces)),
        out_specs=VM,
        input_output_aliases={} if first else {3: 0},
        compiler_params=PARAMS,
        name=name,
    )(info, high, low, *start, *pieces)


AXES = ROW + COL


def move(value, where):
    pairs = []
    for x in range(4):
        for core in range(2):
            for y in range(4):
                for z in range(4):
                    to = where(x, core, y, z)
                    if to is not None:
                        a, b, c, d = to
                        pairs.append((((x * 2 + core) * 4 + y) * 4 + z, ((a * 2 + b) * 4 + c % 4) * 4 + d % 4))
    return lax.ppermute(value, AXES, pairs)


def deal(first, second, core, yh, xi):
    solved = jnp.where(core == 0, first, second)
    lower = yh == 0
    here = jnp.where(lower, solved[:512], solved[512:])
    there = jnp.where(core == 0, solved[512:], solved[:512])
    got = move(there, lambda a, b, c, d: (0, b, 3 - c, d) if a == 0 and b == c // 2 else None)
    mine = jnp.where(core == yh, here, got)
    one = move(mine, lambda a, b, c, d: (1 if b == 0 else 3, b, c, d) if a == 0 else None)
    two = move(mine, lambda a, b, c, d: (3 if b == 0 else 1, b, c, d) if a == 0 else None)
    far = move(one, lambda a, b, c, d: (2, b, c, d) if a == (1 if b == 0 else 3) else None)
    return jnp.where(xi == 0, mine, one + two + far)


def ring(value, first):
    def along(step):
        def where(a, b, c, d):
            on_z = (b == 0) == first
            return (a, b, c, d + step) if on_z else (a, b, c + step, d)

        return where

    before = move(value, along(1))
    after = move(value, along(-1))
    cut = value.shape[0] // 2
    far_low = move(before[:cut], along(1))
    far_high = move(after[cut:], along(-1))
    return after, far_low, far_high, before


def gather(lead, columns, core, yl):
    def holds(a, b, c):
        return a == 0 and (b == 1 or c < 2)

    def step(b_on_z, amount):
        def where(a, b, c, d):
            if not holds(a, b, c):
                return None
            return (a, b, c, d + amount) if b == b_on_z else (a, b, c + 1 - 2 * (c % 2), d)

        return where

    def only(b_only, amount):
        return lambda a, b, c, d: (a, b, c, d + amount) if holds(a, b, c) and b == b_only else None

    mixed = move(lead, step(1, 1))
    after = move(lead, only(1, -1))
    swapped = move(lead, lambda a, b, c, d: (a, b, c + 1 - 2 * (c % 2), d) if holds(a, b, c) and b == 1 else None)
    mixed, swapped, columns = lax.optimization_barrier((mixed, swapped, columns))
    far_low = move(mixed[:512], only(1, 1))
    far_high = move(after[512:], only(1, -1))

    full = jnp.where(yl == 0, lead, mixed)
    lower = jnp.where(yl == 0, mixed[512:], lead[512:])
    zero = core == 0
    first = jnp.concatenate([jnp.where(zero, full, mixed), jnp.where(zero, lower, far_low)], 0)
    second = jnp.concatenate([jnp.where(zero, full, after), jnp.where(zero, lower, far_high)], 0)
    got_first = move(first, step(0, 1))
    got_second = move(second, step(0, -1))
    end_low = move(got_first[:768], only(0, 1))
    end_high = move(got_second[768:], only(0, -1))

    corner_pieces = [first, got_second, got_first, end_low, end_high]
    corner_places = [[(0, n, 0, 0, 1024), (1, n, 1024, 512, 512)] for n in (0, 1, 3)]
    corner_places += [[(0, 2, 0, 0, 768)], [(0, 2, 0, 768, 256), (1, 2, 256, 512, 512)]]
    lower_pieces = [lead, swapped, first, second, got_first, got_second]
    lower_places = [[("own", 0, 0, 0, 1024)], [("pair", 0, 0, 0, 1024)]]
    for group in ("own", "pair"):
        lower_places.append([(group, 3, 0, 0, 1024), (group, 2, 1024, 0, 512)])
        lower_places.append([(group, 1, 0, 0, 1024), (group, 2, 1024, 512, 512)])
    return (corner_pieces, corner_places), (lower_pieces, lower_places), columns


def shards(factor, cross_cov):
    xi, core = lax.axis_index("x"), lax.axis_index("core")
    yh, yl, z = lax.axis_index("yh"), lax.axis_index("yl"), lax.axis_index("z")
    row_id = 2 * xi + core
    col_id = 8 * yh + 4 * yl + z
    local = factor[:, 0]
    rhs = cross_cov[:, 0]

    diagonal = ((row_id == 0) & (yh == 0)) | ((row_id == 1) & (yh == 1))
    info = jnp.stack([diagonal.astype(jnp.int32), (4 * yl + z).astype(jnp.int32)])
    lead = invert_diagonal(info, local[0])

    columns = lax.all_to_all(arrange_rhs(rhs), COL, 0, 0, tiled=True).reshape(1024, TILE)
    upper_left, lower_row, columns = gather(lead, columns, core, yl)

    def place(active):
        return jnp.stack([yl, z, (active & (xi == 0)).astype(jnp.int32)]).astype(jnp.int32)

    first = solve(place((core == 0) & (yh == 0)), *upper_left, columns, False, "solve_first")
    sent = move(first, lambda a, b, c, d: (0, 1, c, d) if (a, b) == (0, 0) and c < 2 else None)
    rest = residual(place((core == 1) & (yh == 0)), *lower_row, columns, sent)
    second_rhs = move(rest, lambda a, b, c, d: (0, 1, 3 - c, d) if (a, b) == (0, 1) and c < 2 else None)
    by_rows, rest = lax.optimization_barrier((arrange(local), rest))
    left = lax.all_to_all(by_rows, COL, 0, 0, tiled=True)
    second = solve(place((core == 1) & (yh == 1)), *lower_row, second_rhs, True, "solve_second")
    mine, left = lax.optimization_barrier((deal(first, second, core, yh, xi), left))

    def swap(value):
        return move(value, lambda a, b, c, d: (a, 1 - b, c, d))

    given = swap(lax.dynamic_slice_in_dim(left, 8 * (1 - core), 8, 0))
    info2 = jnp.stack([xi, core, 2 * yh + yl, z, col_id]).astype(jnp.int32)

    after, far_low, far_high, before = ring(mine, True)
    near = jnp.stack([mine, after, jnp.concatenate([far_low, far_high], 0), before])

    def along(step):
        return lambda a, b, c, d: (a, b, c + step, d) if b == 0 else (a, b, c, d + step)

    before, after = move(near, along(1)), move(near, along(-1))
    high, low = prepare(info2[:2], left, given)
    sums = accumulate(info2, None, high, low, [near], [(0, 0)], "update_near")
    before, after, sums = lax.optimization_barrier((before, after, sums))
    far_low, far_high = move(before[:2], along(1)), move(after[2:], along(-1))
    sums = accumulate(info2, sums, high, low, [after, before], [(1, 0), (3, 0)], "update_next")
    far_low, far_high, sums = lax.optimization_barrier((far_low, far_high, sums))
    sums = accumulate(info2, sums, high, low, [far_low, far_high], [(2, 0), (2, 2)], "update_far")

    replaced = (xi == 0) & (lax.broadcasted_iota(jnp.int32, (256, 1024), 0) < 64)
    base = jnp.where(replaced, 0.0, rhs.reshape(256, 1024))
    out = base - (sums[:256] + swap(sums[256:]))
    return out.reshape(4, 1, 64, 1024)


def solution(mesh):
    fine = Mesh(mesh.devices.reshape(4, 2, 2, 2, 4), ROW + COL)
    return jax.shard_map(
        shards,
        mesh=fine,
        in_specs=(P(None, ROW, None, COL), P(None, ROW, COL, None)),
        out_specs=P(None, ROW, COL, None),
        check_vma=False,
    )
```

```python
import jax
import jax.numpy as jnp
from jax import lax
from jax.experimental import pallas as pl
from jax.experimental.pallas import tpu as pltpu
from jax.sharding import Mesh, PartitionSpec as P

ROW = ("x", "core")
COL = ("yh", "yl", "z")
F32 = jnp.float32
BF16 = jnp.bfloat16
TILE = 128
PARAMS = pltpu.CompilerParams(vmem_limit_bytes=20 * 2**20)
VM = pl.BlockSpec(memory_space=pltpu.VMEM)
SM = pl.BlockSpec(memory_space=pltpu.SMEM)


def split(value):
    high = value.astype(BF16)
    return high, (value - high.astype(F32)).astype(BF16)


def mm(a, b):
    return jnp.dot(a, b, preferred_element_type=F32)


def pack_left(value):
    return jnp.concatenate(split(value), 1)


def pack_right(value):
    high, low = split(value)
    return jnp.concatenate(
        [jnp.concatenate([high, low], 1), jnp.concatenate([high, jnp.zeros_like(low)], 1)], 0
    )


def packed_product(left, right):
    out = mm(left, right)
    return out[:, :TILE] + out[:, TILE:]


def invert_body(info, lead_ref, out_ref):
    out_ref[...] = lead_ref[...]

    @pl.when(info[0] == 1)
    def _():
        start = pl.multiple_of(info[1] * TILE, TILE)
        block = lead_ref[pl.ds(start, TILE), :]
        i = lax.broadcasted_iota(jnp.int32, (TILE, TILE), 0)
        j = lax.broadcasted_iota(jnp.int32, (TILE, TILE), 1)
        zero = jnp.zeros((TILE, TILE), F32)
        inverse = jnp.where(i == j, 1.0 / jnp.where(i == j, block, 1.0), zero)
        step = 1
        while step < TILE:
            below = ((i // (2 * step)) == (j // (2 * step))) & ((i // step) > (j // step))
            corner = jnp.where(below, block, zero)
            product = packed_product(pack_left(corner), pack_right(inverse))
            inverse = inverse - packed_product(pack_left(inverse), pack_right(product))
            step *= 2
        out_ref[pl.ds(start, TILE), :] = inverse


def invert_diagonal(info, lead):
    return pl.pallas_call(
        invert_body,
        out_shape=jax.ShapeDtypeStruct(lead.shape, F32),
        in_specs=[SM, VM],
        out_specs=VM,
        compiler_params=PARAMS,
        name="invert_diagonal",
    )(info, lead)


def solve(active, tri, rhs):
    def body(active, tri_ref, rhs_ref, out_ref):
        @pl.when(active[0] == 1)
        def _():
            out_ref[...] = rhs_ref[...]
            for k in range(8):
                here = pl.ds(k * TILE, TILE)
                solved = packed_product(pack_left(tri_ref[k, here, :]), pack_right(out_ref[here, :]))
                out_ref[here, :] = solved
                right = pack_right(solved)
                for i in range(k + 1, 8):
                    there = pl.ds(i * TILE, TILE)
                    out_ref[there, :] = out_ref[there, :] - packed_product(pack_left(tri_ref[k, there, :]), right)

    return pl.pallas_call(
        body,
        out_shape=jax.ShapeDtypeStruct(rhs.shape, F32),
        in_specs=[SM, VM, VM],
        out_specs=VM,
        compiler_params=PARAMS,
        name="block_solve",
    )(active, tri, rhs)


def residual(active, tri, rhs, x):
    def body(active, tri_ref, rhs_ref, x_ref, out_ref):
        @pl.when(active[0] == 1)
        def _():
            for k in range(8):
                right = pack_right(x_ref[pl.ds(k * TILE, TILE), :])
                for i in range(8):
                    there = pl.ds(i * TILE, TILE)
                    base = rhs_ref[there, :] if k == 0 else out_ref[there, :]
                    out_ref[there, :] = base - packed_product(pack_left(tri_ref[k, there, :]), right)

    return pl.pallas_call(
        body,
        out_shape=jax.ShapeDtypeStruct(rhs.shape, F32),
        in_specs=[SM, VM, VM, VM],
        out_specs=VM,
        compiler_params=PARAMS,
        name="block_residual",
    )(active, tri, rhs, x)


def arrange_body(factor_ref, out_ref):
    for c in range(16):
        for a in range(4):
            out_ref[c, pl.ds(64 * a, 64), :] = factor_ref[a, pl.ds(64 * c, 64), :]


def arrange(factor):
    return pl.pallas_call(
        arrange_body,
        out_shape=jax.ShapeDtypeStruct((16, 256, TILE), F32),
        in_specs=[VM],
        out_specs=VM,
        compiler_params=PARAMS,
        name="arrange_rows",
    )(factor)


def arrange_rhs_body(rhs_ref, out_ref):
    for n in range(16):
        out_ref[n, :, :] = rhs_ref[0, :, pl.ds(n % 8 * TILE, TILE)]


def arrange_rhs(rhs):
    return pl.pallas_call(
        arrange_rhs_body,
        grid=(1,),
        out_shape=jax.ShapeDtypeStruct((16, 64, TILE), F32),
        in_specs=[pl.BlockSpec((1, 64, 1024), lambda i: (0, 0, 0))],
        out_specs=pl.BlockSpec((16, 64, TILE), lambda i: (0, 0, 0)),
        compiler_params=PARAMS,
        name="arrange_rhs",
    )(rhs)


def prepare_body(info, left_ref, other_ref, high_ref, low_ref):
    for side, ref in enumerate((left_ref, other_ref)):
        rows = pl.ds(256 * side, 256)
        first = 8 * info[1] if side == 0 else 0
        for n in range(4):
            high, low = split(jnp.concatenate([ref[first + 2 * n], ref[first + 2 * n + 1]], 1))
            high_ref[n, rows, :] = high
            low_ref[n, rows, :] = low

    @pl.when(info[0] == 0)
    def _():
        for n in range(4):
            for side in range(2):
                high_ref[n, pl.ds(256 * side, 64), :] = jnp.zeros((64, 256), BF16)
                low_ref[n, pl.ds(256 * side, 64), :] = jnp.zeros((64, 256), BF16)


def prepare(info, left, other):
    return pl.pallas_call(
        prepare_body,
        out_shape=[jax.ShapeDtypeStruct((4, 512, 256), BF16)] * 2,
        in_specs=[SM, VM, VM],
        out_specs=[VM, VM],
        compiler_params=PARAMS,
        name="prepare_update",
    )(info, left, other)


def accumulate(info, sums, high, low, pieces, places, name):
    first = sums is None

    def body(info, high_ref, low_ref, *refs):
        out_ref = refs[-1]
        x, core, y, z, col = (info[k] for k in range(5))
        if first:
            out_ref[...] = jnp.zeros(out_ref.shape, F32)
        else:
            out_ref[...] = refs[0][...]
        for ref, (far, slot) in zip(refs[0 if first else 1 :], places):
            for n in range(ref.shape[0]):
                near = slot + n
                py = lax.rem(y + jnp.where(core == 0, far, near), 4)
                pz = lax.rem(z + jnp.where(core == 0, near, far), 4)
                upper = py // 2
                bit = jnp.where(upper == 0, py, 3 - py)
                cols = pl.ds(pl.multiple_of((4 * bit + pz) * TILE, TILE), TILE)
                total = None
                for h in range(2):
                    x_high, x_low = split(ref[n, pl.ds(256 * h, 256), :])
                    wide = mm(high_ref[2 * upper + h], jnp.concatenate([x_high, x_low], 1))
                    term = wide[:, :TILE] + (wide[:, TILE:] + mm(low_ref[2 * upper + h], x_high))
                    total = term if total is None else total + term
                out_ref[:, cols] = out_ref[:, cols] + total

                @pl.when((x == 0) & (col // 8 == upper))
                def _():
                    there = pl.ds(pl.multiple_of(lax.rem(col, 8) * 64, 64), 64)
                    here = pl.ds(0, 64)
                    out_ref[here, cols] = out_ref[here, cols] - ref[n, there, :]

    start = [] if first else [sums]
    return pl.pallas_call(
        body,
        out_shape=jax.ShapeDtypeStruct((512, 1024), F32),
        in_specs=[SM] + [VM] * (2 + len(start) + len(pieces)),
        out_specs=VM,
        input_output_aliases={} if first else {3: 0},
        compiler_params=PARAMS,
        name=name,
    )(info, high, low, *start, *pieces)


AXES = ROW + COL


def move(value, where):
    pairs = []
    for x in range(4):
        for core in range(2):
            for y in range(4):
                for z in range(4):
                    to = where(x, core, y, z)
                    if to is not None:
                        a, b, c, d = to
                        pairs.append((((x * 2 + core) * 4 + y) * 4 + z, ((a * 2 + b) * 4 + c % 4) * 4 + d % 4))
    return lax.ppermute(value, AXES, pairs)


def deal(first, second, core, yh, xi):
    solved = jnp.where(core == 0, first, second)
    lower = yh == 0
    here = jnp.where(lower, solved[:512], solved[512:])
    there = jnp.where(core == 0, solved[512:], solved[:512])
    got = move(there, lambda a, b, c, d: (0, b, 3 - c, d) if a == 0 and b == c // 2 else None)
    mine = jnp.where(core == yh, here, got)
    one = move(mine, lambda a, b, c, d: (1 if b == 0 else 3, b, c, d) if a == 0 else None)
    two = move(mine, lambda a, b, c, d: (3 if b == 0 else 1, b, c, d) if a == 0 else None)
    far = move(one, lambda a, b, c, d: (2, b, c, d) if a == (1 if b == 0 else 3) else None)
    return jnp.where(xi == 0, mine, one + two + far)


def ring(value, first):
    def along(step):
        def where(a, b, c, d):
            on_z = (b == 0) == first
            return (a, b, c, d + step) if on_z else (a, b, c + step, d)

        return where

    before = move(value, along(1))
    after = move(value, along(-1))
    cut = value.shape[0] // 2
    far_low = move(before[:cut], along(1))
    far_high = move(after[cut:], along(-1))
    return after, far_low, far_high, before


def shards(factor, cross_cov):
    xi, core = lax.axis_index("x"), lax.axis_index("core")
    yh, yl, z = lax.axis_index("yh"), lax.axis_index("yl"), lax.axis_index("z")
    row_id = 2 * xi + core
    col_id = 8 * yh + 4 * yl + z
    local = factor[:, 0]
    rhs = cross_cov[:, 0]

    diagonal = ((row_id == 0) & (yh == 0)) | ((row_id == 1) & (yh == 1))
    info = jnp.stack([diagonal.astype(jnp.int32), (4 * yl + z).astype(jnp.int32)])
    lead = invert_diagonal(info, local[0])

    tri = lax.all_gather(lead, ("yl", "z"), axis=0, tiled=False)

    columns = lax.all_to_all(arrange_rhs(rhs), COL, 0, 0, tiled=True).reshape(1024, TILE)

    def only(condition):
        return jnp.reshape(condition & (xi == 0), (1,)).astype(jnp.int32)

    first = solve(only((core == 0) & (yh == 0)), tri, columns)
    sent = move(first, lambda a, b, c, d: (0, 1, c, d) if (a, b) == (0, 0) and c < 2 else None)
    rest = residual(only((core == 1) & (yh == 0)), tri, columns, sent)
    second_rhs = move(rest, lambda a, b, c, d: (0, 1, 3 - c, d) if (a, b) == (0, 1) and c < 2 else None)
    by_rows, rest = lax.optimization_barrier((arrange(local), rest))
    left = lax.all_to_all(by_rows, COL, 0, 0, tiled=True)
    second = solve(only((core == 1) & (yh == 1)), tri, second_rhs)
    mine, left = lax.optimization_barrier((deal(first, second, core, yh, xi), left))

    def swap(value):
        return move(value, lambda a, b, c, d: (a, 1 - b, c, d))

    given = swap(lax.dynamic_slice_in_dim(left, 8 * (1 - core), 8, 0))
    info2 = jnp.stack([xi, core, 2 * yh + yl, z, col_id]).astype(jnp.int32)

    after, far_low, far_high, before = ring(mine, True)
    near = jnp.stack([mine, after, jnp.concatenate([far_low, far_high], 0), before])

    def along(step):
        return lambda a, b, c, d: (a, b, c + step, d) if b == 0 else (a, b, c, d + step)

    before, after = move(near, along(1)), move(near, along(-1))
    high, low = prepare(info2[:2], left, given)
    sums = accumulate(info2, None, high, low, [near], [(0, 0)], "update_near")
    before, after, sums = lax.optimization_barrier((before, after, sums))
    far_low, far_high = move(before[:2], along(1)), move(after[2:], along(-1))
    sums = accumulate(info2, sums, high, low, [after, before], [(1, 0), (3, 0)], "update_next")
    far_low, far_high, sums = lax.optimization_barrier((far_low, far_high, sums))
    sums = accumulate(info2, sums, high, low, [far_low, far_high], [(2, 0), (2, 2)], "update_far")

    replaced = (xi == 0) & (lax.broadcasted_iota(jnp.int32, (256, 1024), 0) < 64)
    base = jnp.where(replaced, 0.0, rhs.reshape(256, 1024))
    out = base - (sums[:256] + swap(sums[256:]))
    return out.reshape(4, 1, 64, 1024)


def solution(mesh):
    fine = Mesh(mesh.devices.reshape(4, 2, 2, 2, 4), ROW + COL)
    return jax.shard_map(
        shards,
        mesh=fine,
        in_specs=(P(None, ROW, None, COL), P(None, ROW, COL, None)),
        out_specs=P(None, ROW, COL, None),
        check_vma=False,
    )
```

```python
import jax
import jax.numpy as jnp
from jax import lax
from jax.experimental import pallas as pl
from jax.experimental.pallas import tpu as pltpu
from jax.sharding import Mesh, PartitionSpec as P

ROW = ("x", "core")
COL = ("yh", "yl", "z")
F32 = jnp.float32
BF16 = jnp.bfloat16
TILE = 128
PARAMS = pltpu.CompilerParams(vmem_limit_bytes=20 * 2**20)
VM = pl.BlockSpec(memory_space=pltpu.VMEM)
SM = pl.BlockSpec(memory_space=pltpu.SMEM)
FAR = pl.BlockSpec(memory_space=pltpu.HBM)


def split(value):
    high = value.astype(BF16)
    return high, (value - high.astype(F32)).astype(BF16)


def mm(a, b):
    return jnp.dot(a, b, preferred_element_type=F32)


def pack_left(value):
    return jnp.concatenate(split(value), 1)


def pack_right(value):
    high, low = split(value)
    return jnp.concatenate(
        [jnp.concatenate([high, low], 1), jnp.concatenate([high, jnp.zeros_like(low)], 1)], 0
    )


def packed_product(left, right):
    out = mm(left, right)
    return out[:, :TILE] + out[:, TILE:]


def invert_body(info, lead_ref, out_ref):
    out_ref[...] = lead_ref[...]

    @pl.when(info[0] == 1)
    def _():
        start = pl.multiple_of(info[1] * TILE, TILE)
        block = lead_ref[pl.ds(start, TILE), :]
        i = lax.broadcasted_iota(jnp.int32, (TILE, TILE), 0)
        j = lax.broadcasted_iota(jnp.int32, (TILE, TILE), 1)
        zero = jnp.zeros((TILE, TILE), F32)
        inverse = jnp.where(i == j, 1.0 / jnp.where(i == j, block, 1.0), zero)
        step = 1
        while step < TILE:
            below = ((i // (2 * step)) == (j // (2 * step))) & ((i // step) > (j // step))
            corner = jnp.where(below, block, zero)
            product = packed_product(pack_left(corner), pack_right(inverse))
            inverse = inverse - packed_product(pack_left(inverse), pack_right(product))
            step *= 2
        out_ref[pl.ds(start, TILE), :] = inverse


def invert_diagonal(info, lead):
    return pl.pallas_call(
        invert_body,
        out_shape=jax.ShapeDtypeStruct(lead.shape, F32),
        in_specs=[SM, VM],
        out_specs=VM,
        compiler_params=PARAMS,
        name="invert_diagonal",
    )(info, lead)


def substitute(tri_ref, rhs_ref, out_ref, ready):
    out_ref[...] = rhs_ref[...]
    for k in range(8):
        ready(k)
        here = pl.ds(k * TILE, TILE)
        solved = packed_product(tri_ref[k, here, :], pack_right(out_ref[here, :]))
        out_ref[here, :] = solved
        right = pack_right(solved)
        for i in range(k + 1, 8):
            there = pl.ds(i * TILE, TILE)
            out_ref[there, :] = out_ref[there, :] - packed_product(tri_ref[k, there, :], right)


def pack_pieces(info, refs, places, tri_ref):
    for ref, parts in zip(refs, places):
        for half, steps, start, to, rows in parts:
            half = {"own": info[0], "pair": 1 - info[0]}.get(half, half)
            k = 4 * half + lax.rem(info[1] + steps, 4)
            tri_ref[k, pl.ds(to, rows), :] = pack_left(ref[pl.ds(start, rows), :])


def solve_first(info, pieces, places, rhs):
    def body(info, *refs):
        rhs_ref, out_ref, tri_ref = refs[-3:]

        @pl.when(info[2] == 1)
        def _():
            pack_pieces(info, refs, places, tri_ref)
            substitute(tri_ref, rhs_ref, out_ref, lambda k: None)

    return pl.pallas_call(
        body,
        out_shape=jax.ShapeDtypeStruct(rhs.shape, F32),
        in_specs=[SM] + [VM] * (len(pieces) + 1),
        out_specs=VM,
        scratch_shapes=[pltpu.VMEM((8, 1024, 256), BF16)],
        compiler_params=PARAMS,
        name="solve_first",
    )(info, *pieces, rhs)


def residual_or_pack(info, pieces, places, rhs, x):
    count = len(pieces)

    def body(info, *refs):
        rhs_ref, x_ref, out_ref, tri_out, tri_ref, semaphore = refs[count:]

        @pl.when(info[2] == 1)
        def _():
            out_ref[...] = rhs_ref[...]
            for ref, parts in zip(refs, places):
                for half, steps, start, to, rows in parts:
                    half = {"own": info[0], "pair": 1 - info[0]}[half]
                    k = 4 * half + lax.rem(info[1] + steps, 4)
                    right = pack_right(x_ref[pl.ds(pl.multiple_of(k * TILE, TILE), TILE), :])
                    for n in range(0, rows, TILE):
                        there = pl.ds(to + n, TILE)
                        left = pack_left(ref[pl.ds(start + n, TILE), :])
                        out_ref[there, :] = out_ref[there, :] - packed_product(left, right)

        @pl.when(info[2] == 2)
        def _():
            pack_pieces(info, refs, places, tri_ref)
            copy = pltpu.make_async_copy(tri_ref, tri_out, semaphore)
            copy.start()
            copy.wait()

    return pl.pallas_call(
        body,
        out_shape=[jax.ShapeDtypeStruct(rhs.shape, F32), jax.ShapeDtypeStruct((8, 1024, 256), BF16)],
        in_specs=[SM] + [VM] * (count + 2),
        out_specs=[VM, FAR],
        scratch_shapes=[pltpu.VMEM((8, 1024, 256), BF16), pltpu.SemaphoreType.DMA],
        compiler_params=PARAMS,
        name="residual_or_pack",
    )(info, *pieces, rhs, x)


def solve_second(info, tri, rhs):
    def body(info, tri_in, rhs_ref, out_ref, tri_ref, semaphores):
        @pl.when(info[2] == 1)
        def _():
            copies = [pltpu.make_async_copy(tri_in.at[k], tri_ref.at[k], semaphores.at[k]) for k in range(8)]
            for copy in copies:
                copy.start()
            substitute(tri_ref, rhs_ref, out_ref, lambda k: copies[k].wait())

    return pl.pallas_call(
        body,
        out_shape=jax.ShapeDtypeStruct(rhs.shape, F32),
        in_specs=[SM, FAR, VM],
        out_specs=VM,
        scratch_shapes=[pltpu.VMEM((8, 1024, 256), BF16), pltpu.SemaphoreType.DMA((8,))],
        compiler_params=PARAMS,
        name="solve_second",
    )(info, tri, rhs)


def arrange_body(factor_ref, out_ref):
    for c in range(16):
        for a in range(4):
            out_ref[c, pl.ds(64 * a, 64), :] = factor_ref[a, pl.ds(64 * c, 64), :]


def arrange(factor):
    return pl.pallas_call(
        arrange_body,
        out_shape=jax.ShapeDtypeStruct((16, 256, TILE), F32),
        in_specs=[VM],
        out_specs=VM,
        compiler_params=PARAMS,
        name="arrange_rows",
    )(factor)


def arrange_rhs_body(info, rhs_ref, out_ref):
    for n in range(8):
        to = jnp.where(info[0] == 0, n, (n + 4) % 8)
        out_ref[to, :, :] = rhs_ref[0, :, pl.ds(n * TILE, TILE)]


def arrange_rhs(yh, rhs):
    return pl.pallas_call(
        arrange_rhs_body,
        grid=(1,),
        out_shape=jax.ShapeDtypeStruct((8, 64, TILE), F32),
        in_specs=[SM, pl.BlockSpec((1, 64, 1024), lambda i: (0, 0, 0))],
        out_specs=pl.BlockSpec((8, 64, TILE), lambda i: (0, 0, 0)),
        compiler_params=PARAMS,
        name="arrange_rhs",
    )(jnp.reshape(yh, (1,)).astype(jnp.int32), rhs)


def prepare_body(info, left_ref, other_ref, high_ref, low_ref):
    for side, ref in enumerate((left_ref, other_ref)):
        rows = pl.ds(256 * side, 256)
        first = 8 * info[1] if side == 0 else 0
        for n in range(4):
            high, low = split(jnp.concatenate([ref[first + 2 * n], ref[first + 2 * n + 1]], 1))
            high_ref[n, rows, :] = high
            low_ref[n, rows, :] = low

    @pl.when(info[0] == 0)
    def _():
        for n in range(4):
            for side in range(2):
                high_ref[n, pl.ds(256 * side, 64), :] = jnp.zeros((64, 256), BF16)
                low_ref[n, pl.ds(256 * side, 64), :] = jnp.zeros((64, 256), BF16)


def prepare(info, left, other):
    return pl.pallas_call(
        prepare_body,
        out_shape=[jax.ShapeDtypeStruct((4, 512, 256), BF16)] * 2,
        in_specs=[SM, VM, VM],
        out_specs=[VM, VM],
        compiler_params=PARAMS,
        name="prepare_update",
    )(info, left, other)


def accumulate(info, sums, high, low, pieces, places, name):
    first = sums is None

    def body(info, high_ref, low_ref, *refs):
        out_ref = refs[-1]
        x, core, y, z, col = (info[k] for k in range(5))
        if first:
            out_ref[...] = jnp.zeros(out_ref.shape, F32)
        else:
            out_ref[...] = refs[0][...]
        for ref, (far, slot) in zip(refs[0 if first else 1 :], places):
            for n in range(ref.shape[0]):
                near = slot + n
                py = lax.rem(y + jnp.where(core == 0, far, near), 4)
                pz = lax.rem(z + jnp.where(core == 0, near, far), 4)
                upper = py // 2
                bit = jnp.where(upper == 0, py, 3 - py)
                cols = pl.ds(pl.multiple_of((4 * bit + pz) * TILE, TILE), TILE)
                total = None
                for h in range(2):
                    x_high, x_low = split(ref[n, pl.ds(256 * h, 256), :])
                    wide = mm(high_ref[2 * upper + h], jnp.concatenate([x_high, x_low], 1))
                    term = wide[:, :TILE] + (wide[:, TILE:] + mm(low_ref[2 * upper + h], x_high))
                    total = term if total is None else total + term
                out_ref[:, cols] = out_ref[:, cols] + total

                @pl.when((x == 0) & (col // 8 == upper))
                def _():
                    there = pl.ds(pl.multiple_of(lax.rem(col, 8) * 64, 64), 64)
                    here = pl.ds(0, 64)
                    out_ref[here, cols] = out_ref[here, cols] - ref[n, there, :]

    start = [] if first else [sums]
    return pl.pallas_call(
        body,
        out_shape=jax.ShapeDtypeStruct((512, 1024), F32),
        in_specs=[SM] + [VM] * (2 + len(start) + len(pieces)),
        out_specs=VM,
        input_output_aliases={} if first else {3: 0},
        compiler_params=PARAMS,
        name=name,
    )(info, high, low, *start, *pieces)


AXES = ROW + COL


def move(value, where):
    pairs = []
    for x in range(4):
        for core in range(2):
            for y in range(4):
                for z in range(4):
                    to = where(x, core, y, z)
                    if to is not None:
                        a, b, c, d = to
                        pairs.append((((x * 2 + core) * 4 + y) * 4 + z, ((a * 2 + b) * 4 + c % 4) * 4 + d % 4))
    return lax.ppermute(value, AXES, pairs)


def deal(first, second, core, yh, xi):
    solved = jnp.where(core == 0, first, second)
    lower = yh == 0
    here = jnp.where(lower, solved[:512], solved[512:])
    there = jnp.where(core == 0, solved[512:], solved[:512])
    got = move(there, lambda a, b, c, d: (0, b, 3 - c, d) if a == 0 and b == c // 2 else None)
    mine = jnp.where(core == yh, here, got)
    one = move(mine, lambda a, b, c, d: (1 if b == 0 else 3, b, c, d) if a == 0 else None)
    two = move(mine, lambda a, b, c, d: (3 if b == 0 else 1, b, c, d) if a == 0 else None)
    far = move(one, lambda a, b, c, d: (2, b, c, d) if a == (1 if b == 0 else 3) else None)
    return jnp.where(xi == 0, mine, one + two + far)


def ring(value, first):
    def along(step):
        def where(a, b, c, d):
            on_z = (b == 0) == first
            return (a, b, c, d + step) if on_z else (a, b, c + step, d)

        return where

    before = move(value, along(1))
    after = move(value, along(-1))
    cut = value.shape[0] // 2
    far_low = move(before[:cut], along(1))
    far_high = move(after[cut:], along(-1))
    return after, far_low, far_high, before


def gather(lead, half, core, yl):
    def holds(a, b, c):
        return a == 0 and (b == 1 or c < 2)

    def step(b_on_z, amount):
        def where(a, b, c, d):
            if not holds(a, b, c):
                return None
            return (a, b, c, d + amount) if b == b_on_z else (a, b, c + 1 - 2 * (c % 2), d)

        return where

    def only(b_only, amount):
        return lambda a, b, c, d: (a, b, c, d + amount) if holds(a, b, c) and b == b_only else None

    mixed = move(lead, step(1, 1))
    after = move(lead, only(1, -1))
    swapped = move(lead, lambda a, b, c, d: (a, b, c + 1 - 2 * (c % 2), d) if holds(a, b, c) and b == 1 else None)
    mixed, swapped, half = lax.optimization_barrier((mixed, swapped, half))
    other_half = move(half, lambda a, b, c, d: (0, b, 3 - c, d) if a == 0 and c >= 2 else None)
    far_low = move(mixed[:512], only(1, 1))
    far_high = move(after[512:], only(1, -1))

    full = jnp.where(yl == 0, lead, mixed)
    lower = jnp.where(yl == 0, mixed[512:], lead[512:])
    zero = core == 0
    first = jnp.concatenate([jnp.where(zero, full, mixed), jnp.where(zero, lower, far_low)], 0)
    second = jnp.concatenate([jnp.where(zero, full, after), jnp.where(zero, lower, far_high)], 0)
    got_first = move(first, step(0, 1))
    got_second = move(second, step(0, -1))
    got_first, other_half = lax.optimization_barrier((got_first, other_half))
    end_low = move(got_first[:768], only(0, 1))
    end_high = move(got_second[768:], only(0, -1))

    corner_pieces = [first, got_second, got_first, end_low, end_high]
    corner_places = [[(0, n, 0, 0, 1024), (1, n, 1024, 512, 512)] for n in (0, 1, 3)]
    corner_places += [[(0, 2, 0, 0, 768)], [(0, 2, 0, 768, 256), (1, 2, 256, 512, 512)]]
    lower_pieces = [lead, swapped, first, second, got_first, got_second]
    lower_places = [[("own", 0, 0, 0, 1024)], [("pair", 0, 0, 0, 1024)]]
    for group in ("own", "pair"):
        lower_places.append([(group, 3, 0, 0, 1024), (group, 2, 1024, 0, 512)])
        lower_places.append([(group, 1, 0, 0, 1024), (group, 2, 1024, 512, 512)])
    return (corner_pieces, corner_places), (lower_pieces, lower_places), jnp.concatenate([half, other_half], 0)


def shards(factor, cross_cov):
    xi, core = lax.axis_index("x"), lax.axis_index("core")
    yh, yl, z = lax.axis_index("yh"), lax.axis_index("yl"), lax.axis_index("z")
    row_id = 2 * xi + core
    col_id = 8 * yh + 4 * yl + z
    local = factor[:, 0]
    rhs = cross_cov[:, 0]

    diagonal = ((row_id == 0) & (yh == 0)) | ((row_id == 1) & (yh == 1))
    info = jnp.stack([diagonal.astype(jnp.int32), (4 * yl + z).astype(jnp.int32)])
    lead = invert_diagonal(info, local[0])

    half = lax.all_to_all(arrange_rhs(yh, rhs), ("yl", "z"), 0, 0, tiled=True).reshape(512, TILE)
    upper_left, lower_row, columns = gather(lead, half, core, yl)

    def place(what):
        return jnp.stack([yl, z, jnp.where(xi == 0, what, 0)]).astype(jnp.int32)

    first = solve_first(place((core == 0) & (yh == 0)), *upper_left, columns)
    sent = move(first, lambda a, b, c, d: (0, 1, c, d) if (a, b) == (0, 0) and c < 2 else None)
    rest, tri = residual_or_pack(place(core * (1 + yh)), *lower_row, columns, sent)
    second_rhs = move(rest, lambda a, b, c, d: (0, 1, 3 - c, d) if (a, b) == (0, 1) and c < 2 else None)
    by_rows, rest = lax.optimization_barrier((arrange(local), rest))
    left = lax.all_to_all(by_rows, COL, 0, 0, tiled=True)
    second = solve_second(place((core == 1) & (yh == 1)), tri, second_rhs)
    mine, left = lax.optimization_barrier((deal(first, second, core, yh, xi), left))

    def swap(value):
        return move(value, lambda a, b, c, d: (a, 1 - b, c, d))

    given = swap(lax.dynamic_slice_in_dim(left, 8 * (1 - core), 8, 0))
    info2 = jnp.stack([xi, core, 2 * yh + yl, z, col_id]).astype(jnp.int32)

    after, far_low, far_high, before = ring(mine, True)
    near = jnp.stack([mine, after, jnp.concatenate([far_low, far_high], 0), before])

    def along(step):
        return lambda a, b, c, d: (a, b, c + step, d) if b == 0 else (a, b, c, d + step)

    before, after = move(near, along(1)), move(near, along(-1))
    high, low = prepare(info2[:2], left, given)
    sums = accumulate(info2, None, high, low, [near], [(0, 0)], "update_near")
    before, after, sums = lax.optimization_barrier((before, after, sums))
    far_low, far_high = move(before[:2], along(1)), move(after[2:], along(-1))
    sums = accumulate(info2, sums, high, low, [after, before], [(1, 0), (3, 0)], "update_next")
    far_low, far_high, sums = lax.optimization_barrier((far_low, far_high, sums))
    sums = accumulate(info2, sums, high, low, [far_low, far_high], [(2, 0), (2, 2)], "update_far")

    replaced = (xi == 0) & (lax.broadcasted_iota(jnp.int32, (256, 1024), 0) < 64)
    base = jnp.where(replaced, 0.0, rhs.reshape(256, 1024))
    out = base - (sums[:256] + swap(sums[256:]))
    return out.reshape(4, 1, 64, 1024)


def solution(mesh):
    fine = Mesh(mesh.devices.reshape(4, 2, 2, 2, 4), ROW + COL)
    return jax.shard_map(
        shards,
        mesh=fine,
        in_specs=(P(None, ROW, None, COL), P(None, ROW, COL, None)),
        out_specs=P(None, ROW, COL, None),
        check_vma=False,
    )
```

```python
import jax
import jax.numpy as jnp
from jax import lax
from jax.experimental import pallas as pl
from jax.experimental.pallas import tpu as pltpu
from jax.sharding import Mesh, PartitionSpec as P

ROW = ("x", "core")
COL = ("yh", "yl", "z")
F32 = jnp.float32
BF16 = jnp.bfloat16
TILE = 128
STORE = 112
PARAMS = pltpu.CompilerParams(vmem_limit_bytes=20 * 2**20)
VM = pl.BlockSpec(memory_space=pltpu.VMEM)
SM = pl.BlockSpec(memory_space=pltpu.SMEM)
FAR = pl.BlockSpec(memory_space=pltpu.HBM)


def split(value):
    high = value.astype(BF16)
    return high, (value - high.astype(F32)).astype(BF16)


def mm(a, b):
    return jnp.dot(a, b, preferred_element_type=F32)


def pack_left(value):
    return jnp.concatenate(split(value), 1)


def pack_right(value):
    high, low = split(value)
    return jnp.concatenate(
        [jnp.concatenate([high, low], 1), jnp.concatenate([high, jnp.zeros_like(low)], 1)], 0
    )


def packed_product(left, right):
    out = mm(left, right)
    return out[:, :TILE] + out[:, TILE:]


def invert_body(info, lead_ref, out_ref):
    out_ref[...] = lead_ref[...]

    @pl.when(info[0] == 1)
    def _():
        start = pl.multiple_of(info[1] * TILE, TILE)
        block = lead_ref[pl.ds(start, TILE), :]
        i = lax.broadcasted_iota(jnp.int32, (TILE, TILE), 0)
        j = lax.broadcasted_iota(jnp.int32, (TILE, TILE), 1)
        zero = jnp.zeros((TILE, TILE), F32)
        inverse = jnp.where(i == j, 1.0 / jnp.where(i == j, block, 1.0), zero)
        step = 1
        while step < TILE:
            below = ((i // (2 * step)) == (j // (2 * step))) & ((i // step) > (j // step))
            corner = jnp.where(below, block, zero)
            product = packed_product(pack_left(corner), pack_right(inverse))
            inverse = inverse - packed_product(pack_left(inverse), pack_right(product))
            step *= 2
        out_ref[pl.ds(start, TILE), :] = inverse


def invert_diagonal(info, lead):
    return pl.pallas_call(
        invert_body,
        out_shape=jax.ShapeDtypeStruct(lead.shape, F32),
        in_specs=[SM, VM],
        out_specs=VM,
        compiler_params=PARAMS,
        name="invert_diagonal",
    )(info, lead)


def substitute(tri_ref, rhs_ref, out_ref, ready):
    out_ref[...] = rhs_ref[...]
    for k in range(8):
        ready(k)
        here = pl.ds(k * TILE, TILE)
        solved = packed_product(tri_ref[k, here, :], pack_right(out_ref[here, :]))
        out_ref[here, :] = solved
        right = pack_right(solved)
        for i in range(k + 1, 8):
            there = pl.ds(i * TILE, TILE)
            out_ref[there, :] = out_ref[there, :] - packed_product(tri_ref[k, there, :], right)


def pack_pieces(info, refs, places, tri_ref):
    for ref, parts in zip(refs, places):
        for half, steps, start, to, rows in parts:
            half = {"own": info[0], "pair": 1 - info[0]}.get(half, half)
            k = 4 * half + lax.rem(info[1] + steps, 4)
            tri_ref[k, pl.ds(to, rows), :] = pack_left(ref[pl.ds(start, rows), :])


def solve_first(info, pieces, places, rhs):
    def body(info, *refs):
        rhs_ref, out_ref, tri_ref = refs[-3:]

        @pl.when(info[2] == 1)
        def _():
            pack_pieces(info, refs, places, tri_ref)
            substitute(tri_ref, rhs_ref, out_ref, lambda k: None)

    return pl.pallas_call(
        body,
        out_shape=jax.ShapeDtypeStruct(rhs.shape, F32),
        in_specs=[SM] + [VM] * (len(pieces) + 1),
        out_specs=VM,
        scratch_shapes=[pltpu.VMEM((8, 1024, 256), BF16)],
        compiler_params=PARAMS,
        name="solve_first",
    )(info, *pieces, rhs)


def residual_or_pack(info, pieces, places, rhs, x):
    count = len(pieces)

    def body(info, *refs):
        rhs_ref, x_ref, out_ref, tri_out, tri_ref, semaphore = refs[count:]

        @pl.when(info[2] == 1)
        def _():
            out_ref[...] = rhs_ref[...]
            for ref, parts in zip(refs, places):
                for half, steps, start, to, rows in parts:
                    half = {"own": info[0], "pair": 1 - info[0]}[half]
                    k = 4 * half + lax.rem(info[1] + steps, 4)
                    right = pack_right(x_ref[pl.ds(pl.multiple_of(k * TILE, TILE), TILE), :])
                    for n in range(0, rows, TILE):
                        there = pl.ds(to + n, TILE)
                        left = pack_left(ref[pl.ds(start + n, TILE), :])
                        out_ref[there, :] = out_ref[there, :] - packed_product(left, right)

        @pl.when(info[2] == 2)
        def _():
            pack_pieces(info, refs, places, tri_ref)
            copy = pltpu.make_async_copy(tri_ref, tri_out.at[pl.ds(0, 8)], semaphore)
            copy.start()
            copy.wait()

    return pl.pallas_call(
        body,
        out_shape=[jax.ShapeDtypeStruct(rhs.shape, F32), jax.ShapeDtypeStruct((STORE, 1024, 256), BF16)],
        in_specs=[SM] + [VM] * (count + 2),
        out_specs=[VM, FAR],
        scratch_shapes=[pltpu.VMEM((8, 1024, 256), BF16), pltpu.SemaphoreType.DMA],
        compiler_params=PARAMS,
        name="residual_or_pack",
    )(info, *pieces, rhs, x)


def solve_second(info, tri, rhs):
    def body(info, tri_in, rhs_ref, out_ref, tri_ref, semaphores):
        @pl.when(info[2] == 1)
        def _():
            copies = [pltpu.make_async_copy(tri_in.at[k], tri_ref.at[k], semaphores.at[k]) for k in range(8)]
            for copy in copies:
                copy.start()
            substitute(tri_ref, rhs_ref, out_ref, lambda k: copies[k].wait())

    return pl.pallas_call(
        body,
        out_shape=jax.ShapeDtypeStruct(rhs.shape, F32),
        in_specs=[SM, FAR, VM],
        out_specs=VM,
        scratch_shapes=[pltpu.VMEM((8, 1024, 256), BF16), pltpu.SemaphoreType.DMA((8,))],
        compiler_params=PARAMS,
        name="solve_second",
    )(info, tri, rhs)


def arrange_body(factor_ref, out_ref):
    for c in range(16):
        for a in range(4):
            out_ref[c, pl.ds(64 * a, 64), :] = factor_ref[a, pl.ds(64 * c, 64), :]


def arrange(factor):
    return pl.pallas_call(
        arrange_body,
        out_shape=jax.ShapeDtypeStruct((16, 256, TILE), F32),
        in_specs=[VM],
        out_specs=VM,
        compiler_params=PARAMS,
        name="arrange_rows",
    )(factor)


def arrange_rhs_body(info, rhs_ref, out_ref):
    for n in range(8):
        to = jnp.where(info[0] == 0, n, (n + 4) % 8)
        out_ref[to, :, :] = rhs_ref[0, :, pl.ds(n * TILE, TILE)]


def arrange_rhs(yh, rhs):
    return pl.pallas_call(
        arrange_rhs_body,
        grid=(1,),
        out_shape=jax.ShapeDtypeStruct((8, 64, TILE), F32),
        in_specs=[SM, pl.BlockSpec((1, 64, 1024), lambda i: (0, 0, 0))],
        out_specs=pl.BlockSpec((8, 64, TILE), lambda i: (0, 0, 0)),
        compiler_params=PARAMS,
        name="arrange_rhs",
    )(jnp.reshape(yh, (1,)).astype(jnp.int32), rhs)


def prepare_body(info, left_ref, other_ref, high_ref, low_ref):
    for side, ref in enumerate((left_ref, other_ref)):
        rows = pl.ds(256 * side, 256)
        first = 8 * info[1] if side == 0 else 0
        for n in range(4):
            high, low = split(jnp.concatenate([ref[first + 2 * n], ref[first + 2 * n + 1]], 1))
            high_ref[n, rows, :] = high
            low_ref[n, rows, :] = low

    @pl.when(info[0] == 0)
    def _():
        for n in range(4):
            for side in range(2):
                high_ref[n, pl.ds(256 * side, 64), :] = jnp.zeros((64, 256), BF16)
                low_ref[n, pl.ds(256 * side, 64), :] = jnp.zeros((64, 256), BF16)


def prepare(info, left, other):
    return pl.pallas_call(
        prepare_body,
        out_shape=[jax.ShapeDtypeStruct((4, 512, 256), BF16)] * 2,
        in_specs=[SM, VM, VM],
        out_specs=[VM, VM],
        compiler_params=PARAMS,
        name="prepare_update",
    )(info, left, other)


def accumulate(info, sums, high, low, pieces, places, name):
    first = sums is None

    def body(info, high_ref, low_ref, *refs):
        out_ref = refs[-1]
        x, core, y, z, col = (info[k] for k in range(5))
        if first:
            out_ref[...] = jnp.zeros(out_ref.shape, F32)
        else:
            out_ref[...] = refs[0][...]
        for ref, (far, slot) in zip(refs[0 if first else 1 :], places):
            for n in range(ref.shape[0]):
                near = slot + n
                py = lax.rem(y + jnp.where(core == 0, far, near), 4)
                pz = lax.rem(z + jnp.where(core == 0, near, far), 4)
                upper = py // 2
                bit = jnp.where(upper == 0, py, 3 - py)
                cols = pl.ds(pl.multiple_of((4 * bit + pz) * TILE, TILE), TILE)
                total = None
                for h in range(2):
                    x_high, x_low = split(ref[n, pl.ds(256 * h, 256), :])
                    wide = mm(high_ref[2 * upper + h], jnp.concatenate([x_high, x_low], 1))
                    term = wide[:, :TILE] + (wide[:, TILE:] + mm(low_ref[2 * upper + h], x_high))
                    total = term if total is None else total + term
                out_ref[:, cols] = out_ref[:, cols] + total

                @pl.when((x == 0) & (col // 8 == upper))
                def _():
                    there = pl.ds(pl.multiple_of(lax.rem(col, 8) * 64, 64), 64)
                    here = pl.ds(0, 64)
                    out_ref[here, cols] = out_ref[here, cols] - ref[n, there, :]

    start = [] if first else [sums]
    return pl.pallas_call(
        body,
        out_shape=jax.ShapeDtypeStruct((512, 1024), F32),
        in_specs=[SM] + [VM] * (2 + len(start) + len(pieces)),
        out_specs=VM,
        input_output_aliases={} if first else {3: 0},
        compiler_params=PARAMS,
        name=name,
    )(info, high, low, *start, *pieces)


AXES = ROW + COL


def move(value, where):
    pairs = []
    for x in range(4):
        for core in range(2):
            for y in range(4):
                for z in range(4):
                    to = where(x, core, y, z)
                    if to is not None:
                        a, b, c, d = to
                        pairs.append((((x * 2 + core) * 4 + y) * 4 + z, ((a * 2 + b) * 4 + c % 4) * 4 + d % 4))
    return lax.ppermute(value, AXES, pairs)


def deal(first, second, core, yh, xi, by_rows):
    solved = jnp.where(core == 0, first, second)
    lower = yh == 0
    here = jnp.where(lower, solved[:512], solved[512:])
    there = jnp.where(core == 0, solved[512:], solved[:512])
    got = move(there, lambda a, b, c, d: (0, b, 3 - c, d) if a == 0 and b == c // 2 else None)
    got, by_rows = lax.optimization_barrier((got, by_rows))
    left = lax.all_to_all(by_rows, COL, 0, 0, tiled=True)
    mine = jnp.where(core == yh, here, got)
    one = move(mine, lambda a, b, c, d: (1 if b == 0 else 3, b, c, d) if a == 0 else None)
    two = move(mine, lambda a, b, c, d: (3 if b == 0 else 1, b, c, d) if a == 0 else None)
    far = move(one, lambda a, b, c, d: (2, b, c, d) if a == (1 if b == 0 else 3) else None)
    return jnp.where(xi == 0, mine, one + two + far), left


def ring(value, first):
    def along(step):
        def where(a, b, c, d):
            on_z = (b == 0) == first
            return (a, b, c, d + step) if on_z else (a, b, c + step, d)

        return where

    before = move(value, along(1))
    after = move(value, along(-1))
    cut = value.shape[0] // 2
    far_low = move(before[:cut], along(1))
    far_high = move(after[cut:], along(-1))
    return after, far_low, far_high, before


def gather(lead, half, core, yl):
    def holds(a, b, c):
        return a == 0 and (b == 1 or c < 2)

    def step(b_on_z, amount):
        def where(a, b, c, d):
            if not holds(a, b, c):
                return None
            return (a, b, c, d + amount) if b == b_on_z else (a, b, c + 1 - 2 * (c % 2), d)

        return where

    def only(b_only, amount):
        return lambda a, b, c, d: (a, b, c, d + amount) if holds(a, b, c) and b == b_only else None

    mixed = move(lead, step(1, 1))
    after = move(lead, only(1, -1))
    swapped = move(lead, lambda a, b, c, d: (a, b, c + 1 - 2 * (c % 2), d) if holds(a, b, c) and b == 1 else None)
    mixed, swapped, half = lax.optimization_barrier((mixed, swapped, half))
    other_half = move(half, lambda a, b, c, d: (0, b, 3 - c, d) if a == 0 and c >= 2 else None)
    far_low = move(mixed[:512], only(1, 1))
    far_high = move(after[512:], only(1, -1))

    full = jnp.where(yl == 0, lead, mixed)
    lower = jnp.where(yl == 0, mixed[512:], lead[512:])
    zero = core == 0
    first = jnp.concatenate([jnp.where(zero, full, mixed), jnp.where(zero, lower, far_low)], 0)
    second = jnp.concatenate([jnp.where(zero, full, after), jnp.where(zero, lower, far_high)], 0)
    got_first = move(first, step(0, 1))
    got_second = move(second, step(0, -1))
    got_first, other_half = lax.optimization_barrier((got_first, other_half))
    end_low = move(got_first[:768], only(0, 1))
    end_high = move(got_second[768:], only(0, -1))

    corner_pieces = [first, got_second, got_first, end_low, end_high]
    corner_places = [[(0, n, 0, 0, 1024), (1, n, 1024, 512, 512)] for n in (0, 1, 3)]
    corner_places += [[(0, 2, 0, 0, 768)], [(0, 2, 0, 768, 256), (1, 2, 256, 512, 512)]]
    lower_pieces = [lead, swapped, first, second, got_first, got_second]
    lower_places = [[("own", 0, 0, 0, 1024)], [("pair", 0, 0, 0, 1024)]]
    for group in ("own", "pair"):
        lower_places.append([(group, 3, 0, 0, 1024), (group, 2, 1024, 0, 512)])
        lower_places.append([(group, 1, 0, 0, 1024), (group, 2, 1024, 512, 512)])
    return (corner_pieces, corner_places), (lower_pieces, lower_places), jnp.concatenate([half, other_half], 0)


def shards(factor, cross_cov):
    xi, core = lax.axis_index("x"), lax.axis_index("core")
    yh, yl, z = lax.axis_index("yh"), lax.axis_index("yl"), lax.axis_index("z")
    row_id = 2 * xi + core
    col_id = 8 * yh + 4 * yl + z
    local = factor[:, 0]
    rhs = cross_cov[:, 0]

    diagonal = ((row_id == 0) & (yh == 0)) | ((row_id == 1) & (yh == 1))
    info = jnp.stack([diagonal.astype(jnp.int32), (4 * yl + z).astype(jnp.int32)])
    lead = invert_diagonal(info, local[0])

    half = lax.all_to_all(arrange_rhs(yh, rhs), ("yl", "z"), 0, 0, tiled=True).reshape(512, TILE)
    upper_left, lower_row, columns = gather(lead, half, core, yl)

    def place(what):
        return jnp.stack([yl, z, jnp.where(xi == 0, what, 0)]).astype(jnp.int32)

    first = solve_first(place((core == 0) & (yh == 0)), *upper_left, columns)
    sent = move(first, lambda a, b, c, d: (0, 1, c, d) if (a, b) == (0, 0) and c < 2 else None)
    rest, tri = residual_or_pack(place(core * (1 + yh)), *lower_row, columns, sent)
    second_rhs = move(rest, lambda a, b, c, d: (0, 1, 3 - c, d) if (a, b) == (0, 1) and c < 2 else None)
    second = solve_second(place((core == 1) & (yh == 1)), tri, second_rhs)
    mine, left = deal(first, second, core, yh, xi, arrange(local))

    def swap(value):
        return move(value, lambda a, b, c, d: (a, 1 - b, c, d))

    info2 = jnp.stack([xi, core, 2 * yh + yl, z, col_id]).astype(jnp.int32)

    after, far_low, far_high, before = ring(mine, True)
    low = jnp.stack([mine, after])
    high = jnp.stack([jnp.concatenate([far_low, far_high], 0), before])

    left, _ = lax.optimization_barrier((left, high))
    given = swap(lax.dynamic_slice_in_dim(left, 8 * (1 - core), 8, 0))

    def along(step):
        return lambda a, b, c, d: (a, b, c + step, d) if b == 0 else (a, b, c, d + step)

    low_before, low_after = move(low, along(1)), move(low, along(-1))
    high_after, high_before = move(high, along(-1)), move(high, along(1))
    parts = prepare(info2[:2], left, given)

    def add(sums, pieces, places, name):
        return accumulate(info2, sums, *parts, pieces, places, name)

    sums = add(None, [low, high], [(0, 0), (0, 2)], "update_near")
    low_before, high_after, sums = lax.optimization_barrier((low_before, high_after, sums))
    far_low, far_high = move(low_before, along(1)), move(high_after, along(-1))
    sums = add(
        sums, [low_after, high_after, low_before, high_before], [(1, 0), (1, 2), (3, 0), (3, 2)], "update_next"
    )
    far_low, far_high, sums = lax.optimization_barrier((far_low, far_high, sums))
    sums = add(sums, [far_low, far_high], [(2, 0), (2, 2)], "update_far")

    replaced = (xi == 0) & (lax.broadcasted_iota(jnp.int32, (256, 1024), 0) < 64)
    base = jnp.where(replaced, 0.0, rhs.reshape(256, 1024))
    out = base - (sums[:256] + swap(sums[256:]))
    return out.reshape(4, 1, 64, 1024)


def solution(mesh):
    fine = Mesh(mesh.devices.reshape(4, 2, 2, 2, 4), ROW + COL)
    return jax.shard_map(
        shards,
        mesh=fine,
        in_specs=(P(None, ROW, None, COL), P(None, ROW, COL, None)),
        out_specs=P(None, ROW, COL, None),
        check_vma=False,
    )
```

```python
import jax
import jax.numpy as jnp
from jax import lax
from jax.experimental import pallas as pl
from jax.experimental.pallas import tpu as pltpu
from jax.sharding import Mesh, PartitionSpec as P

ROW = ("x", "core")
COL = ("yh", "yl", "z")
F32 = jnp.float32
BF16 = jnp.bfloat16
TILE = 128
STORE = 112
PARAMS = pltpu.CompilerParams(vmem_limit_bytes=20 * 2**20)
VM = pl.BlockSpec(memory_space=pltpu.VMEM)
SM = pl.BlockSpec(memory_space=pltpu.SMEM)
FAR = pl.BlockSpec(memory_space=pltpu.HBM)


def split(value):
    high = value.astype(BF16)
    return high, (value - high.astype(F32)).astype(BF16)


def mm(a, b):
    return jnp.dot(a, b, preferred_element_type=F32)


def pack_left(value):
    return jnp.concatenate(split(value), 1)


def pack_right(value):
    high, low = split(value)
    return jnp.concatenate(
        [jnp.concatenate([high, low], 1), jnp.concatenate([high, jnp.zeros_like(low)], 1)], 0
    )


def packed_product(left, right):
    out = mm(left, right)
    return out[:, :TILE] + out[:, TILE:]


def invert_body(info, lead_ref, out_ref):
    out_ref[...] = lead_ref[...]

    @pl.when(info[0] == 1)
    def _():
        start = pl.multiple_of(info[1] * TILE, TILE)
        block = lead_ref[pl.ds(start, TILE), :]
        i = lax.broadcasted_iota(jnp.int32, (TILE, TILE), 0)
        j = lax.broadcasted_iota(jnp.int32, (TILE, TILE), 1)
        zero = jnp.zeros((TILE, TILE), F32)
        inverse = jnp.where(i == j, 1.0 / jnp.where(i == j, block, 1.0), zero)
        step = 1
        while step < TILE:
            below = ((i // (2 * step)) == (j // (2 * step))) & ((i // step) > (j // step))
            corner = jnp.where(below, block, zero)
            product = packed_product(pack_left(corner), pack_right(inverse))
            inverse = inverse - packed_product(pack_left(inverse), pack_right(product))
            step *= 2
        out_ref[pl.ds(start, TILE), :] = inverse


def invert_diagonal(info, lead):
    return pl.pallas_call(
        invert_body,
        out_shape=jax.ShapeDtypeStruct(lead.shape, F32),
        in_specs=[SM, VM],
        out_specs=VM,
        compiler_params=PARAMS,
        name="invert_diagonal",
    )(info, lead)


def substitute(tri_ref, rhs_ref, out_ref, ready):
    out_ref[...] = rhs_ref[...]
    for k in range(8):
        ready(k)
        here = pl.ds(k * TILE, TILE)
        solved = packed_product(tri_ref[k, here, :], pack_right(out_ref[here, :]))
        out_ref[here, :] = solved
        right = pack_right(solved)
        for i in range(k + 1, 8):
            there = pl.ds(i * TILE, TILE)
            out_ref[there, :] = out_ref[there, :] - packed_product(tri_ref[k, there, :], right)


def pack_pieces(info, refs, places, tri_ref):
    for ref, parts in zip(refs, places):
        for half, steps, start, to, rows in parts:
            half = {"own": info[0], "pair": 1 - info[0]}.get(half, half)
            k = 4 * half + lax.rem(info[1] + steps, 4)
            tri_ref[k, pl.ds(to, rows), :] = pack_left(ref[pl.ds(start, rows), :])


def solve_first(info, pieces, places, rhs):
    def body(info, *refs):
        rhs_ref, out_ref, tri_ref = refs[-3:]

        @pl.when(info[2] == 1)
        def _():
            pack_pieces(info, refs, places, tri_ref)
            substitute(tri_ref, rhs_ref, out_ref, lambda k: None)

    return pl.pallas_call(
        body,
        out_shape=jax.ShapeDtypeStruct(rhs.shape, F32),
        in_specs=[SM] + [VM] * (len(pieces) + 1),
        out_specs=VM,
        scratch_shapes=[pltpu.VMEM((8, 1024, 256), BF16)],
        compiler_params=PARAMS,
        name="solve_first",
    )(info, *pieces, rhs)


def residual_or_pack(info, pieces, places, rhs, x):
    count = len(pieces)

    def body(info, *refs):
        rhs_ref, x_ref, out_ref, tri_out, tri_ref, semaphore = refs[count:]

        @pl.when(info[2] == 1)
        def _():
            out_ref[...] = rhs_ref[...]
            for ref, parts in zip(refs, places):
                for half, steps, start, to, rows in parts:
                    half = {"own": info[0], "pair": 1 - info[0]}[half]
                    k = 4 * half + lax.rem(info[1] + steps, 4)
                    right = pack_right(x_ref[pl.ds(pl.multiple_of(k * TILE, TILE), TILE), :])
                    for n in range(0, rows, TILE):
                        there = pl.ds(to + n, TILE)
                        left = pack_left(ref[pl.ds(start + n, TILE), :])
                        out_ref[there, :] = out_ref[there, :] - packed_product(left, right)

        @pl.when(info[2] == 2)
        def _():
            pack_pieces(info, refs, places, tri_ref)
            copy = pltpu.make_async_copy(tri_ref, tri_out.at[pl.ds(0, 8)], semaphore)
            copy.start()
            copy.wait()

    return pl.pallas_call(
        body,
        out_shape=[jax.ShapeDtypeStruct(rhs.shape, F32), jax.ShapeDtypeStruct((STORE, 1024, 256), BF16)],
        in_specs=[SM] + [VM] * (count + 2),
        out_specs=[VM, FAR],
        scratch_shapes=[pltpu.VMEM((8, 1024, 256), BF16), pltpu.SemaphoreType.DMA],
        compiler_params=PARAMS,
        name="residual_or_pack",
    )(info, *pieces, rhs, x)


def solve_second(info, tri, rhs):
    def body(info, tri_in, rhs_ref, out_ref, tri_ref, semaphores):
        @pl.when(info[2] == 1)
        def _():
            copies = [pltpu.make_async_copy(tri_in.at[k], tri_ref.at[k], semaphores.at[k]) for k in range(8)]
            for copy in copies:
                copy.start()
            substitute(tri_ref, rhs_ref, out_ref, lambda k: copies[k].wait())

    return pl.pallas_call(
        body,
        out_shape=jax.ShapeDtypeStruct(rhs.shape, F32),
        in_specs=[SM, FAR, VM],
        out_specs=VM,
        scratch_shapes=[pltpu.VMEM((8, 1024, 256), BF16), pltpu.SemaphoreType.DMA((8,))],
        compiler_params=PARAMS,
        name="solve_second",
    )(info, tri, rhs)


def arrange_body(factor_ref, out_ref):
    for c in range(16):
        for a in range(4):
            out_ref[c, pl.ds(64 * a, 64), :] = factor_ref[a, pl.ds(64 * c, 64), :]


def arrange(factor):
    return pl.pallas_call(
        arrange_body,
        out_shape=jax.ShapeDtypeStruct((16, 256, TILE), F32),
        in_specs=[VM],
        out_specs=VM,
        compiler_params=PARAMS,
        name="arrange_rows",
    )(factor)


def arrange_rhs_body(info, rhs_ref, out_ref):
    for n in range(8):
        to = jnp.where(info[0] == 0, n, (n + 4) % 8)
        out_ref[to, :, :] = rhs_ref[0, :, pl.ds(n * TILE, TILE)]


def arrange_rhs(yh, rhs):
    return pl.pallas_call(
        arrange_rhs_body,
        grid=(1,),
        out_shape=jax.ShapeDtypeStruct((8, 64, TILE), F32),
        in_specs=[SM, pl.BlockSpec((1, 64, 1024), lambda i: (0, 0, 0))],
        out_specs=pl.BlockSpec((8, 64, TILE), lambda i: (0, 0, 0)),
        compiler_params=PARAMS,
        name="arrange_rhs",
    )(jnp.reshape(yh, (1,)).astype(jnp.int32), rhs)


def prepare_body(info, left_ref, other_ref, high_ref, low_ref):
    for side, ref in enumerate((left_ref, other_ref)):
        rows = pl.ds(256 * side, 256)
        first = 8 * info[1] if side == 0 else 0
        for n in range(4):
            high, low = split(jnp.concatenate([ref[first + 2 * n], ref[first + 2 * n + 1]], 1))
            high_ref[n, rows, :] = high
            low_ref[n, rows, :] = low

    @pl.when(info[0] == 0)
    def _():
        for n in range(4):
            for side in range(2):
                high_ref[n, pl.ds(256 * side, 64), :] = jnp.zeros((64, 256), BF16)
                low_ref[n, pl.ds(256 * side, 64), :] = jnp.zeros((64, 256), BF16)


def prepare(info, left, other):
    return pl.pallas_call(
        prepare_body,
        out_shape=[jax.ShapeDtypeStruct((4, 512, 256), BF16)] * 2,
        in_specs=[SM, VM, VM],
        out_specs=[VM, VM],
        compiler_params=PARAMS,
        name="prepare_update",
    )(info, left, other)


def accumulate(info, sums, high, low, pieces, places, name):
    first = sums is None

    def body(info, high_ref, low_ref, *refs):
        out_ref = refs[-1]
        x, core, y, z, col = (info[k] for k in range(5))
        if first:
            out_ref[...] = jnp.zeros(out_ref.shape, F32)
        else:
            out_ref[...] = refs[0][...]
        for ref, (far, slot) in zip(refs[0 if first else 1 :], places):
            for n in range(ref.shape[0]):
                near = slot + n
                py = lax.rem(y + jnp.where(core == 0, far, near), 4)
                pz = lax.rem(z + jnp.where(core == 0, near, far), 4)
                upper = py // 2
                bit = jnp.where(upper == 0, py, 3 - py)
                cols = pl.ds(pl.multiple_of((4 * bit + pz) * TILE, TILE), TILE)
                total = None
                for h in range(2):
                    x_high, x_low = split(ref[n, pl.ds(256 * h, 256), :])
                    wide = mm(high_ref[2 * upper + h], jnp.concatenate([x_high, x_low], 1))
                    term = wide[:, :TILE] + (wide[:, TILE:] + mm(low_ref[2 * upper + h], x_high))
                    total = term if total is None else total + term
                out_ref[:, cols] = out_ref[:, cols] + total

                @pl.when((x == 0) & (col // 8 == upper))
                def _():
                    there = pl.ds(pl.multiple_of(lax.rem(col, 8) * 64, 64), 64)
                    here = pl.ds(0, 64)
                    out_ref[here, cols] = out_ref[here, cols] - ref[n, there, :]

    start = [] if first else [sums]
    return pl.pallas_call(
        body,
        out_shape=jax.ShapeDtypeStruct((512, 1024), F32),
        in_specs=[SM] + [VM] * (2 + len(start) + len(pieces)),
        out_specs=VM,
        input_output_aliases={} if first else {3: 0},
        compiler_params=PARAMS,
        name=name,
    )(info, high, low, *start, *pieces)


AXES = ROW + COL


def move(value, where):
    pairs = []
    for x in range(4):
        for core in range(2):
            for y in range(4):
                for z in range(4):
                    to = where(x, core, y, z)
                    if to is not None:
                        a, b, c, d = to
                        pairs.append((((x * 2 + core) * 4 + y) * 4 + z, ((a * 2 + b) * 4 + c % 4) * 4 + d % 4))
    return lax.ppermute(value, AXES, pairs)


def deal(first, second, core, yh, xi):
    solved = jnp.where(core == 0, first, second)
    lower = yh == 0
    here = jnp.where(lower, solved[:512], solved[512:])
    there = jnp.where(core == 0, solved[512:], solved[:512])
    got = move(there, lambda a, b, c, d: (0, b, 3 - c, d) if a == 0 and b == c // 2 else None)
    mine = jnp.where(core == yh, here, got)
    one = move(mine, lambda a, b, c, d: (1 if b == 0 else 3, b, c, d) if a == 0 else None)
    two = move(mine, lambda a, b, c, d: (3 if b == 0 else 1, b, c, d) if a == 0 else None)
    far = move(one, lambda a, b, c, d: (2, b, c, d) if a == (1 if b == 0 else 3) else None)
    return jnp.where(xi == 0, mine, one + two + far)


def ring(value, first):
    def along(step):
        def where(a, b, c, d):
            on_z = (b == 0) == first
            return (a, b, c, d + step) if on_z else (a, b, c + step, d)

        return where

    before = move(value, along(1))
    after = move(value, along(-1))
    cut = value.shape[0] // 2
    far_low = move(before[:cut], along(1))
    far_high = move(after[cut:], along(-1))
    return after, far_low, far_high, before


def gather(lead, half, core, yl):
    def holds(a, b, c):
        return a == 0 and (b == 1 or c < 2)

    def step(b_on_z, amount):
        def where(a, b, c, d):
            if not holds(a, b, c):
                return None
            return (a, b, c, d + amount) if b == b_on_z else (a, b, c + 1 - 2 * (c % 2), d)

        return where

    def only(b_only, amount):
        return lambda a, b, c, d: (a, b, c, d + amount) if holds(a, b, c) and b == b_only else None

    mixed = move(lead, step(1, 1))
    after = move(lead, only(1, -1))
    swapped = move(lead, lambda a, b, c, d: (a, b, c + 1 - 2 * (c % 2), d) if holds(a, b, c) and b == 1 else None)
    mixed, swapped, half = lax.optimization_barrier((mixed, swapped, half))
    other_half = move(half, lambda a, b, c, d: (0, b, 3 - c, d) if a == 0 and c >= 2 else None)
    far_low = move(mixed[:512], only(1, 1))
    far_high = move(after[512:], only(1, -1))

    full = jnp.where(yl == 0, lead, mixed)
    lower = jnp.where(yl == 0, mixed[512:], lead[512:])
    zero = core == 0
    first = jnp.concatenate([jnp.where(zero, full, mixed), jnp.where(zero, lower, far_low)], 0)
    second = jnp.concatenate([jnp.where(zero, full, after), jnp.where(zero, lower, far_high)], 0)
    got_first = move(first, step(0, 1))
    got_second = move(second, step(0, -1))
    got_first, other_half = lax.optimization_barrier((got_first, other_half))
    end_low = move(got_first[:768], only(0, 1))
    end_high = move(got_second[768:], only(0, -1))

    corner_pieces = [first, got_second, got_first, end_low, end_high]
    corner_places = [[(0, n, 0, 0, 1024), (1, n, 1024, 512, 512)] for n in (0, 1, 3)]
    corner_places += [[(0, 2, 0, 0, 768)], [(0, 2, 0, 768, 256), (1, 2, 256, 512, 512)]]
    lower_pieces = [lead, swapped, first, second, got_first, got_second]
    lower_places = [[("own", 0, 0, 0, 1024)], [("pair", 0, 0, 0, 1024)]]
    for group in ("own", "pair"):
        lower_places.append([(group, 3, 0, 0, 1024), (group, 2, 1024, 0, 512)])
        lower_places.append([(group, 1, 0, 0, 1024), (group, 2, 1024, 512, 512)])
    return (corner_pieces, corner_places), (lower_pieces, lower_places), jnp.concatenate([half, other_half], 0)


def shards(factor, cross_cov):
    xi, core = lax.axis_index("x"), lax.axis_index("core")
    yh, yl, z = lax.axis_index("yh"), lax.axis_index("yl"), lax.axis_index("z")
    row_id = 2 * xi + core
    col_id = 8 * yh + 4 * yl + z
    local = factor[:, 0]
    rhs = cross_cov[:, 0]

    diagonal = ((row_id == 0) & (yh == 0)) | ((row_id == 1) & (yh == 1))
    info = jnp.stack([diagonal.astype(jnp.int32), (4 * yl + z).astype(jnp.int32)])
    lead = invert_diagonal(info, local[0])

    half = lax.all_to_all(arrange_rhs(yh, rhs), ("yl", "z"), 0, 0, tiled=True).reshape(512, TILE)
    upper_left, lower_row, columns = gather(lead, half, core, yl)

    def place(what):
        return jnp.stack([yl, z, jnp.where(xi == 0, what, 0)]).astype(jnp.int32)

    first = solve_first(place((core == 0) & (yh == 0)), *upper_left, columns)
    sent = move(first, lambda a, b, c, d: (0, 1, c, d) if (a, b) == (0, 0) and c < 2 else None)
    rest, tri = residual_or_pack(place(core * (1 + yh)), *lower_row, columns, sent)
    second_rhs = move(rest, lambda a, b, c, d: (0, 1, 3 - c, d) if (a, b) == (0, 1) and c < 2 else None)
    second = solve_second(place((core == 1) & (yh == 1)), tri, second_rhs)
    mine = deal(first, second, core, yh, xi)
    by_rows, _ = lax.optimization_barrier((arrange(local), mine))
    left = lax.all_to_all(by_rows, COL, 0, 0, tiled=True)

    def swap(value):
        return move(value, lambda a, b, c, d: (a, 1 - b, c, d))

    info2 = jnp.stack([xi, core, 2 * yh + yl, z, col_id]).astype(jnp.int32)

    after, far_low, far_high, before = ring(mine, True)
    low = jnp.stack([mine, after])
    high = jnp.stack([jnp.concatenate([far_low, far_high], 0), before])

    left, _ = lax.optimization_barrier((left, high))
    given = swap(lax.dynamic_slice_in_dim(left, 8 * (1 - core), 8, 0))

    def along(step):
        return lambda a, b, c, d: (a, b, c + step, d) if b == 0 else (a, b, c, d + step)

    low_before, low_after = move(low, along(1)), move(low, along(-1))
    high_after, high_before = move(high, along(-1)), move(high, along(1))
    parts = prepare(info2[:2], left, given)

    def add(sums, pieces, places, name):
        return accumulate(info2, sums, *parts, pieces, places, name)

    sums = add(None, [low, high], [(0, 0), (0, 2)], "update_near")
    low_before, high_after, sums = lax.optimization_barrier((low_before, high_after, sums))
    far_low, far_high = move(low_before, along(1)), move(high_after, along(-1))
    sums = add(
        sums, [low_after, high_after, low_before, high_before], [(1, 0), (1, 2), (3, 0), (3, 2)], "update_next"
    )
    far_low, far_high, sums = lax.optimization_barrier((far_low, far_high, sums))
    sums = add(sums, [far_low, far_high], [(2, 0), (2, 2)], "update_far")

    replaced = (xi == 0) & (lax.broadcasted_iota(jnp.int32, (256, 1024), 0) < 64)
    base = jnp.where(replaced, 0.0, rhs.reshape(256, 1024))
    out = base - (sums[:256] + swap(sums[256:]))
    return out.reshape(4, 1, 64, 1024)


def solution(mesh):
    fine = Mesh(mesh.devices.reshape(4, 2, 2, 2, 4), ROW + COL)
    return jax.shard_map(
        shards,
        mesh=fine,
        in_specs=(P(None, ROW, None, COL), P(None, ROW, COL, None)),
        out_specs=P(None, ROW, COL, None),
        check_vma=False,
    )
```

```python
import jax
import jax.numpy as jnp
from jax import lax
from jax.experimental import pallas as pl
from jax.experimental.pallas import tpu as pltpu
from jax.sharding import Mesh, PartitionSpec as P

ROW = ("x", "core")
COL = ("yh", "yl", "z")
F32 = jnp.float32
BF16 = jnp.bfloat16
TILE = 128
STORE = 112
PARAMS = pltpu.CompilerParams(vmem_limit_bytes=20 * 2**20)
VM = pl.BlockSpec(memory_space=pltpu.VMEM)
SM = pl.BlockSpec(memory_space=pltpu.SMEM)
FAR = pl.BlockSpec(memory_space=pltpu.HBM)


def split(value):
    high = value.astype(BF16)
    return high, (value - high.astype(F32)).astype(BF16)


def mm(a, b):
    return jnp.dot(a, b, preferred_element_type=F32)


def pack_left(value):
    return jnp.concatenate(split(value), 1)


def pack_right(value):
    high, low = split(value)
    return jnp.concatenate(
        [jnp.concatenate([high, low], 1), jnp.concatenate([high, jnp.zeros_like(low)], 1)], 0
    )


def packed_product(left, right):
    out = mm(left, right)
    return out[:, :TILE] + out[:, TILE:]


def invert_body(info, lead_ref, out_ref):
    out_ref[...] = lead_ref[...]

    @pl.when(info[0] == 1)
    def _():
        start = pl.multiple_of(info[1] * TILE, TILE)
        block = lead_ref[pl.ds(start, TILE), :]
        i = lax.broadcasted_iota(jnp.int32, (TILE, TILE), 0)
        j = lax.broadcasted_iota(jnp.int32, (TILE, TILE), 1)
        zero = jnp.zeros((TILE, TILE), F32)
        inverse = jnp.where(i == j, 1.0 / jnp.where(i == j, block, 1.0), zero)
        step = 1
        while step < TILE:
            below = ((i // (2 * step)) == (j // (2 * step))) & ((i // step) > (j // step))
            corner = jnp.where(below, block, zero)
            product = packed_product(pack_left(corner), pack_right(inverse))
            inverse = inverse - packed_product(pack_left(inverse), pack_right(product))
            step *= 2
        out_ref[pl.ds(start, TILE), :] = inverse


def invert_diagonal(info, lead):
    return pl.pallas_call(
        invert_body,
        out_shape=jax.ShapeDtypeStruct(lead.shape, F32),
        in_specs=[SM, VM],
        out_specs=VM,
        compiler_params=PARAMS,
        name="invert_diagonal",
    )(info, lead)


def substitute(tri_ref, rhs_ref, out_ref, ready):
    out_ref[...] = rhs_ref[...]
    for k in range(8):
        ready(k)
        here = pl.ds(k * TILE, TILE)
        solved = packed_product(tri_ref[k, here, :], pack_right(out_ref[here, :]))
        out_ref[here, :] = solved
        right = pack_right(solved)
        for i in range(k + 1, 8):
            there = pl.ds(i * TILE, TILE)
            out_ref[there, :] = out_ref[there, :] - packed_product(tri_ref[k, there, :], right)


def pack_pieces(info, refs, places, tri_ref):
    for ref, parts in zip(refs, places):
        for half, steps, start, to, rows in parts:
            half = {"own": info[0], "pair": 1 - info[0]}.get(half, half)
            k = 4 * half + lax.rem(info[1] + steps, 4)
            tri_ref[k, pl.ds(to, rows), :] = pack_left(ref[pl.ds(start, rows), :])


def solve_first(info, pieces, places, rhs):
    def body(info, *refs):
        rhs_ref, out_ref, tri_ref = refs[-3:]

        @pl.when(info[2] == 1)
        def _():
            pack_pieces(info, refs, places, tri_ref)
            substitute(tri_ref, rhs_ref, out_ref, lambda k: None)

    return pl.pallas_call(
        body,
        out_shape=jax.ShapeDtypeStruct(rhs.shape, F32),
        in_specs=[SM] + [VM] * (len(pieces) + 1),
        out_specs=VM,
        scratch_shapes=[pltpu.VMEM((8, 1024, 256), BF16)],
        compiler_params=PARAMS,
        name="solve_first",
    )(info, *pieces, rhs)


def residual_or_pack(info, pieces, places, rhs, x):
    count = len(pieces)

    def body(info, *refs):
        rhs_ref, x_ref, out_ref, tri_out, tri_ref, semaphore = refs[count:]

        @pl.when(info[2] == 1)
        def _():
            out_ref[...] = rhs_ref[...]
            for ref, parts in zip(refs, places):
                for half, steps, start, to, rows in parts:
                    half = {"own": info[0], "pair": 1 - info[0]}[half]
                    k = 4 * half + lax.rem(info[1] + steps, 4)
                    right = pack_right(x_ref[pl.ds(pl.multiple_of(k * TILE, TILE), TILE), :])
                    for n in range(0, rows, TILE):
                        there = pl.ds(to + n, TILE)
                        left = pack_left(ref[pl.ds(start + n, TILE), :])
                        out_ref[there, :] = out_ref[there, :] - packed_product(left, right)

        @pl.when(info[2] == 2)
        def _():
            pack_pieces(info, refs, places, tri_ref)
            copy = pltpu.make_async_copy(tri_ref, tri_out.at[pl.ds(0, 8)], semaphore)
            copy.start()
            copy.wait()

    return pl.pallas_call(
        body,
        out_shape=[jax.ShapeDtypeStruct(rhs.shape, F32), jax.ShapeDtypeStruct((STORE, 1024, 256), BF16)],
        in_specs=[SM] + [VM] * (count + 2),
        out_specs=[VM, FAR],
        scratch_shapes=[pltpu.VMEM((8, 1024, 256), BF16), pltpu.SemaphoreType.DMA],
        compiler_params=PARAMS,
        name="residual_or_pack",
    )(info, *pieces, rhs, x)


def solve_second(info, tri, rhs):
    def body(info, tri_in, rhs_ref, out_ref, tri_ref, semaphores):
        @pl.when(info[2] == 1)
        def _():
            copies = [pltpu.make_async_copy(tri_in.at[k], tri_ref.at[k], semaphores.at[k]) for k in range(8)]
            for copy in copies:
                copy.start()
            substitute(tri_ref, rhs_ref, out_ref, lambda k: copies[k].wait())

    return pl.pallas_call(
        body,
        out_shape=jax.ShapeDtypeStruct(rhs.shape, F32),
        in_specs=[SM, FAR, VM],
        out_specs=VM,
        scratch_shapes=[pltpu.VMEM((8, 1024, 256), BF16), pltpu.SemaphoreType.DMA((8,))],
        compiler_params=PARAMS,
        name="solve_second",
    )(info, tri, rhs)


def arrange_body(factor_ref, out_ref):
    for c in range(16):
        for a in range(4):
            out_ref[c, pl.ds(64 * a, 64), :] = factor_ref[a, pl.ds(64 * c, 64), :]


def arrange(factor):
    return pl.pallas_call(
        arrange_body,
        out_shape=jax.ShapeDtypeStruct((16, 256, TILE), F32),
        in_specs=[VM],
        out_specs=VM,
        compiler_params=PARAMS,
        name="arrange_rows",
    )(factor)


def arrange_rhs_body(info, rhs_ref, out_ref):
    for n in range(8):
        to = jnp.where(info[0] == 0, n, (n + 4) % 8)
        out_ref[to, :, :] = rhs_ref[0, :, pl.ds(n * TILE, TILE)]


def arrange_rhs(yh, rhs):
    return pl.pallas_call(
        arrange_rhs_body,
        grid=(1,),
        out_shape=jax.ShapeDtypeStruct((8, 64, TILE), F32),
        in_specs=[SM, pl.BlockSpec((1, 64, 1024), lambda i: (0, 0, 0))],
        out_specs=pl.BlockSpec((8, 64, TILE), lambda i: (0, 0, 0)),
        compiler_params=PARAMS,
        name="arrange_rhs",
    )(jnp.reshape(yh, (1,)).astype(jnp.int32), rhs)


def prepare_body(info, left_ref, other_ref, high_ref, low_ref):
    for side, ref in enumerate((left_ref, other_ref)):
        rows = pl.ds(256 * side, 256)
        first = 8 * info[1] if side == 0 else 0
        for n in range(4):
            high, low = split(jnp.concatenate([ref[first + 2 * n], ref[first + 2 * n + 1]], 1))
            high_ref[n, rows, :] = high
            low_ref[n, rows, :] = low

    @pl.when(info[0] == 0)
    def _():
        for n in range(4):
            for side in range(2):
                high_ref[n, pl.ds(256 * side, 64), :] = jnp.zeros((64, 256), BF16)
                low_ref[n, pl.ds(256 * side, 64), :] = jnp.zeros((64, 256), BF16)


def prepare(info, left, other):
    return pl.pallas_call(
        prepare_body,
        out_shape=[jax.ShapeDtypeStruct((4, 512, 256), BF16)] * 2,
        in_specs=[SM, VM, VM],
        out_specs=[VM, VM],
        compiler_params=PARAMS,
        name="prepare_update",
    )(info, left, other)


def accumulate(info, sums, high, low, pieces, places, name):
    first = sums is None

    def body(info, high_ref, low_ref, *refs):
        out_ref = refs[-1]
        x, core, y, z, col = (info[k] for k in range(5))
        if first:
            out_ref[...] = jnp.zeros(out_ref.shape, F32)
        else:
            out_ref[...] = refs[0][...]
        for ref, (far, slot) in zip(refs[0 if first else 1 :], places):
            for n in range(ref.shape[0]):
                near = slot + n
                py = lax.rem(y + jnp.where(core == 0, far, near), 4)
                pz = lax.rem(z + jnp.where(core == 0, near, far), 4)
                upper = py // 2
                bit = jnp.where(upper == 0, py, 3 - py)
                cols = pl.ds(pl.multiple_of((4 * bit + pz) * TILE, TILE), TILE)
                total = None
                for h in range(2):
                    x_high, x_low = split(ref[n, pl.ds(256 * h, 256), :])
                    wide = mm(high_ref[2 * upper + h], jnp.concatenate([x_high, x_low], 1))
                    term = wide[:, :TILE] + (wide[:, TILE:] + mm(low_ref[2 * upper + h], x_high))
                    total = term if total is None else total + term
                out_ref[:, cols] = out_ref[:, cols] + total

                @pl.when((x == 0) & (col // 8 == upper))
                def _():
                    there = pl.ds(pl.multiple_of(lax.rem(col, 8) * 64, 64), 64)
                    here = pl.ds(0, 64)
                    out_ref[here, cols] = out_ref[here, cols] - ref[n, there, :]

    start = [] if first else [sums]
    return pl.pallas_call(
        body,
        out_shape=jax.ShapeDtypeStruct((512, 1024), F32),
        in_specs=[SM] + [VM] * (2 + len(start) + len(pieces)),
        out_specs=VM,
        input_output_aliases={} if first else {3: 0},
        compiler_params=PARAMS,
        name=name,
    )(info, high, low, *start, *pieces)


AXES = ROW + COL


def move(value, where):
    pairs = []
    for x in range(4):
        for core in range(2):
            for y in range(4):
                for z in range(4):
                    to = where(x, core, y, z)
                    if to is not None:
                        a, b, c, d = to
                        pairs.append((((x * 2 + core) * 4 + y) * 4 + z, ((a * 2 + b) * 4 + c % 4) * 4 + d % 4))
    return lax.ppermute(value, AXES, pairs)


def deal(first, second, core, yh, xi):
    solved = jnp.where(core == 0, first, second)
    lower = yh == 0
    here = jnp.where(lower, solved[:512], solved[512:])
    there = jnp.where(core == 0, solved[512:], solved[:512])
    got = move(there, lambda a, b, c, d: (0, b, 3 - c, d) if a == 0 and b == c // 2 else None)
    mine = jnp.where(core == yh, here, got)
    one = move(mine, lambda a, b, c, d: (1 if b == 0 else 3, b, c, d) if a == 0 else None)
    two = move(mine, lambda a, b, c, d: (3 if b == 0 else 1, b, c, d) if a == 0 else None)
    far = move(one, lambda a, b, c, d: (2, b, c, d) if a == (1 if b == 0 else 3) else None)
    return jnp.where(xi == 0, mine, one + two + far)


def ring(value, first):
    def along(step):
        def where(a, b, c, d):
            on_z = (b == 0) == first
            return (a, b, c, d + step) if on_z else (a, b, c + step, d)

        return where

    before = move(value, along(1))
    after = move(value, along(-1))
    cut = value.shape[0] // 2
    far_low = move(before[:cut], along(1))
    far_high = move(after[cut:], along(-1))
    return after, far_low, far_high, before


def gather(lead, half, by_rows, core, yl):
    def holds(a, b, c):
        return a == 0 and (b == 1 or c < 2)

    def step(b_on_z, amount):
        def where(a, b, c, d):
            if not holds(a, b, c):
                return None
            return (a, b, c, d + amount) if b == b_on_z else (a, b, c + 1 - 2 * (c % 2), d)

        return where

    def only(b_only, amount):
        return lambda a, b, c, d: (a, b, c, d + amount) if holds(a, b, c) and b == b_only else None

    mixed = move(lead, step(1, 1))
    after = move(lead, only(1, -1))
    swapped = move(lead, lambda a, b, c, d: (a, b, c + 1 - 2 * (c % 2), d) if holds(a, b, c) and b == 1 else None)
    mixed, swapped, half = lax.optimization_barrier((mixed, swapped, half))
    other_half = move(half, lambda a, b, c, d: (0, b, 3 - c, d) if a == 0 and c >= 2 else None)
    far_low = move(mixed[:512], only(1, 1))
    far_high = move(after[512:], only(1, -1))

    full = jnp.where(yl == 0, lead, mixed)
    lower = jnp.where(yl == 0, mixed[512:], lead[512:])
    zero = core == 0
    first = jnp.concatenate([jnp.where(zero, full, mixed), jnp.where(zero, lower, far_low)], 0)
    second = jnp.concatenate([jnp.where(zero, full, after), jnp.where(zero, lower, far_high)], 0)
    got_first = move(first, step(0, 1))
    got_second = move(second, step(0, -1))
    got_first, other_half, by_rows = lax.optimization_barrier((got_first, other_half, by_rows))
    end_low = move(got_first[:768], only(0, 1))
    end_high = move(got_second[768:], only(0, -1))

    corner_pieces = [first, got_second, got_first, end_low, end_high]
    corner_places = [[(0, n, 0, 0, 1024), (1, n, 1024, 512, 512)] for n in (0, 1, 3)]
    corner_places += [[(0, 2, 0, 0, 768)], [(0, 2, 0, 768, 256), (1, 2, 256, 512, 512)]]
    lower_pieces = [lead, swapped, first, second, got_first, got_second]
    lower_places = [[("own", 0, 0, 0, 1024)], [("pair", 0, 0, 0, 1024)]]
    for group in ("own", "pair"):
        lower_places.append([(group, 3, 0, 0, 1024), (group, 2, 1024, 0, 512)])
        lower_places.append([(group, 1, 0, 0, 1024), (group, 2, 1024, 512, 512)])
    return (corner_pieces, corner_places), (lower_pieces, lower_places), jnp.concatenate([half, other_half], 0), by_rows


def shards(factor, cross_cov):
    xi, core = lax.axis_index("x"), lax.axis_index("core")
    yh, yl, z = lax.axis_index("yh"), lax.axis_index("yl"), lax.axis_index("z")
    row_id = 2 * xi + core
    col_id = 8 * yh + 4 * yl + z
    local = factor[:, 0]
    rhs = cross_cov[:, 0]

    diagonal = ((row_id == 0) & (yh == 0)) | ((row_id == 1) & (yh == 1))
    info = jnp.stack([diagonal.astype(jnp.int32), (4 * yl + z).astype(jnp.int32)])
    lead = invert_diagonal(info, local[0])

    half = lax.all_to_all(arrange_rhs(yh, rhs), ("yl", "z"), 0, 0, tiled=True).reshape(512, TILE)
    upper_left, lower_row, columns, by_rows = gather(lead, half, arrange(local), core, yl)

    def place(what):
        return jnp.stack([yl, z, jnp.where(xi == 0, what, 0)]).astype(jnp.int32)

    first = solve_first(place((core == 0) & (yh == 0)), *upper_left, columns)
    sent = move(first, lambda a, b, c, d: (0, 1, c, d) if (a, b) == (0, 0) and c < 2 else None)
    by_rows, _ = lax.optimization_barrier((by_rows, first))
    left = lax.all_to_all(by_rows, COL, 0, 0, tiled=True)
    rest, tri = residual_or_pack(place(core * (1 + yh)), *lower_row, columns, sent)
    second_rhs = move(rest, lambda a, b, c, d: (0, 1, 3 - c, d) if (a, b) == (0, 1) and c < 2 else None)
    second = solve_second(place((core == 1) & (yh == 1)), tri, second_rhs)
    second, left = lax.optimization_barrier((second, left))
    mine = deal(first, second, core, yh, xi)

    def swap(value):
        return move(value, lambda a, b, c, d: (a, 1 - b, c, d))

    info2 = jnp.stack([xi, core, 2 * yh + yl, z, col_id]).astype(jnp.int32)

    after, far_low, far_high, before = ring(mine, True)
    low = jnp.stack([mine, after])
    high = jnp.stack([jnp.concatenate([far_low, far_high], 0), before])

    left, _ = lax.optimization_barrier((left, high))
    given = swap(lax.dynamic_slice_in_dim(left, 8 * (1 - core), 8, 0))

    def along(step):
        return lambda a, b, c, d: (a, b, c + step, d) if b == 0 else (a, b, c, d + step)

    low_before, low_after = move(low, along(1)), move(low, along(-1))
    high_after, high_before = move(high, along(-1)), move(high, along(1))
    parts = prepare(info2[:2], left, given)

    def add(sums, pieces, places, name):
        return accumulate(info2, sums, *parts, pieces, places, name)

    sums = add(None, [low, high], [(0, 0), (0, 2)], "update_near")
    low_before, high_after, sums = lax.optimization_barrier((low_before, high_after, sums))
    far_low, far_high = move(low_before, along(1)), move(high_after, along(-1))
    sums = add(
        sums, [low_after, high_after, low_before, high_before], [(1, 0), (1, 2), (3, 0), (3, 2)], "update_next"
    )
    far_low, far_high, sums = lax.optimization_barrier((far_low, far_high, sums))
    sums = add(sums, [far_low, far_high], [(2, 0), (2, 2)], "update_far")

    replaced = (xi == 0) & (lax.broadcasted_iota(jnp.int32, (256, 1024), 0) < 64)
    base = jnp.where(replaced, 0.0, rhs.reshape(256, 1024))
    out = base - (sums[:256] + swap(sums[256:]))
    return out.reshape(4, 1, 64, 1024)


def solution(mesh):
    fine = Mesh(mesh.devices.reshape(4, 2, 2, 2, 4), ROW + COL)
    return jax.shard_map(
        shards,
        mesh=fine,
        in_specs=(P(None, ROW, None, COL), P(None, ROW, COL, None)),
        out_specs=P(None, ROW, COL, None),
        check_vma=False,
    )
```

```python
import jax
import jax.numpy as jnp
from jax import lax
from jax.experimental import pallas as pl
from jax.experimental.pallas import tpu as pltpu
from jax.sharding import Mesh, PartitionSpec as P

ROW = ("x", "core")
COL = ("yh", "yl", "z")
F32 = jnp.float32
BF16 = jnp.bfloat16
TILE = 128
STORE = 112
PARAMS = pltpu.CompilerParams(vmem_limit_bytes=20 * 2**20)
VM = pl.BlockSpec(memory_space=pltpu.VMEM)
SM = pl.BlockSpec(memory_space=pltpu.SMEM)
FAR = pl.BlockSpec(memory_space=pltpu.HBM)


def split(value):
    high = value.astype(BF16)
    return high, (value - high.astype(F32)).astype(BF16)


def mm(a, b):
    return jnp.dot(a, b, preferred_element_type=F32)


def pack_left(value):
    return jnp.concatenate(split(value), 1)


def pack_right(value):
    high, low = split(value)
    return jnp.concatenate(
        [jnp.concatenate([high, low], 1), jnp.concatenate([high, jnp.zeros_like(low)], 1)], 0
    )


def packed_product(left, right):
    out = mm(left, right)
    return out[:, :TILE] + out[:, TILE:]


def invert_body(info, lead_ref, out_ref):
    out_ref[...] = lead_ref[...]

    @pl.when(info[0] == 1)
    def _():
        start = pl.multiple_of(info[1] * TILE, TILE)
        block = lead_ref[pl.ds(start, TILE), :]
        i = lax.broadcasted_iota(jnp.int32, (TILE, TILE), 0)
        j = lax.broadcasted_iota(jnp.int32, (TILE, TILE), 1)
        zero = jnp.zeros((TILE, TILE), F32)
        inverse = jnp.where(i == j, 1.0 / jnp.where(i == j, block, 1.0), zero)
        step = 1
        while step < TILE:
            below = ((i // (2 * step)) == (j // (2 * step))) & ((i // step) > (j // step))
            corner = jnp.where(below, block, zero)
            product = packed_product(pack_left(corner), pack_right(inverse))
            inverse = inverse - packed_product(pack_left(inverse), pack_right(product))
            step *= 2
        out_ref[pl.ds(start, TILE), :] = inverse


def invert_diagonal(info, lead):
    return pl.pallas_call(
        invert_body,
        out_shape=jax.ShapeDtypeStruct(lead.shape, F32),
        in_specs=[SM, VM],
        out_specs=VM,
        compiler_params=PARAMS,
        name="invert_diagonal",
    )(info, lead)


def substitute(tri_ref, rhs_ref, out_ref, ready):
    out_ref[...] = rhs_ref[...]
    for k in range(8):
        ready(k)
        here = pl.ds(k * TILE, TILE)
        solved = packed_product(tri_ref[k, here, :], pack_right(out_ref[here, :]))
        out_ref[here, :] = solved
        right = pack_right(solved)
        for i in range(k + 1, 8):
            there = pl.ds(i * TILE, TILE)
            out_ref[there, :] = out_ref[there, :] - packed_product(tri_ref[k, there, :], right)


def pack_pieces(info, refs, places, tri_ref):
    for ref, parts in zip(refs, places):
        for half, steps, start, to, rows in parts:
            half = {"own": info[0], "pair": 1 - info[0]}.get(half, half)
            k = 4 * half + lax.rem(info[1] + steps, 4)
            tri_ref[k, pl.ds(to, rows), :] = pack_left(ref[pl.ds(start, rows), :])


def solve_first(info, pieces, places, rhs):
    def body(info, *refs):
        rhs_ref, out_ref, tri_ref = refs[-3:]

        @pl.when(info[2] == 1)
        def _():
            pack_pieces(info, refs, places, tri_ref)
            substitute(tri_ref, rhs_ref, out_ref, lambda k: None)

    return pl.pallas_call(
        body,
        out_shape=jax.ShapeDtypeStruct(rhs.shape, F32),
        in_specs=[SM] + [VM] * (len(pieces) + 1),
        out_specs=VM,
        scratch_shapes=[pltpu.VMEM((8, 1024, 256), BF16)],
        compiler_params=PARAMS,
        name="solve_first",
    )(info, *pieces, rhs)


def residual_or_pack(info, pieces, places, rhs, x):
    count = len(pieces)

    def body(info, *refs):
        rhs_ref, x_ref, out_ref, tri_out, tri_ref, semaphore = refs[count:]

        @pl.when(info[2] == 1)
        def _():
            out_ref[...] = rhs_ref[...]
            for ref, parts in zip(refs, places):
                for half, steps, start, to, rows in parts:
                    half = {"own": info[0], "pair": 1 - info[0]}[half]
                    k = 4 * half + lax.rem(info[1] + steps, 4)
                    right = pack_right(x_ref[pl.ds(pl.multiple_of(k * TILE, TILE), TILE), :])
                    for n in range(0, rows, TILE):
                        there = pl.ds(to + n, TILE)
                        left = pack_left(ref[pl.ds(start + n, TILE), :])
                        out_ref[there, :] = out_ref[there, :] - packed_product(left, right)

        @pl.when(info[2] == 2)
        def _():
            pack_pieces(info, refs, places, tri_ref)
            copy = pltpu.make_async_copy(tri_ref, tri_out.at[pl.ds(0, 8)], semaphore)
            copy.start()
            copy.wait()

    return pl.pallas_call(
        body,
        out_shape=[jax.ShapeDtypeStruct(rhs.shape, F32), jax.ShapeDtypeStruct((STORE, 1024, 256), BF16)],
        in_specs=[SM] + [VM] * (count + 2),
        out_specs=[VM, FAR],
        scratch_shapes=[pltpu.VMEM((8, 1024, 256), BF16), pltpu.SemaphoreType.DMA],
        compiler_params=PARAMS,
        name="residual_or_pack",
    )(info, *pieces, rhs, x)


def solve_second(info, tri, rhs):
    def body(info, tri_in, rhs_ref, out_ref, tri_ref, semaphores):
        @pl.when(info[2] == 1)
        def _():
            copies = [pltpu.make_async_copy(tri_in.at[k], tri_ref.at[k], semaphores.at[k]) for k in range(8)]
            for copy in copies:
                copy.start()
            substitute(tri_ref, rhs_ref, out_ref, lambda k: copies[k].wait())

    return pl.pallas_call(
        body,
        out_shape=jax.ShapeDtypeStruct(rhs.shape, F32),
        in_specs=[SM, FAR, VM],
        out_specs=VM,
        scratch_shapes=[pltpu.VMEM((8, 1024, 256), BF16), pltpu.SemaphoreType.DMA((8,))],
        compiler_params=PARAMS,
        name="solve_second",
    )(info, tri, rhs)


def arrange_body(factor_ref, out_ref):
    for c in range(16):
        for a in range(4):
            out_ref[c, pl.ds(64 * a, 64), :] = factor_ref[a, pl.ds(64 * c, 64), :]


def arrange(factor):
    return pl.pallas_call(
        arrange_body,
        out_shape=jax.ShapeDtypeStruct((16, 256, TILE), F32),
        in_specs=[VM],
        out_specs=VM,
        compiler_params=PARAMS,
        name="arrange_rows",
    )(factor)


def arrange_rhs_body(info, rhs_ref, out_ref):
    for n in range(8):
        to = jnp.where(info[0] == 0, n, (n + 4) % 8)
        out_ref[to, :, :] = rhs_ref[0, :, pl.ds(n * TILE, TILE)]


def arrange_rhs(yh, rhs):
    return pl.pallas_call(
        arrange_rhs_body,
        grid=(1,),
        out_shape=jax.ShapeDtypeStruct((8, 64, TILE), F32),
        in_specs=[SM, pl.BlockSpec((1, 64, 1024), lambda i: (0, 0, 0))],
        out_specs=pl.BlockSpec((8, 64, TILE), lambda i: (0, 0, 0)),
        compiler_params=PARAMS,
        name="arrange_rhs",
    )(jnp.reshape(yh, (1,)).astype(jnp.int32), rhs)


def prepare_body(info, left_ref, other_ref, high_ref, low_ref):
    for side, ref in enumerate((left_ref, other_ref)):
        rows = pl.ds(256 * side, 256)
        first = 8 * info[1] if side == 0 else 0
        for n in range(4):
            high, low = split(jnp.concatenate([ref[first + 2 * n], ref[first + 2 * n + 1]], 1))
            high_ref[n, rows, :] = high
            low_ref[n, rows, :] = low

    @pl.when(info[0] == 0)
    def _():
        for n in range(4):
            for side in range(2):
                high_ref[n, pl.ds(256 * side, 64), :] = jnp.zeros((64, 256), BF16)
                low_ref[n, pl.ds(256 * side, 64), :] = jnp.zeros((64, 256), BF16)


def prepare(info, left, other):
    return pl.pallas_call(
        prepare_body,
        out_shape=[jax.ShapeDtypeStruct((4, 512, 256), BF16)] * 2,
        in_specs=[SM, VM, VM],
        out_specs=[VM, VM],
        compiler_params=PARAMS,
        name="prepare_update",
    )(info, left, other)


def accumulate(info, sums, high, low, pieces, places, name):
    first = sums is None

    def body(info, high_ref, low_ref, *refs):
        out_ref = refs[-1]
        x, core, y, z, col = (info[k] for k in range(5))
        if first:
            out_ref[...] = jnp.zeros(out_ref.shape, F32)
        else:
            out_ref[...] = refs[0][...]
        for ref, (far, slot) in zip(refs[0 if first else 1 :], places):
            for n in range(ref.shape[0]):
                near = slot + n
                py = lax.rem(y + jnp.where(core == 0, far, near), 4)
                pz = lax.rem(z + jnp.where(core == 0, near, far), 4)
                upper = py // 2
                bit = jnp.where(upper == 0, py, 3 - py)
                cols = pl.ds(pl.multiple_of((4 * bit + pz) * TILE, TILE), TILE)
                total = None
                for h in range(2):
                    x_high, x_low = split(ref[n, pl.ds(256 * h, 256), :])
                    wide = mm(high_ref[2 * upper + h], jnp.concatenate([x_high, x_low], 1))
                    term = wide[:, :TILE] + (wide[:, TILE:] + mm(low_ref[2 * upper + h], x_high))
                    total = term if total is None else total + term
                out_ref[:, cols] = out_ref[:, cols] + total

                @pl.when((x == 0) & (col // 8 == upper))
                def _():
                    there = pl.ds(pl.multiple_of(lax.rem(col, 8) * 64, 64), 64)
                    here = pl.ds(0, 64)
                    out_ref[here, cols] = out_ref[here, cols] - ref[n, there, :]

    start = [] if first else [sums]
    return pl.pallas_call(
        body,
        out_shape=jax.ShapeDtypeStruct((512, 1024), F32),
        in_specs=[SM] + [VM] * (2 + len(start) + len(pieces)),
        out_specs=VM,
        input_output_aliases={} if first else {3: 0},
        compiler_params=PARAMS,
        name=name,
    )(info, high, low, *start, *pieces)


AXES = ROW + COL


def move(value, where):
    pairs = []
    for x in range(4):
        for core in range(2):
            for y in range(4):
                for z in range(4):
                    to = where(x, core, y, z)
                    if to is not None:
                        a, b, c, d = to
                        pairs.append((((x * 2 + core) * 4 + y) * 4 + z, ((a * 2 + b) * 4 + c % 4) * 4 + d % 4))
    return lax.ppermute(value, AXES, pairs)


def deal(first, second, core, yh, xi):
    solved = jnp.where(core == 0, first, second)
    lower = yh == 0
    here = jnp.where(lower, solved[:512], solved[512:])
    there = jnp.where(core == 0, solved[512:], solved[:512])
    got = move(there, lambda a, b, c, d: (0, b, 3 - c, d) if a == 0 and b == c // 2 else None)
    mine = jnp.where(core == yh, here, got)
    one = move(mine, lambda a, b, c, d: (1 if b == 0 else 3, b, c, d) if a == 0 else None)
    two = move(mine, lambda a, b, c, d: (3 if b == 0 else 1, b, c, d) if a == 0 else None)
    far = move(one, lambda a, b, c, d: (2, b, c, d) if a == (1 if b == 0 else 3) else None)
    return jnp.where(xi == 0, mine, one + two + far)


def ring(value, first):
    def along(step):
        def where(a, b, c, d):
            on_z = (b == 0) == first
            return (a, b, c, d + step) if on_z else (a, b, c + step, d)

        return where

    before = move(value, along(1))
    after = move(value, along(-1))
    cut = value.shape[0] // 2
    far_low = move(before[:cut], along(1))
    far_high = move(after[cut:], along(-1))
    return after, far_low, far_high, before


def gather(lead, half, by_rows, core, yl):
    def holds(a, b, c):
        return a == 0 and (b == 1 or c < 2)

    def step(b_on_z, amount):
        def where(a, b, c, d):
            if not holds(a, b, c):
                return None
            return (a, b, c, d + amount) if b == b_on_z else (a, b, c + 1 - 2 * (c % 2), d)

        return where

    def only(b_only, amount):
        return lambda a, b, c, d: (a, b, c, d + amount) if holds(a, b, c) and b == b_only else None

    mixed = move(lead, step(1, 1))
    after = move(lead, only(1, -1))
    swapped = move(lead, lambda a, b, c, d: (a, b, c + 1 - 2 * (c % 2), d) if holds(a, b, c) and b == 1 else None)
    mixed, swapped, half = lax.optimization_barrier((mixed, swapped, half))
    other_half = move(half, lambda a, b, c, d: (0, b, 3 - c, d) if a == 0 and c >= 2 else None)
    far_low = move(mixed[:512], only(1, 1))
    far_high = move(after[512:], only(1, -1))

    full = jnp.where(yl == 0, lead, mixed)
    lower = jnp.where(yl == 0, mixed[512:], lead[512:])
    zero = core == 0
    first = jnp.concatenate([jnp.where(zero, full, mixed), jnp.where(zero, lower, far_low)], 0)
    second = jnp.concatenate([jnp.where(zero, full, after), jnp.where(zero, lower, far_high)], 0)
    got_first = move(first, step(0, 1))
    got_second = move(second, step(0, -1))
    got_first, other_half, by_rows = lax.optimization_barrier((got_first, other_half, by_rows))
    end_low = move(got_first[:768], only(0, 1))
    end_high = move(got_second[768:], only(0, -1))

    corner_pieces = [first, got_second, got_first, end_low, end_high]
    corner_places = [[(0, n, 0, 0, 1024), (1, n, 1024, 512, 512)] for n in (0, 1, 3)]
    corner_places += [[(0, 2, 0, 0, 768)], [(0, 2, 0, 768, 256), (1, 2, 256, 512, 512)]]
    lower_pieces = [lead, swapped, first, second, got_first, got_second]
    lower_places = [[("own", 0, 0, 0, 1024)], [("pair", 0, 0, 0, 1024)]]
    for group in ("own", "pair"):
        lower_places.append([(group, 3, 0, 0, 1024), (group, 2, 1024, 0, 512)])
        lower_places.append([(group, 1, 0, 0, 1024), (group, 2, 1024, 512, 512)])
    return (corner_pieces, corner_places), (lower_pieces, lower_places), jnp.concatenate([half, other_half], 0), by_rows


def shards(factor, cross_cov):
    xi, core = lax.axis_index("x"), lax.axis_index("core")
    yh, yl, z = lax.axis_index("yh"), lax.axis_index("yl"), lax.axis_index("z")
    row_id = 2 * xi + core
    col_id = 8 * yh + 4 * yl + z
    local = factor[:, 0]
    rhs = cross_cov[:, 0]

    diagonal = ((row_id == 0) & (yh == 0)) | ((row_id == 1) & (yh == 1))
    info = jnp.stack([diagonal.astype(jnp.int32), (4 * yl + z).astype(jnp.int32)])
    lead = invert_diagonal(info, local[0])

    half = lax.all_to_all(arrange_rhs(yh, rhs), ("yl", "z"), 0, 0, tiled=True).reshape(512, TILE)
    upper_left, lower_row, columns, by_rows = gather(lead, half, arrange(local), core, yl)

    def place(what):
        return jnp.stack([yl, z, jnp.where(xi == 0, what, 0)]).astype(jnp.int32)

    first = solve_first(place((core == 0) & (yh == 0)), *upper_left, columns)
    sent = move(first, lambda a, b, c, d: (0, 1, c, d) if (a, b) == (0, 0) and c < 2 else None)
    by_rows, _ = lax.optimization_barrier((by_rows, first))
    left = lax.all_to_all(by_rows, COL, 0, 0, tiled=True)
    rest, tri = residual_or_pack(place(core * (1 + yh)), *lower_row, columns, sent)
    second_rhs = move(rest, lambda a, b, c, d: (0, 1, 3 - c, d) if (a, b) == (0, 1) and c < 2 else None)
    second = solve_second(place((core == 1) & (yh == 1)), tri, second_rhs)
    mine = deal(first, second, core, yh, xi)
    mine, left = lax.optimization_barrier((mine, left))

    def swap(value):
        return move(value, lambda a, b, c, d: (a, 1 - b, c, d))

    info2 = jnp.stack([xi, core, 2 * yh + yl, z, col_id]).astype(jnp.int32)

    after, far_low, far_high, before = ring(mine, True)
    low = jnp.stack([mine, after])
    high = jnp.stack([jnp.concatenate([far_low, far_high], 0), before])

    left, _ = lax.optimization_barrier((left, high))
    given = swap(lax.dynamic_slice_in_dim(left, 8 * (1 - core), 8, 0))

    def along(step):
        return lambda a, b, c, d: (a, b, c + step, d) if b == 0 else (a, b, c, d + step)

    low_before, low_after = move(low, along(1)), move(low, along(-1))
    high_after, high_before = move(high, along(-1)), move(high, along(1))
    parts = prepare(info2[:2], left, given)

    def add(sums, pieces, places, name):
        return accumulate(info2, sums, *parts, pieces, places, name)

    sums = add(None, [low, high], [(0, 0), (0, 2)], "update_near")
    low_before, high_after, sums = lax.optimization_barrier((low_before, high_after, sums))
    far_low, far_high = move(low_before, along(1)), move(high_after, along(-1))
    sums = add(
        sums, [low_after, high_after, low_before, high_before], [(1, 0), (1, 2), (3, 0), (3, 2)], "update_next"
    )
    far_low, far_high, sums = lax.optimization_barrier((far_low, far_high, sums))
    sums = add(sums, [far_low, far_high], [(2, 0), (2, 2)], "update_far")

    replaced = (xi == 0) & (lax.broadcasted_iota(jnp.int32, (256, 1024), 0) < 64)
    base = jnp.where(replaced, 0.0, rhs.reshape(256, 1024))
    out = base - (sums[:256] + swap(sums[256:]))
    return out.reshape(4, 1, 64, 1024)


def solution(mesh):
    fine = Mesh(mesh.devices.reshape(4, 2, 2, 2, 4), ROW + COL)
    return jax.shard_map(
        shards,
        mesh=fine,
        in_specs=(P(None, ROW, None, COL), P(None, ROW, COL, None)),
        out_specs=P(None, ROW, COL, None),
        check_vma=False,
    )
```

```python
import jax
import jax.numpy as jnp
from jax import lax
from jax.experimental import pallas as pl
from jax.experimental.pallas import tpu as pltpu
from jax.sharding import Mesh, PartitionSpec as P

ROW = ("x", "core")
COL = ("yh", "yl", "z")
F32 = jnp.float32
BF16 = jnp.bfloat16
TILE = 128
STORE = 112
PARAMS = pltpu.CompilerParams(vmem_limit_bytes=20 * 2**20)
VM = pl.BlockSpec(memory_space=pltpu.VMEM)
SM = pl.BlockSpec(memory_space=pltpu.SMEM)
FAR = pl.BlockSpec(memory_space=pltpu.HBM)


def split(value):
    high = value.astype(BF16)
    return high, (value - high.astype(F32)).astype(BF16)


def mm(a, b):
    return jnp.dot(a, b, preferred_element_type=F32)


def pack_left(value):
    return jnp.concatenate(split(value), 1)


def pack_right(value):
    high, low = split(value)
    return jnp.concatenate(
        [jnp.concatenate([high, low], 1), jnp.concatenate([high, jnp.zeros_like(low)], 1)], 0
    )


def packed_product(left, right):
    out = mm(left, right)
    return out[:, :TILE] + out[:, TILE:]


def invert_body(info, lead_ref, out_ref):
    out_ref[...] = lead_ref[...]

    @pl.when(info[0] == 1)
    def _():
        start = pl.multiple_of(info[1] * TILE, TILE)
        block = lead_ref[pl.ds(start, TILE), :]
        i = lax.broadcasted_iota(jnp.int32, (TILE, TILE), 0)
        j = lax.broadcasted_iota(jnp.int32, (TILE, TILE), 1)
        zero = jnp.zeros((TILE, TILE), F32)
        inverse = jnp.where(i == j, 1.0 / jnp.where(i == j, block, 1.0), zero)
        step = 1
        while step < TILE:
            below = ((i // (2 * step)) == (j // (2 * step))) & ((i // step) > (j // step))
            corner = jnp.where(below, block, zero)
            product = packed_product(pack_left(corner), pack_right(inverse))
            inverse = inverse - packed_product(pack_left(inverse), pack_right(product))
            step *= 2
        out_ref[pl.ds(start, TILE), :] = inverse


def invert_diagonal(info, lead):
    return pl.pallas_call(
        invert_body,
        out_shape=jax.ShapeDtypeStruct(lead.shape, F32),
        in_specs=[SM, VM],
        out_specs=VM,
        compiler_params=PARAMS,
        name="invert_diagonal",
    )(info, lead)


def substitute(tri_ref, rhs_ref, out_ref, ready):
    out_ref[...] = rhs_ref[...]
    for k in range(8):
        ready(k)
        here = pl.ds(k * TILE, TILE)
        solved = packed_product(tri_ref[k, here, :], pack_right(out_ref[here, :]))
        out_ref[here, :] = solved
        right = pack_right(solved)
        for i in range(k + 1, 8):
            there = pl.ds(i * TILE, TILE)
            out_ref[there, :] = out_ref[there, :] - packed_product(tri_ref[k, there, :], right)


def pack_pieces(info, refs, places, tri_ref):
    for ref, parts in zip(refs, places):
        for half, steps, start, to, rows in parts:
            half = {"own": info[0], "pair": 1 - info[0]}.get(half, half)
            k = 4 * half + lax.rem(info[1] + steps, 4)
            tri_ref[k, pl.ds(to, rows), :] = pack_left(ref[pl.ds(start, rows), :])


def solve_first(info, pieces, places, rhs):
    def body(info, *refs):
        rhs_ref, out_ref, tri_ref = refs[-3:]

        @pl.when(info[2] == 1)
        def _():
            pack_pieces(info, refs, places, tri_ref)
            substitute(tri_ref, rhs_ref, out_ref, lambda k: None)

    return pl.pallas_call(
        body,
        out_shape=jax.ShapeDtypeStruct(rhs.shape, F32),
        in_specs=[SM] + [VM] * (len(pieces) + 1),
        out_specs=VM,
        scratch_shapes=[pltpu.VMEM((8, 1024, 256), BF16)],
        compiler_params=PARAMS,
        name="solve_first",
    )(info, *pieces, rhs)


def residual_or_pack(info, pieces, places, rhs, x):
    count = len(pieces)

    def body(info, *refs):
        rhs_ref, x_ref, out_ref, tri_out, tri_ref, semaphore = refs[count:]

        @pl.when(info[2] == 1)
        def _():
            out_ref[...] = rhs_ref[...]
            for ref, parts in zip(refs, places):
                for half, steps, start, to, rows in parts:
                    half = {"own": info[0], "pair": 1 - info[0]}[half]
                    k = 4 * half + lax.rem(info[1] + steps, 4)
                    right = pack_right(x_ref[pl.ds(pl.multiple_of(k * TILE, TILE), TILE), :])
                    for n in range(0, rows, TILE):
                        there = pl.ds(to + n, TILE)
                        left = pack_left(ref[pl.ds(start + n, TILE), :])
                        out_ref[there, :] = out_ref[there, :] - packed_product(left, right)

        @pl.when(info[2] == 2)
        def _():
            pack_pieces(info, refs, places, tri_ref)
            copy = pltpu.make_async_copy(tri_ref, tri_out.at[pl.ds(0, 8)], semaphore)
            copy.start()
            copy.wait()

    return pl.pallas_call(
        body,
        out_shape=[jax.ShapeDtypeStruct(rhs.shape, F32), jax.ShapeDtypeStruct((STORE, 1024, 256), BF16)],
        in_specs=[SM] + [VM] * (count + 2),
        out_specs=[VM, FAR],
        scratch_shapes=[pltpu.VMEM((8, 1024, 256), BF16), pltpu.SemaphoreType.DMA],
        compiler_params=PARAMS,
        name="residual_or_pack",
    )(info, *pieces, rhs, x)


def solve_second(info, tri, rhs):
    def body(info, tri_in, rhs_ref, out_ref, tri_ref, semaphores):
        @pl.when(info[2] == 1)
        def _():
            copies = [pltpu.make_async_copy(tri_in.at[k], tri_ref.at[k], semaphores.at[k]) for k in range(8)]
            for copy in copies:
                copy.start()
            substitute(tri_ref, rhs_ref, out_ref, lambda k: copies[k].wait())

    return pl.pallas_call(
        body,
        out_shape=jax.ShapeDtypeStruct(rhs.shape, F32),
        in_specs=[SM, FAR, VM],
        out_specs=VM,
        scratch_shapes=[pltpu.VMEM((8, 1024, 256), BF16), pltpu.SemaphoreType.DMA((8,))],
        compiler_params=PARAMS,
        name="solve_second",
    )(info, tri, rhs)


def arrange_body(factor_ref, out_ref):
    for c in range(16):
        for a in range(4):
            out_ref[c, pl.ds(64 * a, 64), :] = factor_ref[a, pl.ds(64 * c, 64), :]


def arrange(factor):
    return pl.pallas_call(
        arrange_body,
        out_shape=jax.ShapeDtypeStruct((16, 256, TILE), F32),
        in_specs=[VM],
        out_specs=VM,
        compiler_params=PARAMS,
        name="arrange_rows",
    )(factor)


def arrange_rhs_body(info, rhs_ref, out_ref):
    for n in range(8):
        to = jnp.where(info[0] == 0, n, (n + 4) % 8)
        out_ref[to, :, :] = rhs_ref[0, :, pl.ds(n * TILE, TILE)]


def arrange_rhs(yh, rhs):
    return pl.pallas_call(
        arrange_rhs_body,
        grid=(1,),
        out_shape=jax.ShapeDtypeStruct((8, 64, TILE), F32),
        in_specs=[SM, pl.BlockSpec((1, 64, 1024), lambda i: (0, 0, 0))],
        out_specs=pl.BlockSpec((8, 64, TILE), lambda i: (0, 0, 0)),
        compiler_params=PARAMS,
        name="arrange_rhs",
    )(jnp.reshape(yh, (1,)).astype(jnp.int32), rhs)


def prepare_body(info, left_ref, other_ref, high_ref, low_ref):
    for side, ref in enumerate((left_ref, other_ref)):
        rows = pl.ds(256 * side, 256)
        first = 8 * info[1] if side == 0 else 0
        for n in range(4):
            high, low = split(jnp.concatenate([ref[first + 2 * n], ref[first + 2 * n + 1]], 1))
            high_ref[n, rows, :] = high
            low_ref[n, rows, :] = low

    @pl.when(info[0] == 0)
    def _():
        for n in range(4):
            for side in range(2):
                high_ref[n, pl.ds(256 * side, 64), :] = jnp.zeros((64, 256), BF16)
                low_ref[n, pl.ds(256 * side, 64), :] = jnp.zeros((64, 256), BF16)


def prepare(info, left, other):
    return pl.pallas_call(
        prepare_body,
        out_shape=[jax.ShapeDtypeStruct((4, 512, 256), BF16)] * 2,
        in_specs=[SM, VM, VM],
        out_specs=[VM, VM],
        compiler_params=PARAMS,
        name="prepare_update",
    )(info, left, other)


def accumulate(info, sums, high, low, pieces, places, name):
    first = sums is None

    def body(info, high_ref, low_ref, *refs):
        out_ref = refs[-1]
        x, core, y, z, col = (info[k] for k in range(5))
        if first:
            out_ref[...] = jnp.zeros(out_ref.shape, F32)
        else:
            out_ref[...] = refs[0][...]
        for ref, (far, slot) in zip(refs[0 if first else 1 :], places):
            for n in range(ref.shape[0]):
                near = slot + n
                py = lax.rem(y + jnp.where(core == 0, far, near), 4)
                pz = lax.rem(z + jnp.where(core == 0, near, far), 4)
                upper = py // 2
                bit = jnp.where(upper == 0, py, 3 - py)
                cols = pl.ds(pl.multiple_of((4 * bit + pz) * TILE, TILE), TILE)
                total = None
                for h in range(2):
                    x_high, x_low = split(ref[n, pl.ds(256 * h, 256), :])
                    wide = mm(high_ref[2 * upper + h], jnp.concatenate([x_high, x_low], 1))
                    term = wide[:, :TILE] + (wide[:, TILE:] + mm(low_ref[2 * upper + h], x_high))
                    total = term if total is None else total + term
                out_ref[:, cols] = out_ref[:, cols] + total

                @pl.when((x == 0) & (col // 8 == upper))
                def _():
                    there = pl.ds(pl.multiple_of(lax.rem(col, 8) * 64, 64), 64)
                    here = pl.ds(0, 64)
                    out_ref[here, cols] = out_ref[here, cols] - ref[n, there, :]

    start = [] if first else [sums]
    return pl.pallas_call(
        body,
        out_shape=jax.ShapeDtypeStruct((512, 1024), F32),
        in_specs=[SM] + [VM] * (2 + len(start) + len(pieces)),
        out_specs=VM,
        input_output_aliases={} if first else {3: 0},
        compiler_params=PARAMS,
        name=name,
    )(info, high, low, *start, *pieces)


AXES = ROW + COL


def move(value, where):
    pairs = []
    for x in range(4):
        for core in range(2):
            for y in range(4):
                for z in range(4):
                    to = where(x, core, y, z)
                    if to is not None:
                        a, b, c, d = to
                        pairs.append((((x * 2 + core) * 4 + y) * 4 + z, ((a * 2 + b) * 4 + c % 4) * 4 + d % 4))
    return lax.ppermute(value, AXES, pairs)


def deal(first, second, core, yh, xi):
    here = jnp.where(core == 0, first[:512], second[512:])
    there = jnp.where(core == 0, first[512:], second[:512])
    got = move(there, lambda a, b, c, d: (0, b, 3 - c, d) if a == 0 and b == c // 2 else None)
    mine = jnp.where(core == yh, here, got)
    one = move(mine, lambda a, b, c, d: (1 if b == 0 else 3, b, c, d) if a == 0 else None)
    two = move(mine, lambda a, b, c, d: (3 if b == 0 else 1, b, c, d) if a == 0 else None)
    far = move(one, lambda a, b, c, d: (2, b, c, d) if a == (1 if b == 0 else 3) else None)
    return jnp.where(xi == 0, mine, one + two + far)


def gather(lead, half, by_rows, core, yl):
    def holds(a, b, c):
        return a == 0 and (b == 1 or c < 2)

    def step(b_on_z, amount):
        def where(a, b, c, d):
            if not holds(a, b, c):
                return None
            return (a, b, c, d + amount) if b == b_on_z else (a, b, c + 1 - 2 * (c % 2), d)

        return where

    def only(b_only, amount):
        return lambda a, b, c, d: (a, b, c, d + amount) if holds(a, b, c) and b == b_only else None

    mixed = move(lead, step(1, 1))
    after = move(lead, only(1, -1))
    swapped = move(lead, lambda a, b, c, d: (a, b, c + 1 - 2 * (c % 2), d) if holds(a, b, c) and b == 1 else None)
    mixed, swapped, half = lax.optimization_barrier((mixed, swapped, half))
    other_half = move(half, lambda a, b, c, d: (0, b, 3 - c, d) if a == 0 and c >= 2 else None)
    far_low = move(mixed[:512], only(1, 1))
    far_high = move(after[512:], only(1, -1))

    full = jnp.where(yl == 0, lead, mixed)
    lower = jnp.where(yl == 0, mixed[512:], lead[512:])
    zero = core == 0
    first = jnp.concatenate([jnp.where(zero, full, mixed), jnp.where(zero, lower, far_low)], 0)
    second = jnp.concatenate([jnp.where(zero, full, after), jnp.where(zero, lower, far_high)], 0)
    got_first = move(first, step(0, 1))
    got_second = move(second, step(0, -1))
    got_first, other_half, by_rows = lax.optimization_barrier((got_first, other_half, by_rows))
    end_low = move(got_first[:768], only(0, 1))
    end_high = move(got_second[768:], only(0, -1))

    corner_pieces = [first, got_second, got_first, end_low, end_high]
    corner_places = [[(0, n, 0, 0, 1024), (1, n, 1024, 512, 512)] for n in (0, 1, 3)]
    corner_places += [[(0, 2, 0, 0, 768)], [(0, 2, 0, 768, 256), (1, 2, 256, 512, 512)]]
    lower_pieces = [lead, swapped, first, second, got_first, got_second]
    lower_places = [[("own", 0, 0, 0, 1024)], [("pair", 0, 0, 0, 1024)]]
    for group in ("own", "pair"):
        lower_places.append([(group, 3, 0, 0, 1024), (group, 2, 1024, 0, 512)])
        lower_places.append([(group, 1, 0, 0, 1024), (group, 2, 1024, 512, 512)])
    return (corner_pieces, corner_places), (lower_pieces, lower_places), jnp.concatenate([half, other_half], 0), by_rows


def shards(factor, cross_cov):
    xi, core = lax.axis_index("x"), lax.axis_index("core")
    yh, yl, z = lax.axis_index("yh"), lax.axis_index("yl"), lax.axis_index("z")
    row_id = 2 * xi + core
    col_id = 8 * yh + 4 * yl + z
    local = factor[:, 0]
    rhs = cross_cov[:, 0]

    diagonal = ((row_id == 0) & (yh == 0)) | ((row_id == 1) & (yh == 1))
    info = jnp.stack([diagonal.astype(jnp.int32), (4 * yl + z).astype(jnp.int32)])
    lead = invert_diagonal(info, local[0])

    half = lax.all_to_all(arrange_rhs(yh, rhs), ("yl", "z"), 0, 0, tiled=True).reshape(512, TILE)
    upper_left, lower_row, columns, by_rows = gather(lead, half, arrange(local), core, yl)

    def place(what):
        return jnp.stack([yl, z, jnp.where(xi == 0, what, 0)]).astype(jnp.int32)

    first = solve_first(place((core == 0) & (yh == 0)), *upper_left, columns)
    sent = move(first, lambda a, b, c, d: (0, 1, c, d) if (a, b) == (0, 0) and c < 2 else None)
    by_rows, _ = lax.optimization_barrier((by_rows, first))
    left = lax.all_to_all(by_rows, COL, 0, 0, tiled=True)
    rest, tri = residual_or_pack(place(core * (1 + yh)), *lower_row, columns, sent)
    second_rhs = move(rest, lambda a, b, c, d: (0, 1, 3 - c, d) if (a, b) == (0, 1) and c < 2 else None)
    second = solve_second(place((core == 1) & (yh == 1)), tri, second_rhs)
    mine = deal(first, second, core, yh, xi)
    mine, left = lax.optimization_barrier((mine, left))

    def swap(value):
        return move(value, lambda a, b, c, d: (a, 1 - b, c, d))

    info2 = jnp.stack([xi, core, 2 * yh + yl, z, col_id]).astype(jnp.int32)

    def first_step(step):
        return lambda a, b, c, d: (a, b, c, d + step) if b == 0 else (a, b, c + step, d)

    def second_step(step):
        return lambda a, b, c, d: (a, b, c + step, d) if b == 0 else (a, b, c, d + step)

    before, after = lax.optimization_barrier((move(mine, first_step(1)), move(mine, first_step(-1))))
    far_low, far_high = move(before[:256], first_step(1)), move(after[256:], first_step(-1))
    low = jnp.concatenate([mine, after], 0).reshape(2, 512, TILE)
    low_before, low_after = move(low, second_step(1)), move(low, second_step(-1))
    left, _ = lax.optimization_barrier((left, low))
    given = swap(lax.dynamic_slice_in_dim(left, 8 * (1 - core), 8, 0))
    high = jnp.concatenate([far_low, far_high, before], 0).reshape(2, 512, TILE)
    high_after, high_before = move(high, second_step(-1)), move(high, second_step(1))
    parts = prepare(info2[:2], left, given)

    def add(sums, pieces, places, name):
        return accumulate(info2, sums, *parts, pieces, places, name)

    sums = add(None, [low, high], [(0, 0), (0, 2)], "update_near")
    low_before, high_after, sums = lax.optimization_barrier((low_before, high_after, sums))
    far_low, far_high = move(low_before, second_step(1)), move(high_after, second_step(-1))
    sums = add(
        sums, [low_after, high_after, low_before, high_before], [(1, 0), (1, 2), (3, 0), (3, 2)], "update_next"
    )
    far_low, far_high, sums = lax.optimization_barrier((far_low, far_high, sums))
    sums = add(sums, [far_low, far_high], [(2, 0), (2, 2)], "update_far")

    replaced = (xi == 0) & (lax.broadcasted_iota(jnp.int32, (256, 1024), 0) < 64)
    base = jnp.where(replaced, 0.0, rhs.reshape(256, 1024))
    out = base - (sums[:256] + swap(sums[256:]))
    return out.reshape(4, 1, 64, 1024)


def solution(mesh):
    fine = Mesh(mesh.devices.reshape(4, 2, 2, 2, 4), ROW + COL)
    return jax.shard_map(
        shards,
        mesh=fine,
        in_specs=(P(None, ROW, None, COL), P(None, ROW, COL, None)),
        out_specs=P(None, ROW, COL, None),
        check_vma=False,
    )
```

```python
import jax
import jax.numpy as jnp
from jax import lax
from jax.experimental import pallas as pl
from jax.experimental.pallas import tpu as pltpu
from jax.sharding import Mesh, PartitionSpec as P

ROW = ("x", "core")
COL = ("yh", "yl", "z")
F32 = jnp.float32
BF16 = jnp.bfloat16
TILE = 128
STORE = 112
PARAMS = pltpu.CompilerParams(vmem_limit_bytes=20 * 2**20)
VM = pl.BlockSpec(memory_space=pltpu.VMEM)
SM = pl.BlockSpec(memory_space=pltpu.SMEM)
FAR = pl.BlockSpec(memory_space=pltpu.HBM)


def split(value):
    high = value.astype(BF16)
    return high, (value - high.astype(F32)).astype(BF16)


def mm(a, b):
    return jnp.dot(a, b, preferred_element_type=F32)


def pack_left(value):
    return jnp.concatenate(split(value), 1)


def pack_right(value):
    high, low = split(value)
    return jnp.concatenate(
        [jnp.concatenate([high, low], 1), jnp.concatenate([high, jnp.zeros_like(low)], 1)], 0
    )


def packed_product(left, right):
    out = mm(left, right)
    return out[:, :TILE] + out[:, TILE:]


def invert_body(info, lead_ref, out_ref):
    out_ref[...] = lead_ref[...]

    @pl.when(info[0] == 1)
    def _():
        start = pl.multiple_of(info[1] * TILE, TILE)
        block = lead_ref[pl.ds(start, TILE), :]
        i = lax.broadcasted_iota(jnp.int32, (TILE, TILE), 0)
        j = lax.broadcasted_iota(jnp.int32, (TILE, TILE), 1)
        zero = jnp.zeros((TILE, TILE), F32)
        inverse = jnp.where(i == j, 1.0 / jnp.where(i == j, block, 1.0), zero)
        step = 1
        while step < TILE:
            below = ((i // (2 * step)) == (j // (2 * step))) & ((i // step) > (j // step))
            corner = jnp.where(below, block, zero)
            product = packed_product(pack_left(corner), pack_right(inverse))
            inverse = inverse - packed_product(pack_left(inverse), pack_right(product))
            step *= 2
        out_ref[pl.ds(start, TILE), :] = inverse


def invert_diagonal(info, lead):
    return pl.pallas_call(
        invert_body,
        out_shape=jax.ShapeDtypeStruct(lead.shape, F32),
        in_specs=[SM, VM],
        out_specs=VM,
        compiler_params=PARAMS,
        name="invert_diagonal",
    )(info, lead)


def substitute(tri_ref, rhs_ref, out_ref, ready):
    out_ref[...] = rhs_ref[...]
    for k in range(8):
        ready(k)
        here = pl.ds(k * TILE, TILE)
        solved = packed_product(tri_ref[k, here, :], pack_right(out_ref[here, :]))
        out_ref[here, :] = solved
        right = pack_right(solved)
        for i in range(k + 1, 8):
            there = pl.ds(i * TILE, TILE)
            out_ref[there, :] = out_ref[there, :] - packed_product(tri_ref[k, there, :], right)


def pack_pieces(info, refs, places, tri_ref):
    for ref, parts in zip(refs, places):
        for half, steps, start, to, rows in parts:
            half = {"own": info[0], "pair": 1 - info[0]}.get(half, half)
            k = 4 * half + lax.rem(info[1] + steps, 4)
            tri_ref[k, pl.ds(to, rows), :] = pack_left(ref[pl.ds(start, rows), :])


def solve_first(info, pieces, places, rhs):
    def body(info, *refs):
        rhs_ref, out_ref, tri_ref = refs[-3:]

        @pl.when(info[2] == 1)
        def _():
            pack_pieces(info, refs, places, tri_ref)
            substitute(tri_ref, rhs_ref, out_ref, lambda k: None)

    return pl.pallas_call(
        body,
        out_shape=jax.ShapeDtypeStruct(rhs.shape, F32),
        in_specs=[SM] + [VM] * (len(pieces) + 1),
        out_specs=VM,
        scratch_shapes=[pltpu.VMEM((8, 1024, 256), BF16)],
        compiler_params=PARAMS,
        name="solve_first",
    )(info, *pieces, rhs)


def residual_or_pack(info, pieces, places, rhs, x):
    count = len(pieces)

    def body(info, *refs):
        rhs_ref, x_ref, out_ref, tri_out, tri_ref, semaphore = refs[count:]

        @pl.when(info[2] == 1)
        def _():
            out_ref[...] = rhs_ref[...]
            for ref, parts in zip(refs, places):
                for half, steps, start, to, rows in parts:
                    half = {"own": info[0], "pair": 1 - info[0]}[half]
                    k = 4 * half + lax.rem(info[1] + steps, 4)
                    right = pack_right(x_ref[pl.ds(pl.multiple_of(k * TILE, TILE), TILE), :])
                    for n in range(0, rows, TILE):
                        there = pl.ds(to + n, TILE)
                        left = pack_left(ref[pl.ds(start + n, TILE), :])
                        out_ref[there, :] = out_ref[there, :] - packed_product(left, right)

        @pl.when(info[2] == 2)
        def _():
            pack_pieces(info, refs, places, tri_ref)
            copy = pltpu.make_async_copy(tri_ref, tri_out.at[pl.ds(0, 8)], semaphore)
            copy.start()
            copy.wait()

    return pl.pallas_call(
        body,
        out_shape=[jax.ShapeDtypeStruct(rhs.shape, F32), jax.ShapeDtypeStruct((STORE, 1024, 256), BF16)],
        in_specs=[SM] + [VM] * (count + 2),
        out_specs=[VM, FAR],
        scratch_shapes=[pltpu.VMEM((8, 1024, 256), BF16), pltpu.SemaphoreType.DMA],
        compiler_params=PARAMS,
        name="residual_or_pack",
    )(info, *pieces, rhs, x)


def solve_second(info, tri, rhs):
    def body(info, tri_in, rhs_ref, out_ref, tri_ref, semaphores):
        @pl.when(info[2] == 1)
        def _():
            copies = [pltpu.make_async_copy(tri_in.at[k], tri_ref.at[k], semaphores.at[k]) for k in range(8)]
            for copy in copies:
                copy.start()
            substitute(tri_ref, rhs_ref, out_ref, lambda k: copies[k].wait())

    return pl.pallas_call(
        body,
        out_shape=jax.ShapeDtypeStruct(rhs.shape, F32),
        in_specs=[SM, FAR, VM],
        out_specs=VM,
        scratch_shapes=[pltpu.VMEM((8, 1024, 256), BF16), pltpu.SemaphoreType.DMA((8,))],
        compiler_params=PARAMS,
        name="solve_second",
    )(info, tri, rhs)


def arrange_body(factor_ref, out_ref):
    for c in range(16):
        for a in range(4):
            out_ref[c, pl.ds(64 * a, 64), :] = factor_ref[a, pl.ds(64 * c, 64), :]


def arrange(factor):
    return pl.pallas_call(
        arrange_body,
        out_shape=jax.ShapeDtypeStruct((16, 256, TILE), F32),
        in_specs=[VM],
        out_specs=VM,
        compiler_params=PARAMS,
        name="arrange_rows",
    )(factor)


def arrange_rhs_body(info, rhs_ref, out_ref):
    for n in range(8):
        to = jnp.where(info[0] == 0, n, (n + 4) % 8)
        out_ref[to, :, :] = rhs_ref[0, :, pl.ds(n * TILE, TILE)]


def arrange_rhs(yh, rhs):
    return pl.pallas_call(
        arrange_rhs_body,
        grid=(1,),
        out_shape=jax.ShapeDtypeStruct((8, 64, TILE), F32),
        in_specs=[SM, pl.BlockSpec((1, 64, 1024), lambda i: (0, 0, 0))],
        out_specs=pl.BlockSpec((8, 64, TILE), lambda i: (0, 0, 0)),
        compiler_params=PARAMS,
        name="arrange_rhs",
    )(jnp.reshape(yh, (1,)).astype(jnp.int32), rhs)


def prepare_body(info, left_ref, other_ref, high_ref, low_ref):
    for side, ref in enumerate((left_ref, other_ref)):
        rows = pl.ds(256 * side, 256)
        first = 8 * info[1] if side == 0 else 0
        for n in range(4):
            high, low = split(jnp.concatenate([ref[first + 2 * n], ref[first + 2 * n + 1]], 1))
            high_ref[n, rows, :] = high
            low_ref[n, rows, :] = low

    @pl.when(info[0] == 0)
    def _():
        for n in range(4):
            for side in range(2):
                high_ref[n, pl.ds(256 * side, 64), :] = jnp.zeros((64, 256), BF16)
                low_ref[n, pl.ds(256 * side, 64), :] = jnp.zeros((64, 256), BF16)


def prepare(info, left, other):
    return pl.pallas_call(
        prepare_body,
        out_shape=[jax.ShapeDtypeStruct((4, 512, 256), BF16)] * 2,
        in_specs=[SM, VM, VM],
        out_specs=[VM, VM],
        compiler_params=PARAMS,
        name="prepare_update",
    )(info, left, other)


def accumulate(info, sums, high, low, pieces, places, name):
    first = sums is None

    def body(info, high_ref, low_ref, *refs):
        out_ref = refs[-1]
        x, core, y, z, col = (info[k] for k in range(5))
        if first:
            out_ref[...] = jnp.zeros(out_ref.shape, F32)
        else:
            out_ref[...] = refs[0][...]
        for ref, (far, slot) in zip(refs[0 if first else 1 :], places):
            for n in range(ref.shape[0]):
                near = slot + n
                py = lax.rem(y + jnp.where(core == 0, far, near), 4)
                pz = lax.rem(z + jnp.where(core == 0, near, far), 4)
                upper = py // 2
                bit = jnp.where(upper == 0, py, 3 - py)
                cols = pl.ds(pl.multiple_of((4 * bit + pz) * TILE, TILE), TILE)
                total = None
                for h in range(2):
                    x_high, x_low = split(ref[n, pl.ds(256 * h, 256), :])
                    wide = mm(high_ref[2 * upper + h], jnp.concatenate([x_high, x_low], 1))
                    term = wide[:, :TILE] + (wide[:, TILE:] + mm(low_ref[2 * upper + h], x_high))
                    total = term if total is None else total + term
                out_ref[:, cols] = out_ref[:, cols] + total

                @pl.when((x == 0) & (col // 8 == upper))
                def _():
                    there = pl.ds(pl.multiple_of(lax.rem(col, 8) * 64, 64), 64)
                    here = pl.ds(0, 64)
                    out_ref[here, cols] = out_ref[here, cols] - ref[n, there, :]

    start = [] if first else [sums]
    return pl.pallas_call(
        body,
        out_shape=jax.ShapeDtypeStruct((512, 1024), F32),
        in_specs=[SM] + [VM] * (2 + len(start) + len(pieces)),
        out_specs=VM,
        input_output_aliases={} if first else {3: 0},
        compiler_params=PARAMS,
        name=name,
    )(info, high, low, *start, *pieces)


AXES = ROW + COL


def move(value, where):
    pairs = []
    for x in range(4):
        for core in range(2):
            for y in range(4):
                for z in range(4):
                    to = where(x, core, y, z)
                    if to is not None:
                        a, b, c, d = to
                        pairs.append((((x * 2 + core) * 4 + y) * 4 + z, ((a * 2 + b) * 4 + c % 4) * 4 + d % 4))
    return lax.ppermute(value, AXES, pairs)


def deal(first, second, core, yh, xi, by_rows):
    here = jnp.where(core == 0, first[:512], second[512:])
    there = jnp.where(core == 0, first[512:], second[:512])
    got = move(there, lambda a, b, c, d: (0, b, 3 - c, d) if a == 0 and b == c // 2 else None)
    got, by_rows = lax.optimization_barrier((got, by_rows))
    left = lax.all_to_all(by_rows, COL, 0, 0, tiled=True)
    mine = jnp.where(core == yh, here, got)
    one = move(mine, lambda a, b, c, d: (1 if b == 0 else 3, b, c, d) if a == 0 else None)
    two = move(mine, lambda a, b, c, d: (3 if b == 0 else 1, b, c, d) if a == 0 else None)
    far = move(one, lambda a, b, c, d: (2, b, c, d) if a == (1 if b == 0 else 3) else None)
    return jnp.where(xi == 0, mine, one + two + far), left


def gather(lead, half, by_rows, core, yl):
    def holds(a, b, c):
        return a == 0 and (b == 1 or c < 2)

    def step(b_on_z, amount):
        def where(a, b, c, d):
            if not holds(a, b, c):
                return None
            return (a, b, c, d + amount) if b == b_on_z else (a, b, c + 1 - 2 * (c % 2), d)

        return where

    def only(b_only, amount):
        return lambda a, b, c, d: (a, b, c, d + amount) if holds(a, b, c) and b == b_only else None

    mixed = move(lead, step(1, 1))
    after = move(lead, only(1, -1))
    swapped = move(lead, lambda a, b, c, d: (a, b, c + 1 - 2 * (c % 2), d) if holds(a, b, c) and b == 1 else None)
    mixed, swapped, half = lax.optimization_barrier((mixed, swapped, half))
    other_half = move(half, lambda a, b, c, d: (0, b, 3 - c, d) if a == 0 and c >= 2 else None)
    far_low = move(mixed[:512], only(1, 1))
    far_high = move(after[512:], only(1, -1))

    full = jnp.where(yl == 0, lead, mixed)
    lower = jnp.where(yl == 0, mixed[512:], lead[512:])
    zero = core == 0
    first = jnp.concatenate([jnp.where(zero, full, mixed), jnp.where(zero, lower, far_low)], 0)
    second = jnp.concatenate([jnp.where(zero, full, after), jnp.where(zero, lower, far_high)], 0)
    got_first = move(first, step(0, 1))
    got_second = move(second, step(0, -1))
    got_first, other_half, by_rows = lax.optimization_barrier((got_first, other_half, by_rows))
    end_low = move(got_first[:768], only(0, 1))
    end_high = move(got_second[768:], only(0, -1))

    corner_pieces = [first, got_second, got_first, end_low, end_high]
    corner_places = [[(0, n, 0, 0, 1024), (1, n, 1024, 512, 512)] for n in (0, 1, 3)]
    corner_places += [[(0, 2, 0, 0, 768)], [(0, 2, 0, 768, 256), (1, 2, 256, 512, 512)]]
    lower_pieces = [lead, swapped, first, second, got_first, got_second]
    lower_places = [[("own", 0, 0, 0, 1024)], [("pair", 0, 0, 0, 1024)]]
    for group in ("own", "pair"):
        lower_places.append([(group, 3, 0, 0, 1024), (group, 2, 1024, 0, 512)])
        lower_places.append([(group, 1, 0, 0, 1024), (group, 2, 1024, 512, 512)])
    return (corner_pieces, corner_places), (lower_pieces, lower_places), jnp.concatenate([half, other_half], 0), by_rows


def shards(factor, cross_cov):
    xi, core = lax.axis_index("x"), lax.axis_index("core")
    yh, yl, z = lax.axis_index("yh"), lax.axis_index("yl"), lax.axis_index("z")
    row_id = 2 * xi + core
    col_id = 8 * yh + 4 * yl + z
    local = factor[:, 0]
    rhs = cross_cov[:, 0]

    diagonal = ((row_id == 0) & (yh == 0)) | ((row_id == 1) & (yh == 1))
    info = jnp.stack([diagonal.astype(jnp.int32), (4 * yl + z).astype(jnp.int32)])
    lead = invert_diagonal(info, local[0])

    half = lax.all_to_all(arrange_rhs(yh, rhs), ("yl", "z"), 0, 0, tiled=True).reshape(512, TILE)
    upper_left, lower_row, columns, by_rows = gather(lead, half, arrange(local), core, yl)

    def place(what):
        return jnp.stack([yl, z, jnp.where(xi == 0, what, 0)]).astype(jnp.int32)

    first = solve_first(place((core == 0) & (yh == 0)), *upper_left, columns)
    sent = move(first, lambda a, b, c, d: (0, 1, c, d) if (a, b) == (0, 0) and c < 2 else None)
    rest, tri = residual_or_pack(place(core * (1 + yh)), *lower_row, columns, sent)
    second_rhs = move(rest, lambda a, b, c, d: (0, 1, 3 - c, d) if (a, b) == (0, 1) and c < 2 else None)
    second = solve_second(place((core == 1) & (yh == 1)), tri, second_rhs)
    mine, left = deal(first, second, core, yh, xi, by_rows)

    def swap(value):
        return move(value, lambda a, b, c, d: (a, 1 - b, c, d))

    info2 = jnp.stack([xi, core, 2 * yh + yl, z, col_id]).astype(jnp.int32)

    def first_step(step):
        return lambda a, b, c, d: (a, b, c, d + step) if b == 0 else (a, b, c + step, d)

    def second_step(step):
        return lambda a, b, c, d: (a, b, c + step, d) if b == 0 else (a, b, c, d + step)

    before, after = lax.optimization_barrier((move(mine, first_step(1)), move(mine, first_step(-1))))
    far_low, far_high = move(before[:256], first_step(1)), move(after[256:], first_step(-1))
    low = jnp.concatenate([mine, after], 0).reshape(2, 512, TILE)
    low_before, low_after = move(low, second_step(1)), move(low, second_step(-1))
    high = jnp.concatenate([far_low, far_high, before], 0).reshape(2, 512, TILE)
    left, _ = lax.optimization_barrier((left, high))
    given = swap(lax.dynamic_slice_in_dim(left, 8 * (1 - core), 8, 0))
    high_after, high_before = move(high, second_step(-1)), move(high, second_step(1))
    parts = prepare(info2[:2], left, given)

    def add(sums, pieces, places, name):
        return accumulate(info2, sums, *parts, pieces, places, name)

    sums = add(None, [low, high], [(0, 0), (0, 2)], "update_near")
    low_before, high_after, sums = lax.optimization_barrier((low_before, high_after, sums))
    far_low, far_high = move(low_before, second_step(1)), move(high_after, second_step(-1))
    sums = add(
        sums, [low_after, high_after, low_before, high_before], [(1, 0), (1, 2), (3, 0), (3, 2)], "update_next"
    )
    far_low, far_high, sums = lax.optimization_barrier((far_low, far_high, sums))
    sums = add(sums, [far_low, far_high], [(2, 0), (2, 2)], "update_far")

    replaced = (xi == 0) & (lax.broadcasted_iota(jnp.int32, (256, 1024), 0) < 64)
    base = jnp.where(replaced, 0.0, rhs.reshape(256, 1024))
    out = base - (sums[:256] + swap(sums[256:]))
    return out.reshape(4, 1, 64, 1024)


def solution(mesh):
    fine = Mesh(mesh.devices.reshape(4, 2, 2, 2, 4), ROW + COL)
    return jax.shard_map(
        shards,
        mesh=fine,
        in_specs=(P(None, ROW, None, COL), P(None, ROW, COL, None)),
        out_specs=P(None, ROW, COL, None),
        check_vma=False,
    )
```

```python
import jax
import jax.numpy as jnp
from jax import lax
from jax.experimental import pallas as pl
from jax.experimental.pallas import tpu as pltpu
from jax.sharding import Mesh, PartitionSpec as P

ROW = ("x", "core")
COL = ("yh", "yl", "z")
F32 = jnp.float32
BF16 = jnp.bfloat16
TILE = 128
STORE = 112
PARAMS = pltpu.CompilerParams(vmem_limit_bytes=20 * 2**20)
VM = pl.BlockSpec(memory_space=pltpu.VMEM)
SM = pl.BlockSpec(memory_space=pltpu.SMEM)
FAR = pl.BlockSpec(memory_space=pltpu.HBM)


def split(value):
    high = value.astype(BF16)
    return high, (value - high.astype(F32)).astype(BF16)


def mm(a, b):
    return jnp.dot(a, b, preferred_element_type=F32)


def pack_left(value):
    return jnp.concatenate(split(value), 1)


def pack_right(value):
    high, low = split(value)
    return jnp.concatenate(
        [jnp.concatenate([high, low], 1), jnp.concatenate([high, jnp.zeros_like(low)], 1)], 0
    )


def packed_product(left, right):
    out = mm(left, right)
    return out[:, :TILE] + out[:, TILE:]


def invert_body(info, lead_ref, out_ref):
    out_ref[...] = lead_ref[...]

    @pl.when(info[0] == 1)
    def _():
        start = pl.multiple_of(info[1] * TILE, TILE)
        block = lead_ref[pl.ds(start, TILE), :]
        i = lax.broadcasted_iota(jnp.int32, (TILE, TILE), 0)
        j = lax.broadcasted_iota(jnp.int32, (TILE, TILE), 1)
        zero = jnp.zeros((TILE, TILE), F32)
        inverse = jnp.where(i == j, 1.0 / jnp.where(i == j, block, 1.0), zero)
        step = 1
        while step < TILE:
            below = ((i // (2 * step)) == (j // (2 * step))) & ((i // step) > (j // step))
            corner = jnp.where(below, block, zero)
            product = packed_product(pack_left(corner), pack_right(inverse))
            inverse = inverse - packed_product(pack_left(inverse), pack_right(product))
            step *= 2
        out_ref[pl.ds(start, TILE), :] = inverse


def invert_diagonal(info, lead):
    return pl.pallas_call(
        invert_body,
        out_shape=jax.ShapeDtypeStruct(lead.shape, F32),
        in_specs=[SM, VM],
        out_specs=VM,
        compiler_params=PARAMS,
        name="invert_diagonal",
    )(info, lead)


def substitute(tri_ref, rhs_ref, out_ref, ready):
    out_ref[...] = rhs_ref[...]
    for k in range(8):
        ready(k)
        here = pl.ds(k * TILE, TILE)
        solved = packed_product(tri_ref[k, here, :], pack_right(out_ref[here, :]))
        out_ref[here, :] = solved
        right = pack_right(solved)
        for i in range(k + 1, 8):
            there = pl.ds(i * TILE, TILE)
            out_ref[there, :] = out_ref[there, :] - packed_product(tri_ref[k, there, :], right)


def pack_pieces(info, refs, places, tri_ref):
    for ref, parts in zip(refs, places):
        for half, steps, start, to, rows in parts:
            half = {"own": info[0], "pair": 1 - info[0]}.get(half, half)
            k = 4 * half + lax.rem(info[1] + steps, 4)
            tri_ref[k, pl.ds(to, rows), :] = pack_left(ref[pl.ds(start, rows), :])


def solve_first(info, pieces, places, rhs):
    def body(info, *refs):
        rhs_ref, out_ref, tri_ref = refs[-3:]

        @pl.when(info[2] == 1)
        def _():
            pack_pieces(info, refs, places, tri_ref)
            substitute(tri_ref, rhs_ref, out_ref, lambda k: None)

    return pl.pallas_call(
        body,
        out_shape=jax.ShapeDtypeStruct(rhs.shape, F32),
        in_specs=[SM] + [VM] * (len(pieces) + 1),
        out_specs=VM,
        scratch_shapes=[pltpu.VMEM((8, 1024, 256), BF16)],
        compiler_params=PARAMS,
        name="solve_first",
    )(info, *pieces, rhs)


def residual_or_pack(info, pieces, places, rhs, x):
    count = len(pieces)

    def body(info, *refs):
        rhs_ref, x_ref, out_ref, tri_out, tri_ref, semaphore = refs[count:]

        @pl.when(info[2] == 1)
        def _():
            out_ref[...] = rhs_ref[...]
            for ref, parts in zip(refs, places):
                for half, steps, start, to, rows in parts:
                    half = {"own": info[0], "pair": 1 - info[0]}[half]
                    k = 4 * half + lax.rem(info[1] + steps, 4)
                    right = pack_right(x_ref[pl.ds(pl.multiple_of(k * TILE, TILE), TILE), :])
                    for n in range(0, rows, TILE):
                        there = pl.ds(to + n, TILE)
                        left = pack_left(ref[pl.ds(start + n, TILE), :])
                        out_ref[there, :] = out_ref[there, :] - packed_product(left, right)

        @pl.when(info[2] == 2)
        def _():
            pack_pieces(info, refs, places, tri_ref)
            copy = pltpu.make_async_copy(tri_ref, tri_out.at[pl.ds(0, 8)], semaphore)
            copy.start()
            copy.wait()

    return pl.pallas_call(
        body,
        out_shape=[jax.ShapeDtypeStruct(rhs.shape, F32), jax.ShapeDtypeStruct((STORE, 1024, 256), BF16)],
        in_specs=[SM] + [VM] * (count + 2),
        out_specs=[VM, FAR],
        scratch_shapes=[pltpu.VMEM((8, 1024, 256), BF16), pltpu.SemaphoreType.DMA],
        compiler_params=PARAMS,
        name="residual_or_pack",
    )(info, *pieces, rhs, x)


def solve_second(info, tri, rhs):
    def body(info, tri_in, rhs_ref, out_ref, tri_ref, semaphores):
        @pl.when(info[2] == 1)
        def _():
            copies = [pltpu.make_async_copy(tri_in.at[k], tri_ref.at[k], semaphores.at[k]) for k in range(8)]
            for copy in copies:
                copy.start()
            substitute(tri_ref, rhs_ref, out_ref, lambda k: copies[k].wait())

    return pl.pallas_call(
        body,
        out_shape=jax.ShapeDtypeStruct(rhs.shape, F32),
        in_specs=[SM, FAR, VM],
        out_specs=VM,
        scratch_shapes=[pltpu.VMEM((8, 1024, 256), BF16), pltpu.SemaphoreType.DMA((8,))],
        compiler_params=PARAMS,
        name="solve_second",
    )(info, tri, rhs)


def arrange_body(factor_ref, out_ref):
    for c in range(16):
        for a in range(4):
            out_ref[c, pl.ds(64 * a, 64), :] = factor_ref[a, pl.ds(64 * c, 64), :]


def arrange(factor):
    return pl.pallas_call(
        arrange_body,
        out_shape=jax.ShapeDtypeStruct((16, 256, TILE), F32),
        in_specs=[VM],
        out_specs=VM,
        compiler_params=PARAMS,
        name="arrange_rows",
    )(factor)


def arrange_rhs_body(info, rhs_ref, out_ref):
    for n in range(8):
        to = jnp.where(info[0] == 0, n, (n + 4) % 8)
        out_ref[to, :, :] = rhs_ref[0, :, pl.ds(n * TILE, TILE)]


def arrange_rhs(yh, rhs):
    return pl.pallas_call(
        arrange_rhs_body,
        grid=(1,),
        out_shape=jax.ShapeDtypeStruct((8, 64, TILE), F32),
        in_specs=[SM, pl.BlockSpec((1, 64, 1024), lambda i: (0, 0, 0))],
        out_specs=pl.BlockSpec((8, 64, TILE), lambda i: (0, 0, 0)),
        compiler_params=PARAMS,
        name="arrange_rhs",
    )(jnp.reshape(yh, (1,)).astype(jnp.int32), rhs)


def prepare_body(info, left_ref, other_ref, high_ref, low_ref):
    for side, ref in enumerate((left_ref, other_ref)):
        rows = pl.ds(256 * side, 256)
        first = 8 * info[1] if side == 0 else 0
        for n in range(4):
            high, low = split(jnp.concatenate([ref[first + 2 * n], ref[first + 2 * n + 1]], 1))
            high_ref[n, rows, :] = high
            low_ref[n, rows, :] = low

    @pl.when(info[0] == 0)
    def _():
        for n in range(4):
            for side in range(2):
                high_ref[n, pl.ds(256 * side, 64), :] = jnp.zeros((64, 256), BF16)
                low_ref[n, pl.ds(256 * side, 64), :] = jnp.zeros((64, 256), BF16)


def prepare(info, left, other):
    return pl.pallas_call(
        prepare_body,
        out_shape=[jax.ShapeDtypeStruct((4, 512, 256), BF16)] * 2,
        in_specs=[SM, VM, VM],
        out_specs=[VM, VM],
        compiler_params=PARAMS,
        name="prepare_update",
    )(info, left, other)


def accumulate(info, sums, high, low, pieces, places, name):
    first = sums is None

    def body(info, high_ref, low_ref, *refs):
        out_ref = refs[-1]
        x, core, y, z, col = (info[k] for k in range(5))
        if first:
            out_ref[...] = jnp.zeros(out_ref.shape, F32)
        else:
            out_ref[...] = refs[0][...]
        for ref, (far, slot) in zip(refs[0 if first else 1 :], places):
            for n in range(ref.shape[0]):
                near = slot + n
                py = lax.rem(y + jnp.where(core == 0, far, near), 4)
                pz = lax.rem(z + jnp.where(core == 0, near, far), 4)
                upper = py // 2
                bit = jnp.where(upper == 0, py, 3 - py)
                cols = pl.ds(pl.multiple_of((4 * bit + pz) * TILE, TILE), TILE)
                total = None
                for h in range(2):
                    x_high, x_low = split(ref[n, pl.ds(256 * h, 256), :])
                    wide = mm(high_ref[2 * upper + h], jnp.concatenate([x_high, x_low], 1))
                    term = wide[:, :TILE] + (wide[:, TILE:] + mm(low_ref[2 * upper + h], x_high))
                    total = term if total is None else total + term
                out_ref[:, cols] = out_ref[:, cols] + total

                @pl.when((x == 0) & (col // 8 == upper))
                def _():
                    there = pl.ds(pl.multiple_of(lax.rem(col, 8) * 64, 64), 64)
                    here = pl.ds(0, 64)
                    out_ref[here, cols] = out_ref[here, cols] - ref[n, there, :]

    start = [] if first else [sums]
    return pl.pallas_call(
        body,
        out_shape=jax.ShapeDtypeStruct((512, 1024), F32),
        in_specs=[SM] + [VM] * (2 + len(start) + len(pieces)),
        out_specs=VM,
        input_output_aliases={} if first else {3: 0},
        compiler_params=PARAMS,
        name=name,
    )(info, high, low, *start, *pieces)


AXES = ROW + COL


def move(value, where):
    pairs = []
    for x in range(4):
        for core in range(2):
            for y in range(4):
                for z in range(4):
                    to = where(x, core, y, z)
                    if to is not None:
                        a, b, c, d = to
                        pairs.append((((x * 2 + core) * 4 + y) * 4 + z, ((a * 2 + b) * 4 + c % 4) * 4 + d % 4))
    return lax.ppermute(value, AXES, pairs)


def deal(first, second, core, yh, xi, by_rows):
    here = jnp.where(core == 0, first[:512], second[512:])
    there = jnp.where(core == 0, first[512:], second[:512])
    got = move(there, lambda a, b, c, d: (0, b, 3 - c, d) if a == 0 and b == c // 2 else None)
    mine = jnp.where(core == yh, here, got)
    one = move(mine, lambda a, b, c, d: (1 if b == 0 else 3, b, c, d) if a == 0 else None)
    two = move(mine, lambda a, b, c, d: (3 if b == 0 else 1, b, c, d) if a == 0 else None)
    far = move(one, lambda a, b, c, d: (2, b, c, d) if a == (1 if b == 0 else 3) else None)
    by_rows, _ = lax.optimization_barrier((by_rows, one))
    left = lax.all_to_all(by_rows, COL, 0, 0, tiled=True)
    return jnp.where(xi == 0, mine, one + two + far), left


def gather(lead, half, by_rows, core, yl):
    def holds(a, b, c):
        return a == 0 and (b == 1 or c < 2)

    def step(b_on_z, amount):
        def where(a, b, c, d):
            if not holds(a, b, c):
                return None
            return (a, b, c, d + amount) if b == b_on_z else (a, b, c + 1 - 2 * (c % 2), d)

        return where

    def only(b_only, amount):
        return lambda a, b, c, d: (a, b, c, d + amount) if holds(a, b, c) and b == b_only else None

    mixed = move(lead, step(1, 1))
    after = move(lead, only(1, -1))
    swapped = move(lead, lambda a, b, c, d: (a, b, c + 1 - 2 * (c % 2), d) if holds(a, b, c) and b == 1 else None)
    mixed, swapped, half = lax.optimization_barrier((mixed, swapped, half))
    other_half = move(half, lambda a, b, c, d: (0, b, 3 - c, d) if a == 0 and c >= 2 else None)
    far_low = move(mixed[:512], only(1, 1))
    far_high = move(after[512:], only(1, -1))

    full = jnp.where(yl == 0, lead, mixed)
    lower = jnp.where(yl == 0, mixed[512:], lead[512:])
    zero = core == 0
    first = jnp.concatenate([jnp.where(zero, full, mixed), jnp.where(zero, lower, far_low)], 0)
    second = jnp.concatenate([jnp.where(zero, full, after), jnp.where(zero, lower, far_high)], 0)
    got_first = move(first, step(0, 1))
    got_second = move(second, step(0, -1))
    got_first, other_half, by_rows = lax.optimization_barrier((got_first, other_half, by_rows))
    end_low = move(got_first[:768], only(0, 1))
    end_high = move(got_second[768:], only(0, -1))

    corner_pieces = [first, got_second, got_first, end_low, end_high]
    corner_places = [[(0, n, 0, 0, 1024), (1, n, 1024, 512, 512)] for n in (0, 1, 3)]
    corner_places += [[(0, 2, 0, 0, 768)], [(0, 2, 0, 768, 256), (1, 2, 256, 512, 512)]]
    lower_pieces = [lead, swapped, first, second, got_first, got_second]
    lower_places = [[("own", 0, 0, 0, 1024)], [("pair", 0, 0, 0, 1024)]]
    for group in ("own", "pair"):
        lower_places.append([(group, 3, 0, 0, 1024), (group, 2, 1024, 0, 512)])
        lower_places.append([(group, 1, 0, 0, 1024), (group, 2, 1024, 512, 512)])
    return (corner_pieces, corner_places), (lower_pieces, lower_places), jnp.concatenate([half, other_half], 0), by_rows


def shards(factor, cross_cov):
    xi, core = lax.axis_index("x"), lax.axis_index("core")
    yh, yl, z = lax.axis_index("yh"), lax.axis_index("yl"), lax.axis_index("z")
    row_id = 2 * xi + core
    col_id = 8 * yh + 4 * yl + z
    local = factor[:, 0]
    rhs = cross_cov[:, 0]

    diagonal = ((row_id == 0) & (yh == 0)) | ((row_id == 1) & (yh == 1))
    info = jnp.stack([diagonal.astype(jnp.int32), (4 * yl + z).astype(jnp.int32)])
    lead = invert_diagonal(info, local[0])

    half = lax.all_to_all(arrange_rhs(yh, rhs), ("yl", "z"), 0, 0, tiled=True).reshape(512, TILE)
    upper_left, lower_row, columns, by_rows = gather(lead, half, arrange(local), core, yl)

    def place(what):
        return jnp.stack([yl, z, jnp.where(xi == 0, what, 0)]).astype(jnp.int32)

    first = solve_first(place((core == 0) & (yh == 0)), *upper_left, columns)
    sent = move(first, lambda a, b, c, d: (0, 1, c, d) if (a, b) == (0, 0) and c < 2 else None)
    rest, tri = residual_or_pack(place(core * (1 + yh)), *lower_row, columns, sent)
    second_rhs = move(rest, lambda a, b, c, d: (0, 1, 3 - c, d) if (a, b) == (0, 1) and c < 2 else None)
    second = solve_second(place((core == 1) & (yh == 1)), tri, second_rhs)
    mine, left = deal(first, second, core, yh, xi, by_rows)

    def swap(value):
        return move(value, lambda a, b, c, d: (a, 1 - b, c, d))

    info2 = jnp.stack([xi, core, 2 * yh + yl, z, col_id]).astype(jnp.int32)

    def first_step(step):
        return lambda a, b, c, d: (a, b, c, d + step) if b == 0 else (a, b, c + step, d)

    def second_step(step):
        return lambda a, b, c, d: (a, b, c + step, d) if b == 0 else (a, b, c, d + step)

    before, after = lax.optimization_barrier((move(mine, first_step(1)), move(mine, first_step(-1))))
    far_low, far_high = move(before[:256], first_step(1)), move(after[256:], first_step(-1))
    low = jnp.concatenate([mine, after], 0).reshape(2, 512, TILE)
    low_before, low_after = move(low, second_step(1)), move(low, second_step(-1))
    high = jnp.concatenate([far_low, far_high, before], 0).reshape(2, 512, TILE)
    left, _ = lax.optimization_barrier((left, high))
    given = swap(lax.dynamic_slice_in_dim(left, 8 * (1 - core), 8, 0))
    high_after, high_before = move(high, second_step(-1)), move(high, second_step(1))
    parts = prepare(info2[:2], left, given)

    def add(sums, pieces, places, name):
        return accumulate(info2, sums, *parts, pieces, places, name)

    sums = add(None, [low, high], [(0, 0), (0, 2)], "update_near")
    low_before, high_after, sums = lax.optimization_barrier((low_before, high_after, sums))
    far_low, far_high = move(low_before, second_step(1)), move(high_after, second_step(-1))
    sums = add(
        sums, [low_after, high_after, low_before, high_before], [(1, 0), (1, 2), (3, 0), (3, 2)], "update_next"
    )
    far_low, far_high, sums = lax.optimization_barrier((far_low, far_high, sums))
    sums = add(sums, [far_low, far_high], [(2, 0), (2, 2)], "update_far")

    replaced = (xi == 0) & (lax.broadcasted_iota(jnp.int32, (256, 1024), 0) < 64)
    base = jnp.where(replaced, 0.0, rhs.reshape(256, 1024))
    out = base - (sums[:256] + swap(sums[256:]))
    return out.reshape(4, 1, 64, 1024)


def solution(mesh):
    fine = Mesh(mesh.devices.reshape(4, 2, 2, 2, 4), ROW + COL)
    return jax.shard_map(
        shards,
        mesh=fine,
        in_specs=(P(None, ROW, None, COL), P(None, ROW, COL, None)),
        out_specs=P(None, ROW, COL, None),
        check_vma=False,
    )
```

```python
import jax
import jax.numpy as jnp
from jax import lax
from jax.experimental import pallas as pl
from jax.experimental.pallas import tpu as pltpu
from jax.sharding import Mesh, PartitionSpec as P

ROW = ("x", "core")
COL = ("yh", "yl", "z")
F32 = jnp.float32
BF16 = jnp.bfloat16
TILE = 128
STORE = 112
PARAMS = pltpu.CompilerParams(vmem_limit_bytes=20 * 2**20)
VM = pl.BlockSpec(memory_space=pltpu.VMEM)
SM = pl.BlockSpec(memory_space=pltpu.SMEM)
FAR = pl.BlockSpec(memory_space=pltpu.HBM)


def split(value):
    high = value.astype(BF16)
    return high, (value - high.astype(F32)).astype(BF16)


def mm(a, b):
    return jnp.dot(a, b, preferred_element_type=F32)


def pack_left(value):
    return jnp.concatenate(split(value), 1)


def pack_right(value):
    high, low = split(value)
    return jnp.concatenate(
        [jnp.concatenate([high, low], 1), jnp.concatenate([high, jnp.zeros_like(low)], 1)], 0
    )


def packed_product(left, right):
    out = mm(left, right)
    return out[:, :TILE] + out[:, TILE:]


def invert_body(info, lead_ref, out_ref):
    out_ref[...] = lead_ref[...]

    @pl.when(info[0] == 1)
    def _():
        start = pl.multiple_of(info[1] * TILE, TILE)
        block = lead_ref[pl.ds(start, TILE), :]
        i = lax.broadcasted_iota(jnp.int32, (TILE, TILE), 0)
        j = lax.broadcasted_iota(jnp.int32, (TILE, TILE), 1)
        zero = jnp.zeros((TILE, TILE), F32)
        inverse = jnp.where(i == j, 1.0 / jnp.where(i == j, block, 1.0), zero)
        step = 1
        while step < TILE:
            below = ((i // (2 * step)) == (j // (2 * step))) & ((i // step) > (j // step))
            corner = jnp.where(below, block, zero)
            product = packed_product(pack_left(corner), pack_right(inverse))
            inverse = inverse - packed_product(pack_left(inverse), pack_right(product))
            step *= 2
        out_ref[pl.ds(start, TILE), :] = inverse


def invert_diagonal(info, lead):
    return pl.pallas_call(
        invert_body,
        out_shape=jax.ShapeDtypeStruct(lead.shape, F32),
        in_specs=[SM, VM],
        out_specs=VM,
        compiler_params=PARAMS,
        name="invert_diagonal",
    )(info, lead)


def substitute(tri_ref, rhs_ref, out_ref, ready):
    out_ref[...] = rhs_ref[...]
    for k in range(8):
        ready(k)
        here = pl.ds(k * TILE, TILE)
        solved = packed_product(tri_ref[k, here, :], pack_right(out_ref[here, :]))
        out_ref[here, :] = solved
        right = pack_right(solved)
        for i in range(k + 1, 8):
            there = pl.ds(i * TILE, TILE)
            out_ref[there, :] = out_ref[there, :] - packed_product(tri_ref[k, there, :], right)


def pack_pieces(info, refs, places, tri_ref):
    for ref, parts in zip(refs, places):
        for half, steps, start, to, rows in parts:
            half = {"own": info[0], "pair": 1 - info[0]}.get(half, half)
            k = 4 * half + lax.rem(info[1] + steps, 4)
            tri_ref[k, pl.ds(to, rows), :] = pack_left(ref[pl.ds(start, rows), :])


def solve_first(info, pieces, places, rhs):
    def body(info, *refs):
        rhs_ref, out_ref, tri_ref = refs[-3:]

        @pl.when(info[2] == 1)
        def _():
            pack_pieces(info, refs, places, tri_ref)
            substitute(tri_ref, rhs_ref, out_ref, lambda k: None)

    return pl.pallas_call(
        body,
        out_shape=jax.ShapeDtypeStruct(rhs.shape, F32),
        in_specs=[SM] + [VM] * (len(pieces) + 1),
        out_specs=VM,
        scratch_shapes=[pltpu.VMEM((8, 1024, 256), BF16)],
        compiler_params=PARAMS,
        name="solve_first",
    )(info, *pieces, rhs)


def residual_or_pack(info, pieces, places, rhs, x):
    count = len(pieces)

    def body(info, *refs):
        rhs_ref, x_ref, out_ref, tri_out, tri_ref, semaphore = refs[count:]

        @pl.when(info[2] == 1)
        def _():
            out_ref[...] = rhs_ref[...]
            for ref, parts in zip(refs, places):
                for half, steps, start, to, rows in parts:
                    half = {"own": info[0], "pair": 1 - info[0]}[half]
                    k = 4 * half + lax.rem(info[1] + steps, 4)
                    right = pack_right(x_ref[pl.ds(pl.multiple_of(k * TILE, TILE), TILE), :])
                    for n in range(0, rows, TILE):
                        there = pl.ds(to + n, TILE)
                        left = pack_left(ref[pl.ds(start + n, TILE), :])
                        out_ref[there, :] = out_ref[there, :] - packed_product(left, right)

        @pl.when(info[2] == 2)
        def _():
            pack_pieces(info, refs, places, tri_ref)
            copy = pltpu.make_async_copy(tri_ref, tri_out.at[pl.ds(0, 8)], semaphore)
            copy.start()
            copy.wait()

    return pl.pallas_call(
        body,
        out_shape=[jax.ShapeDtypeStruct(rhs.shape, F32), jax.ShapeDtypeStruct((STORE, 1024, 256), BF16)],
        in_specs=[SM] + [VM] * (count + 2),
        out_specs=[VM, FAR],
        scratch_shapes=[pltpu.VMEM((8, 1024, 256), BF16), pltpu.SemaphoreType.DMA],
        compiler_params=PARAMS,
        name="residual_or_pack",
    )(info, *pieces, rhs, x)


def solve_second(info, tri, rhs):
    def body(info, tri_in, rhs_ref, out_ref, tri_ref, semaphores):
        @pl.when(info[2] == 1)
        def _():
            copies = [pltpu.make_async_copy(tri_in.at[k], tri_ref.at[k], semaphores.at[k]) for k in range(8)]
            for copy in copies:
                copy.start()
            substitute(tri_ref, rhs_ref, out_ref, lambda k: copies[k].wait())

    return pl.pallas_call(
        body,
        out_shape=jax.ShapeDtypeStruct(rhs.shape, F32),
        in_specs=[SM, FAR, VM],
        out_specs=VM,
        scratch_shapes=[pltpu.VMEM((8, 1024, 256), BF16), pltpu.SemaphoreType.DMA((8,))],
        compiler_params=PARAMS,
        name="solve_second",
    )(info, tri, rhs)


def arrange_body(factor_ref, out_ref):
    for c in range(16):
        for a in range(4):
            out_ref[c, pl.ds(64 * a, 64), :] = factor_ref[a, pl.ds(64 * c, 64), :]


def arrange(factor):
    return pl.pallas_call(
        arrange_body,
        out_shape=jax.ShapeDtypeStruct((16, 256, TILE), F32),
        in_specs=[VM],
        out_specs=VM,
        compiler_params=PARAMS,
        name="arrange_rows",
    )(factor)


def arrange_rhs_body(info, rhs_ref, out_ref):
    for n in range(8):
        to = jnp.where(info[0] == 0, n, (n + 4) % 8)
        out_ref[to, :, :] = rhs_ref[0, :, pl.ds(n * TILE, TILE)]


def arrange_rhs(yh, rhs):
    return pl.pallas_call(
        arrange_rhs_body,
        grid=(1,),
        out_shape=jax.ShapeDtypeStruct((8, 64, TILE), F32),
        in_specs=[SM, pl.BlockSpec((1, 64, 1024), lambda i: (0, 0, 0))],
        out_specs=pl.BlockSpec((8, 64, TILE), lambda i: (0, 0, 0)),
        compiler_params=PARAMS,
        name="arrange_rhs",
    )(jnp.reshape(yh, (1,)).astype(jnp.int32), rhs)


def prepare_body(info, left_ref, other_ref, high_ref, low_ref):
    for side, ref in enumerate((left_ref, other_ref)):
        rows = pl.ds(256 * side, 256)
        first = 8 * info[1] if side == 0 else 0
        for n in range(4):
            high, low = split(jnp.concatenate([ref[first + 2 * n], ref[first + 2 * n + 1]], 1))
            high_ref[n, rows, :] = high
            low_ref[n, rows, :] = low

    @pl.when(info[0] == 0)
    def _():
        for n in range(4):
            for side in range(2):
                high_ref[n, pl.ds(256 * side, 64), :] = jnp.zeros((64, 256), BF16)
                low_ref[n, pl.ds(256 * side, 64), :] = jnp.zeros((64, 256), BF16)


def prepare(info, left, other):
    return pl.pallas_call(
        prepare_body,
        out_shape=[jax.ShapeDtypeStruct((4, 512, 256), BF16)] * 2,
        in_specs=[SM, VM, VM],
        out_specs=[VM, VM],
        compiler_params=PARAMS,
        name="prepare_update",
    )(info, left, other)


def accumulate(info, sums, high, low, pieces, places, name):
    first = sums is None

    def body(info, high_ref, low_ref, *refs):
        out_ref = refs[-1]
        x, core, y, z, col = (info[k] for k in range(5))
        if first:
            out_ref[...] = jnp.zeros(out_ref.shape, F32)
        else:
            out_ref[...] = refs[0][...]
        for ref, (far, slot) in zip(refs[0 if first else 1 :], places):
            for n in range(ref.shape[0]):
                near = slot + n
                py = lax.rem(y + jnp.where(core == 0, far, near), 4)
                pz = lax.rem(z + jnp.where(core == 0, near, far), 4)
                upper = py // 2
                bit = jnp.where(upper == 0, py, 3 - py)
                cols = pl.ds(pl.multiple_of((4 * bit + pz) * TILE, TILE), TILE)
                total = None
                for h in range(2):
                    x_high, x_low = split(ref[n, pl.ds(256 * h, 256), :])
                    wide = mm(high_ref[2 * upper + h], jnp.concatenate([x_high, x_low], 1))
                    term = wide[:, :TILE] + (wide[:, TILE:] + mm(low_ref[2 * upper + h], x_high))
                    total = term if total is None else total + term
                out_ref[:, cols] = out_ref[:, cols] + total

                @pl.when((x == 0) & (col // 8 == upper))
                def _():
                    there = pl.ds(pl.multiple_of(lax.rem(col, 8) * 64, 64), 64)
                    here = pl.ds(0, 64)
                    out_ref[here, cols] = out_ref[here, cols] - ref[n, there, :]

    start = [] if first else [sums]
    return pl.pallas_call(
        body,
        out_shape=jax.ShapeDtypeStruct((512, 1024), F32),
        in_specs=[SM] + [VM] * (2 + len(start) + len(pieces)),
        out_specs=VM,
        input_output_aliases={} if first else {3: 0},
        compiler_params=PARAMS,
        name=name,
    )(info, high, low, *start, *pieces)


AXES = ROW + COL


def move(value, where):
    pairs = []
    for x in range(4):
        for core in range(2):
            for y in range(4):
                for z in range(4):
                    to = where(x, core, y, z)
                    if to is not None:
                        a, b, c, d = to
                        pairs.append((((x * 2 + core) * 4 + y) * 4 + z, ((a * 2 + b) * 4 + c % 4) * 4 + d % 4))
    return lax.ppermute(value, AXES, pairs)


def deal(first, second, core, yh, xi, by_rows):
    here = jnp.where(core == 0, first[:512], second[512:])
    there = jnp.where(core == 0, first[512:], second[:512])
    got = move(there, lambda a, b, c, d: (0, b, 3 - c, d) if a == 0 and b == c // 2 else None)
    mine = jnp.where(core == yh, here, got)
    one = move(mine, lambda a, b, c, d: (1 if b == 0 else 3, b, c, d) if a == 0 else None)
    two = move(mine, lambda a, b, c, d: (3 if b == 0 else 1, b, c, d) if a == 0 else None)
    far = move(one, lambda a, b, c, d: (2, b, c, d) if a == (1 if b == 0 else 3) else None)
    by_rows, _, _ = lax.optimization_barrier((by_rows, one, two))
    left = lax.all_to_all(by_rows, COL, 0, 0, tiled=True)
    return jnp.where(xi == 0, mine, one + two + far), left


def gather(lead, half, by_rows, core, yl):
    def holds(a, b, c):
        return a == 0 and (b == 1 or c < 2)

    def step(b_on_z, amount):
        def where(a, b, c, d):
            if not holds(a, b, c):
                return None
            return (a, b, c, d + amount) if b == b_on_z else (a, b, c + 1 - 2 * (c % 2), d)

        return where

    def only(b_only, amount):
        return lambda a, b, c, d: (a, b, c, d + amount) if holds(a, b, c) and b == b_only else None

    mixed = move(lead, step(1, 1))
    after = move(lead, only(1, -1))
    swapped = move(lead, lambda a, b, c, d: (a, b, c + 1 - 2 * (c % 2), d) if holds(a, b, c) and b == 1 else None)
    mixed, swapped, half = lax.optimization_barrier((mixed, swapped, half))
    other_half = move(half, lambda a, b, c, d: (0, b, 3 - c, d) if a == 0 and c >= 2 else None)
    far_low = move(mixed[:512], only(1, 1))
    far_high = move(after[512:], only(1, -1))

    full = jnp.where(yl == 0, lead, mixed)
    lower = jnp.where(yl == 0, mixed[512:], lead[512:])
    zero = core == 0
    first = jnp.concatenate([jnp.where(zero, full, mixed), jnp.where(zero, lower, far_low)], 0)
    second = jnp.concatenate([jnp.where(zero, full, after), jnp.where(zero, lower, far_high)], 0)
    got_first = move(first, step(0, 1))
    got_second = move(second, step(0, -1))
    got_first, other_half, by_rows = lax.optimization_barrier((got_first, other_half, by_rows))
    end_low = move(got_first[:768], only(0, 1))
    end_high = move(got_second[768:], only(0, -1))

    corner_pieces = [first, got_second, got_first, end_low, end_high]
    corner_places = [[(0, n, 0, 0, 1024), (1, n, 1024, 512, 512)] for n in (0, 1, 3)]
    corner_places += [[(0, 2, 0, 0, 768)], [(0, 2, 0, 768, 256), (1, 2, 256, 512, 512)]]
    lower_pieces = [lead, swapped, first, second, got_first, got_second]
    lower_places = [[("own", 0, 0, 0, 1024)], [("pair", 0, 0, 0, 1024)]]
    for group in ("own", "pair"):
        lower_places.append([(group, 3, 0, 0, 1024), (group, 2, 1024, 0, 512)])
        lower_places.append([(group, 1, 0, 0, 1024), (group, 2, 1024, 512, 512)])
    return (corner_pieces, corner_places), (lower_pieces, lower_places), jnp.concatenate([half, other_half], 0), by_rows


def shards(factor, cross_cov):
    xi, core = lax.axis_index("x"), lax.axis_index("core")
    yh, yl, z = lax.axis_index("yh"), lax.axis_index("yl"), lax.axis_index("z")
    row_id = 2 * xi + core
    col_id = 8 * yh + 4 * yl + z
    local = factor[:, 0]
    rhs = cross_cov[:, 0]

    diagonal = ((row_id == 0) & (yh == 0)) | ((row_id == 1) & (yh == 1))
    info = jnp.stack([diagonal.astype(jnp.int32), (4 * yl + z).astype(jnp.int32)])
    lead = invert_diagonal(info, local[0])

    half = lax.all_to_all(arrange_rhs(yh, rhs), ("yl", "z"), 0, 0, tiled=True).reshape(512, TILE)
    upper_left, lower_row, columns, by_rows = gather(lead, half, arrange(local), core, yl)

    def place(what):
        return jnp.stack([yl, z, jnp.where(xi == 0, what, 0)]).astype(jnp.int32)

    first = solve_first(place((core == 0) & (yh == 0)), *upper_left, columns)
    sent = move(first, lambda a, b, c, d: (0, 1, c, d) if (a, b) == (0, 0) and c < 2 else None)
    rest, tri = residual_or_pack(place(core * (1 + yh)), *lower_row, columns, sent)
    second_rhs = move(rest, lambda a, b, c, d: (0, 1, 3 - c, d) if (a, b) == (0, 1) and c < 2 else None)
    second = solve_second(place((core == 1) & (yh == 1)), tri, second_rhs)
    mine, left = deal(first, second, core, yh, xi, by_rows)

    def swap(value):
        return move(value, lambda a, b, c, d: (a, 1 - b, c, d))

    info2 = jnp.stack([xi, core, 2 * yh + yl, z, col_id]).astype(jnp.int32)

    def first_step(step):
        return lambda a, b, c, d: (a, b, c, d + step) if b == 0 else (a, b, c + step, d)

    def second_step(step):
        return lambda a, b, c, d: (a, b, c + step, d) if b == 0 else (a, b, c, d + step)

    before, after = lax.optimization_barrier((move(mine, first_step(1)), move(mine, first_step(-1))))
    far_low, far_high = move(before[:256], first_step(1)), move(after[256:], first_step(-1))
    low = jnp.concatenate([mine, after], 0).reshape(2, 512, TILE)
    low_before, low_after = move(low, second_step(1)), move(low, second_step(-1))
    high = jnp.concatenate([far_low, far_high, before], 0).reshape(2, 512, TILE)
    left, _ = lax.optimization_barrier((left, high))
    given = swap(lax.dynamic_slice_in_dim(left, 8 * (1 - core), 8, 0))
    high_after, high_before = move(high, second_step(-1)), move(high, second_step(1))
    parts = prepare(info2[:2], left, given)

    def add(sums, pieces, places, name):
        return accumulate(info2, sums, *parts, pieces, places, name)

    sums = add(None, [low, high], [(0, 0), (0, 2)], "update_near")
    low_before, high_after, sums = lax.optimization_barrier((low_before, high_after, sums))
    far_low, far_high = move(low_before, second_step(1)), move(high_after, second_step(-1))
    sums = add(
        sums, [low_after, high_after, low_before, high_before], [(1, 0), (1, 2), (3, 0), (3, 2)], "update_next"
    )
    far_low, far_high, sums = lax.optimization_barrier((far_low, far_high, sums))
    sums = add(sums, [far_low, far_high], [(2, 0), (2, 2)], "update_far")

    replaced = (xi == 0) & (lax.broadcasted_iota(jnp.int32, (256, 1024), 0) < 64)
    base = jnp.where(replaced, 0.0, rhs.reshape(256, 1024))
    out = base - (sums[:256] + swap(sums[256:]))
    return out.reshape(4, 1, 64, 1024)


def solution(mesh):
    fine = Mesh(mesh.devices.reshape(4, 2, 2, 2, 4), ROW + COL)
    return jax.shard_map(
        shards,
        mesh=fine,
        in_specs=(P(None, ROW, None, COL), P(None, ROW, COL, None)),
        out_specs=P(None, ROW, COL, None),
        check_vma=False,
    )
```
